512 devices in a mesh: rows: 64 (over y, x, core), rhs: 8 (over z).
Axes of the slice: x: 4, y: 8, z: 8, core: 2. Of those that a mesh axis runs over, the one named last changes fastest.
Arguments:
- right_side: float32 [64, 32768], P('rhs', 'rows'), may hold values from -6 to 6
- tiles: float32 [512, 7, 64, 64], P('rows'), may hold values from -2 to 5.5, as said below
- pivots: float32 [512, 64, 64], P('rows'), may hold values from -0.05 to 0.8, as said below
- columns: int32 [512, 7], P('rows'), may hold values from 0 to 511, as said below
Outputs:
- solution: float32 [64, 32768], P('rhs', 'rows')
- residual: float32 [64, 32768], P('rhs', 'rows')
The draws below stay inside these ranges and needn't reach their ends.
Inputs may be any that keep to these rules, and one draw needn't show every extreme that they name: columns[i, 0] = i. The other six columns of block row i are i - o and i + o for three offsets o shared by all block rows, the largest of them exactly 8, in an order of the slots drawn for each block row; a column that would fall outside 0 to 511 is i itself. tiles[i, 0] is the diagonal tile of block row i; A is symmetric positive definite: the tile of block row i in a slot whose column j differs from i is the transpose of the tile of block row j in its slot whose column is i. Every pivots[i] is symmetric positive definite.
All inputs are finite; a program needn't handle non-finite values.
Results may differ from the reference program's by a relative error of at most 0.0003.
Values sent between devices are 32-bit elements; how exact they have to be, the bound alone decides.
A program may use at most 64 MiB of HBM per device.

```python
import math
import jax
import jax.numpy as jnp
from jax import lax

BS = 64
RHS = 64
TILES = 7
BR_DEV = 8
SPAN = 8
ITERS = 2
NBR = 512


def pattern(key):
    first = jax.random.randint(jax.random.fold_in(key, 11), (), 1, BR_DEV // 2 + 1)
    second = jax.random.randint(jax.random.fold_in(key, 12), (), BR_DEV // 2 + 1, BR_DEV)
    offsets = jnp.stack([first, second, jnp.asarray(BR_DEV, jnp.int32)]).astype(jnp.int32)
    scores = jax.random.randint(jax.random.fold_in(key, 13), (NBR, 6), 0, 1 << 20) * 8
    scores = scores + jnp.arange(6, dtype=jnp.int32)[None]
    kinds = jnp.argsort(scores, axis=1).astype(jnp.int32)
    kind_type = kinds // 2
    upward = kinds % 2 == 0
    reach = offsets[kind_type]
    rows = jnp.arange(NBR, dtype=jnp.int32)[:, None]
    neighbour = jnp.where(upward, rows + reach, rows - reach)
    inside = (neighbour >= 0) & (neighbour < NBR)
    columns = jnp.concatenate([rows, jnp.where(inside, neighbour, rows)], axis=1).astype(jnp.int32)
    edge_row = jnp.where(upward, rows, rows - reach) % NBR
    return (offsets, kind_type, inside, columns, edge_row)


def couplings(key):
    strong = jnp.exp(jax.random.uniform(jax.random.fold_in(key, 21), (NBR, 1), jnp.float32, 0.0, math.log(2.0)))
    weak = 0.15 * jnp.exp(jax.random.uniform(jax.random.fold_in(key, 22), (NBR, 2), jnp.float32, 0.0, math.log(2.0)))
    mass = 0.05 * jnp.exp(jax.random.uniform(jax.random.fold_in(key, 23), (NBR,), jnp.float32, 0.0, math.log(4.0)))
    return (jnp.concatenate([weak, strong], axis=1), mass)


def symmetric_noise(key, lead):
    bound = 0.9 / (BS - 1)
    shape = lead + (BS, BS)
    raw = bound / 2.0 * jax.random.truncated_normal(key, -2.0, 2.0, shape, jnp.float32)
    sym = 0.5 * (raw + jnp.swapaxes(raw, -1, -2))
    return sym * (1.0 - jnp.eye(BS, dtype=jnp.float32))


def draw_columns(key, part):
    offsets, kind_type, inside, columns, edge_row = pattern(key)
    return columns


def draw_tiles(key, part):
    offsets, kind_type, inside, columns, edge_row = pattern(key)
    strength, mass = couplings(key)
    eye = jnp.eye(BS, dtype=jnp.float32)
    edges = strength[:, :, None, None] * (eye[None, None] + symmetric_noise(jax.random.fold_in(key, 31), (NBR, 3)))
    flat = edges.reshape(NBR * 3, BS, BS)
    index = (edge_row * 3 + kind_type).reshape(-1)
    picked = jnp.take(flat, index, axis=0).reshape(NBR, 6, BS, BS)
    inside_f = inside.astype(jnp.float32)[:, :, None, None]
    outer = picked * (1.0 - 2.0 * inside_f)
    extra = symmetric_noise(jax.random.fold_in(key, 32), (NBR,))
    diagonal = jnp.sum(picked * inside_f, axis=1) + mass[:, None, None] * (eye[None] + extra)
    return jnp.concatenate([diagonal[:, None], outer], axis=1)


def draw_pivots(key, part):
    offsets, kind_type, inside, columns, edge_row = pattern(key)
    strength, mass = couplings(key)
    picked = jnp.take(strength.reshape(-1), edge_row * 3 + kind_type)
    total = jnp.sum(picked, axis=1) + mass
    block_rows = SPAN * BR_DEV
    count_blocks = NBR // block_rows
    total_b = total.reshape(count_blocks, block_rows)
    strength_b = strength.reshape(count_blocks, block_rows, 3)

    def step(place, pivot):
        value = lax.dynamic_index_in_dim(total_b, place, 1, False)
        for kind in range(3):
            earlier = jnp.maximum(place - offsets[kind], 0)
            coupling = lax.dynamic_index_in_dim(strength_b[:, :, kind], earlier, 1, False)
            before = lax.dynamic_index_in_dim(pivot, earlier, 1, False)
            value = value - jnp.where(place >= offsets[kind], coupling * coupling / before, 0.0)
        return lax.dynamic_update_index_in_dim(pivot, value, place, 1)
    pivot = lax.fori_loop(0, block_rows, step, jnp.ones_like(total_b))
    scale = 1.0 / pivot.reshape(NBR)
    eye = jnp.eye(BS, dtype=jnp.float32)
    noise = symmetric_noise(jax.random.fold_in(key, 33), (NBR,))
    return scale[:, None, None] * (eye[None] + noise)


def draw_right_side(key, part):
    shape = (RHS, NBR * BS)
    return jax.random.truncated_normal(jax.random.fold_in(key, 41), -6.0, 6.0, shape, jnp.float32)


def setup_inputs(seed: int = 0) -> dict:
    key_of = jax.random.split(jax.random.key(seed), 5)
    return {
        "right_side": draw_right_side(jax.random.fold_in(key_of[4], 71), 0),
        "tiles": draw_tiles(jax.random.fold_in(key_of[4], 71), 0),
        "pivots": draw_pivots(jax.random.fold_in(key_of[4], 71), 0),
        "columns": draw_columns(jax.random.fold_in(key_of[4], 71), 0),
    }


def inner(left, right):
    return jnp.dot(left, right.T, precision=lax.Precision.HIGHEST)

def chol_solve(factor, values):
    middle = lax.linalg.triangular_solve(factor, values, left_side=True, lower=True)
    return lax.linalg.triangular_solve(factor, middle, left_side=True, lower=True, transpose_a=True)

def reference(right_side, tiles, pivots, columns):
    groups = NBR // BR_DEV

    def product(vector):
        blocks = vector.reshape(RHS, NBR, BS)
        tile_groups = tiles.reshape(groups, BR_DEV, TILES, BS, BS)
        col_groups = columns.reshape(groups, BR_DEV, TILES)

        def one_group(pair):
            group_tiles, group_cols = pair
            picked = jnp.take(blocks, group_cols, axis=1)
            return jnp.einsum('ikab,cikb->cia', group_tiles, picked, precision=lax.Precision.HIGHEST)
        result = lax.map(one_group, (tile_groups, col_groups))
        return jnp.transpose(result, (1, 0, 2, 3)).reshape(RHS, NBR * BS)
    block_rows = SPAN * BR_DEV
    count_blocks = NBR // block_rows
    starts = jnp.arange(count_blocks, dtype=jnp.int32) * block_rows

    def precondition(vector):
        source = vector.reshape(RHS, NBR, BS)

        def forward(turn, lowered):
            rows_now = starts + turn
            cols_now = columns[rows_now]
            keep = (cols_now < rows_now[:, None]) & (cols_now >= starts[:, None])
            masked = tiles[rows_now] * keep[:, :, None, None].astype(tiles.dtype)
            picked = jnp.take(lowered, cols_now, axis=1)
            summed = jnp.einsum('jkab,cjkb->cja', masked, picked, precision=lax.Precision.HIGHEST)
            remain = source[:, rows_now] - summed
            value = jnp.einsum('jab,cjb->cja', pivots[rows_now], remain, precision=lax.Precision.HIGHEST)
            return lowered.at[:, rows_now].set(value)
        lowered = lax.fori_loop(0, block_rows, forward, jnp.zeros_like(source))

        def backward(turn, result):
            rows_now = starts + (block_rows - 1) - turn
            cols_now = columns[rows_now]
            keep = (cols_now > rows_now[:, None]) & (cols_now < (starts + block_rows)[:, None])
            masked = tiles[rows_now] * keep[:, :, None, None].astype(tiles.dtype)
            picked = jnp.take(result, cols_now, axis=1)
            summed = jnp.einsum('jkab,cjkb->cja', masked, picked, precision=lax.Precision.HIGHEST)
            value = lowered[:, rows_now] - jnp.einsum('jab,cjb->cja', pivots[rows_now], summed, precision=lax.Precision.HIGHEST)
            return result.at[:, rows_now].set(value)
        result = lax.fori_loop(0, block_rows, backward, lowered)
        return result.reshape(RHS, NBR * BS)
    solution = jnp.zeros_like(right_side)
    residual = right_side
    direction = precondition(residual)
    for turn in range(ITERS):
        image = product(direction)
        gram = inner(direction, image)
        factor = jnp.linalg.cholesky(0.5 * (gram + gram.T))
        alpha = chol_solve(factor, inner(direction, residual))
        solution = solution + jnp.dot(alpha.T, direction, precision=lax.Precision.HIGHEST)
        residual = residual - jnp.dot(alpha.T, image, precision=lax.Precision.HIGHEST)
        if turn + 1 < ITERS:
            preconditioned = precondition(residual)
            beta = -chol_solve(factor, inner(image, preconditioned))
            direction = preconditioned + jnp.dot(beta.T, direction, precision=lax.Precision.HIGHEST)
    return (solution, residual)
```

```python
import functools

import jax
import jax.numpy as jnp
from jax import lax
from jax.experimental import pallas as pl
from jax.experimental.pallas import tpu as pltpu
from jax.sharding import PartitionSpec as P

SPAN = 8
BF, F32 = jnp.bfloat16, jnp.float32
MIB = 1 << 20
VMEM = pl.BlockSpec(memory_space=pltpu.VMEM)
SMEM = pl.BlockSpec(memory_space=pltpu.SMEM)


def parts(x, n):
    out = []
    for _ in range(n):
        high = x.astype(BF)
        out.append(high)
        x = x - high.astype(F32)
    return out


def dot(a, b):
    return jnp.dot(a, b, preferred_element_type=F32)


def mul(a, b):
    (ah, al), (bh, bl) = parts(a, 2), parts(b, 2)
    return dot(ah, bh) + (dot(ah, bl) + dot(al, bh))


def times(x, weights):
    n = x.shape[0]
    count = len(weights)
    stack = jnp.concatenate([p.astype(F32) for p in parts(x, count)], axis=0)
    if count * n % 16:
        stack = jnp.concatenate([stack, jnp.zeros((16 - count * n % 16, x.shape[1]), F32)], axis=0)
    stack = stack.astype(BF)
    total = None
    for w in reversed(weights):
        y = dot(stack, w)
        for i in reversed(range(count)):
            y_i = y[i * n : (i + 1) * n]
            total = y_i if total is None else total + y_i
    return total


def setup_kernel(cols, tiles, pivots, dh, dm, dl, nh, nl, th, tl, sh, sl, dense, pf):
    rows, slots, bs = tiles.shape[0], tiles.shape[1], tiles.shape[2]
    cells = rows * bs
    half = cells // 2
    start = lax.axis_index("rows") * rows
    dense[...] = jnp.zeros(dense.shape, F32)
    for i in range(rows):
        for k in range(slots):
            j = cols[i, k] - start + rows
            at = (pl.ds(pl.multiple_of(j * bs, bs), bs), slice(i * bs, (i + 1) * bs))
            dense[at] = dense[at] + tiles[i, k].T
    for at in range(3):
        part = slice(at * cells, (at + 1) * cells)
        for ref, p in zip((dh, dm, dl), parts(dense[part], 3)):
            ref[part] = p

    def block_diagonal(first):
        zero = jnp.zeros((bs, bs), F32)
        count = half // bs
        return jnp.concatenate(
            [
                jnp.concatenate([pivots[first + i] if i == j else zero for j in range(count)], axis=1)
                for i in range(count)
            ],
            axis=0,
        )

    pa, pb = block_diagonal(0), block_diagonal(rows // 2)
    row = lax.broadcasted_iota(jnp.int32, (half, half), 0)
    col = lax.broadcasted_iota(jnp.int32, (half, half), 1)
    same_pair = row // (2 * bs) == col // (2 * bs)
    eye = (row == col).astype(F32)
    lower = row // bs > col // bs

    def inverse(block):
        first = jnp.where(same_pair, block, 0.0)
        rest = block - first
        f = eye - first
        return f - mul(mul(f, rest), f)

    o = cells
    ga = mul(jnp.where(lower, dense[o : o + half, 0:half], 0.0), pa)
    gb = mul(jnp.where(lower, dense[o + half : o + cells, half:cells], 0.0), pb)
    gx = mul(dense[o + half : o + cells, 0:half], pa)
    fa, fb = inverse(ga), inverse(gb)
    fx = -mul(mul(fb, gx), fa)
    pf[0:half, 0:half] = mul(pa, fa)
    pf[0:half, half:cells] = jnp.zeros((half, half), F32)
    pf[half:cells, 0:half] = mul(pb, fx)
    pf[half:cells, half:cells] = mul(pb, fb)
    right = pf[...]
    n = mul(dense[2 * cells : 3 * cells], right)
    nh[...], nl[...] = parts(n, 2)
    th[...], tl[...] = parts(n.T, 2)
    fxt, fbt = fx.T, fb.T
    low = mul(fbt, right[half:cells])
    sh[half:cells], sl[half:cells] = parts(low, 2)
    high = mul(fxt, right[half:cells])
    corner = mul(fa.T, right[0:half, 0:half])
    high = jnp.concatenate([high[:, 0:half] + corner, high[:, half:cells]], axis=1)
    sh[0:half], sl[0:half] = parts(high, 2)


def setup(cols, tiles, pivots):
    rows, _, bs, _ = tiles.shape
    cells = rows * bs
    shapes = [(3 * cells, cells)] * 3 + [(cells, cells)] * 6
    return pl.pallas_call(
        setup_kernel,
        out_shape=[jax.ShapeDtypeStruct(s, BF) for s in shapes],
        in_specs=[SMEM, VMEM, VMEM],
        out_specs=[VMEM] * 9,
        scratch_shapes=[pltpu.VMEM((3 * cells, cells), F32), pltpu.VMEM((cells, cells), F32)],
        compiler_params=pltpu.CompilerParams(vmem_limit_bytes=40 * MIB),
    )(cols, tiles, pivots)


def krylov_kernel(
    nr, nz,
    r, dh, dm, dl, nh, nl, th, tl, sh, sl,
    v_out, w_out, k_out, r_out,
    va, wa, fsrc, fdst, above, below, c, red_x, red_y, red_z,
    f_send, f_recv, b_send, b_recv, h_send, h_recv,
    z_send, z_recv, x_send, x_recv, y_send, y_recv, k_send, k_recv,
):
    me, mz = lax.axis_index("rows"), lax.axis_index("rhs")
    pos, where = lax.rem(me, SPAN), lax.div(me, SPAN)
    ny = nr // SPAN
    first, last = pos == 0, pos == SPAN - 1
    cells = r.shape[1]

    def x_peer(o):
        return (where * SPAN + lax.rem(pos + o, SPAN), mz)

    def y_peer(o):
        return (lax.rem(where + o, ny) * SPAN + pos, mz)

    def z_peer(o):
        return (me, lax.rem(mz + o, nz))

    barrier = pltpu.get_barrier_semaphore()

    def hello(device):
        pl.semaphore_signal(barrier, inc=1, device_id=device, device_id_type=pl.DeviceIdType.MESH)

    for o in range(1, SPAN):
        hello(x_peer(o))
    for o in range(1, ny):
        hello(y_peer(o))
    for o in range(1, nz):
        hello(z_peer(o))
    from_before, to_next = first & (me > 0), last & (me < nr - 1)

    @pl.when(from_before)
    def _():
        hello((me - 1, mz))

    @pl.when(to_next)
    def _():
        hello((me + 1, mz))

    edges = from_before.astype(jnp.int32) + to_next.astype(jnp.int32)
    pl.semaphore_wait(barrier, SPAN - 1 + ny - 1 + nz - 1 + edges)

    def copy(src, dst, send, recv, device):
        return pltpu.make_async_remote_copy(
            src_ref=src, dst_ref=dst, send_sem=send, recv_sem=recv,
            device_id=device, device_id_type=pl.DeviceIdType.MESH,
        )

    def to_z(array, m, kind):
        return [
            copy(array.at[mz, m], array.at[mz, m], z_send.at[kind, o - 1], z_recv.at[kind, o - 1], z_peer(o))
            for o in range(1, nz)
        ]

    def spread(array, at, send, recv, peer, count):
        return [
            copy(array.at[at], array.at[at], send.at[o - 1], recv.at[o - 1], peer(o)) for o in range(1, count)
        ]

    begun = []
    has_before, has_next = me > 0, me < nr - 1

    @pl.when(me == 0)
    def _():
        below[...] = jnp.zeros(below.shape, F32)

    @pl.when(me == nr - 1)
    def _():
        above[...] = jnp.zeros(above.shape, F32)

    n_parts, t_parts, s_parts = (nh, nl), (th, tl), (sh, sl)

    def values(refs, rows=slice(None)):
        return [ref[rows] for ref in refs]

    for m in range(2):
        source = r if m == 0 else wa.at[mz, 0]
        ahead = copy(fsrc.at[m], fdst.at[m], f_send.at[m], f_recv.at[m], (me + 1, mz))
        back = copy(va.at[mz, m], above.at[m], b_send.at[m], b_recv.at[m], (me - 1, mz))
        on = copy(va.at[mz, m], below.at[m], h_send.at[m], h_recv.at[m], (me + 1, mz))

        @pl.when(first)
        def _():
            c[...] = source[...]

        @pl.when(jnp.logical_not(first))
        def _():
            ahead.wait_recv()
            c[...] = source[...] - fdst[m]

        @pl.when(jnp.logical_not(last))
        def _():
            fsrc[m] = times(c[...], values(t_parts))
            ahead.start()

        c[...] = times(c[...], values(s_parts))

        @pl.when(last)
        def _():
            va[mz, m] = c[...]

        @pl.when(jnp.logical_not(last))
        def _():
            back.wait_recv()
            va[mz, m] = c[...] - times(above[m], values(n_parts))

        @pl.when(has_before)
        def _():
            back.start()

        @pl.when(has_next)
        def _():
            on.start()

        sent = to_z(va, m, 2 * m)
        for s in sent:
            s.start()
        begun += sent

        d = (dh, dm, dl)
        q = times(va[mz, m], values(d, slice(cells, 2 * cells)))

        @pl.when(to_next)
        def _():
            back.wait_recv()

        q = q + times(above[m], values(d, slice(2 * cells, 3 * cells)))

        @pl.when(has_before)
        def _():
            on.wait_recv()

        wa[mz, m] = q + times(below[m], values(d, slice(0, cells)))
        sent = to_z(wa, m, 2 * m + 1)
        for s in sent:
            s.start()
        begun += sent

    for m in range(2):
        for s in to_z(va, m, 2 * m):
            s.wait_recv()
    left = jnp.concatenate([wa[mz, 0], wa[mz, 1], r[...]], axis=0)
    right = va[...].reshape(nz * 16, cells)
    red_x[pos] = lax.dot_general(
        left, right, (((1,), (1,)), ((), ())), precision=lax.Precision.HIGHEST, preferred_element_type=F32
    )

    def exchange(array, at, send, recv, peer, count):
        sent = spread(array, at, send, recv, peer, count)
        for s in sent:
            s.start()
        for s in sent:
            s.wait_recv()
        return sent

    def total(array, count):
        value = array[0]
        for i in range(1, count):
            value = value + array[i]
        return value

    begun += exchange(red_x, pos, x_send, x_recv, x_peer, SPAN)
    red_y[where] = total(red_x, SPAN)
    begun += exchange(red_y, where, y_send, y_recv, y_peer, ny)
    whole = total(red_y, ny)
    r_out[...] = whole[16:24]
    red_z[mz] = whole[0:16]
    begun += exchange(red_z, mz, k_send, k_recv, z_peer, nz)
    k_out[...] = red_z[...].reshape(nz * 16, nz * 16)
    for m in range(2):
        for s in to_z(wa, m, 2 * m + 1):
            s.wait_recv()
    v_out[...] = va[...].reshape(nz * 16, cells)
    w_out[...] = wa[...].reshape(nz * 16, cells)
    for s in begun:
        s.wait_send()
    for m in range(2):
        ahead = copy(fsrc.at[m], fdst.at[m], f_send.at[m], f_recv.at[m], (me + 1, mz))
        back = copy(va.at[mz, m], above.at[m], b_send.at[m], b_recv.at[m], (me - 1, mz))
        on = copy(va.at[mz, m], below.at[m], h_send.at[m], h_recv.at[m], (me + 1, mz))

        @pl.when(jnp.logical_not(last))
        def _():
            ahead.wait_send()

        @pl.when(has_before)
        def _():
            back.wait_send()

        @pl.when(has_next)
        def _():
            on.wait_send()


def krylov(nr, nz, r, matrices):
    rhs, cells = r.shape
    ny = nr // SPAN
    dma = pltpu.SemaphoreType.DMA
    every = nz * 2 * rhs
    return pl.pallas_call(
        functools.partial(krylov_kernel, nr, nz),
        out_shape=[
            jax.ShapeDtypeStruct((every, cells), F32),
            jax.ShapeDtypeStruct((every, cells), F32),
            jax.ShapeDtypeStruct((every, every), F32),
            jax.ShapeDtypeStruct((rhs, every), F32),
        ],
        in_specs=[VMEM] * 10,
        out_specs=[VMEM] * 4,
        scratch_shapes=[
            pltpu.VMEM((nz, 2, rhs, cells), F32),
            pltpu.VMEM((nz, 2, rhs, cells), F32),
            pltpu.VMEM((2, rhs, cells), F32),
            pltpu.VMEM((2, rhs, cells), F32),
            pltpu.VMEM((2, rhs, cells), F32),
            pltpu.VMEM((2, rhs, cells), F32),
            pltpu.VMEM((rhs, cells), F32),
            pltpu.VMEM((SPAN, 3 * rhs, every), F32),
            pltpu.VMEM((ny, 3 * rhs, every), F32),
            pltpu.VMEM((nz, 2 * rhs, every), F32),
        ]
        + [dma((2,))] * 6
        + [dma((4, max(nz - 1, 1)))] * 2
        + [dma((SPAN - 1,))] * 2
        + [dma((max(ny - 1, 1),))] * 2
        + [dma((max(nz - 1, 1),))] * 2,
        compiler_params=pltpu.CompilerParams(
            collective_id=0, has_side_effects=True, vmem_limit_bytes=24 * MIB
        ),
    )(r, *matrices)


def solve_kernel(k_in, rt, v, w, r, x_out, r_out):
    size = k_in.shape[0]
    k = 0.5 * (k_in[...] + k_in[...].T)
    row_of = lax.broadcasted_iota(jnp.int32, (size, 1), 0)
    col_of = lax.broadcasted_iota(jnp.int32, (1, size), 1)
    for step in range(size):
        inv = 1.0 / k[step : step + 1, step : step + 1]
        row = jnp.where(col_of == step, 1.0, k[step : step + 1, :]) * inv
        col = jnp.where(row_of == step, -1.0, k[:, step : step + 1])
        k = jnp.where((row_of == step) | (col_of == step), 0.0, k) - col * row
    high = lax.Precision.HIGHEST
    c = jnp.dot(rt[...], k, precision=high, preferred_element_type=F32)
    x_out[...] = jnp.dot(c, v[...], precision=high, preferred_element_type=F32)
    r_out[...] = r[...] - jnp.dot(c, w[...], precision=high, preferred_element_type=F32)


def solve(k, rt, v, w, r):
    return pl.pallas_call(
        solve_kernel,
        out_shape=[jax.ShapeDtypeStruct(r.shape, F32)] * 2,
        in_specs=[VMEM] * 5,
        out_specs=[VMEM] * 2,
        compiler_params=pltpu.CompilerParams(vmem_limit_bytes=16 * MIB),
    )(k, rt, v, w, r)


def solution(mesh):
    nr, nz = mesh.shape["rows"], mesh.shape["rhs"]

    def shards(right_side, tiles, pivots, columns):
        matrices = setup(columns, tiles, pivots)
        v, w, k, rt = krylov(nr, nz, right_side, matrices)
        return tuple(solve(k, rt, v, w, right_side))

    return jax.shard_map(
        shards,
        mesh=mesh,
        in_specs=(
            P("rhs", "rows"),
            P("rows", None, None, None),
            P("rows", None, None),
            P("rows", None),
        ),
        out_specs=(P("rhs", "rows"), P("rhs", "rows")),
        check_vma=False,
    )
```

```python
import functools

import jax
import jax.numpy as jnp
from jax import lax
from jax.experimental import pallas as pl
from jax.experimental.pallas import tpu as pltpu
from jax.sharding import PartitionSpec as P

SPAN = 8
BF, F32 = jnp.bfloat16, jnp.float32
MIB = 1 << 20
VMEM = pl.BlockSpec(memory_space=pltpu.VMEM)
SMEM = pl.BlockSpec(memory_space=pltpu.SMEM)


def parts(x, n):
    out = []
    for _ in range(n):
        high = x.astype(BF)
        out.append(high)
        x = x - high.astype(F32)
    return out


def dot(a, b):
    return jnp.dot(a, b, preferred_element_type=F32)


def mul(a, b):
    (ah, al), (bh, bl) = parts(a, 2), parts(b, 2)
    return dot(ah, bh) + (dot(ah, bl) + dot(al, bh))


def times(x, weights):
    n = x.shape[0]
    count = len(weights)
    stack = jnp.concatenate([p.astype(F32) for p in parts(x, count)], axis=0)
    if count * n % 16:
        stack = jnp.concatenate([stack, jnp.zeros((16 - count * n % 16, x.shape[1]), F32)], axis=0)
    stack = stack.astype(BF)
    total = None
    for w in reversed(weights):
        y = dot(stack, w)
        for i in reversed(range(count)):
            y_i = y[i * n : (i + 1) * n]
            total = y_i if total is None else total + y_i
    return total


def setup_kernel(cols, tiles, pivots, dh, dm, dl, nh, nl, th, tl, sh, sl, tf, sf, dense, pf):
    rows, slots, bs = tiles.shape[0], tiles.shape[1], tiles.shape[2]
    cells = rows * bs
    half = cells // 2
    start = lax.axis_index("rows") * rows
    dense[...] = jnp.zeros(dense.shape, F32)
    for i in range(rows):
        for k in range(slots):
            j = cols[i, k] - start + rows
            at = (pl.ds(pl.multiple_of(j * bs, bs), bs), slice(i * bs, (i + 1) * bs))
            dense[at] = dense[at] + tiles[i, k].T
    for at in range(3):
        part = slice(at * cells, (at + 1) * cells)
        for ref, p in zip((dh, dm, dl), parts(dense[part], 3)):
            ref[part] = p

    def block_diagonal(first):
        zero = jnp.zeros((bs, bs), F32)
        count = half // bs
        return jnp.concatenate(
            [
                jnp.concatenate([pivots[first + i] if i == j else zero for j in range(count)], axis=1)
                for i in range(count)
            ],
            axis=0,
        )

    pa, pb = block_diagonal(0), block_diagonal(rows // 2)
    row = lax.broadcasted_iota(jnp.int32, (half, half), 0)
    col = lax.broadcasted_iota(jnp.int32, (half, half), 1)
    same_pair = row // (2 * bs) == col // (2 * bs)
    eye = (row == col).astype(F32)
    lower = row // bs > col // bs

    def inverse(block):
        first = jnp.where(same_pair, block, 0.0)
        rest = block - first
        f = eye - first
        return f - mul(mul(f, rest), f)

    o = cells
    ga = mul(jnp.where(lower, dense[o : o + half, 0:half], 0.0), pa)
    gb = mul(jnp.where(lower, dense[o + half : o + cells, half:cells], 0.0), pb)
    gx = mul(dense[o + half : o + cells, 0:half], pa)
    fa, fb = inverse(ga), inverse(gb)
    fx = -mul(mul(fb, gx), fa)
    pf[0:half, 0:half] = mul(pa, fa)
    pf[0:half, half:cells] = jnp.zeros((half, half), F32)
    pf[half:cells, 0:half] = mul(pb, fx)
    pf[half:cells, half:cells] = mul(pb, fb)
    right = pf[...]
    n = mul(dense[2 * cells : 3 * cells], right)
    nh[...], nl[...] = parts(n, 2)
    nt = n.T
    tf[...] = nt
    th[...], tl[...] = parts(nt, 2)
    fxt, fbt = fx.T, fb.T
    low = mul(fbt, right[half:cells])
    sf[half:cells] = low
    sh[half:cells], sl[half:cells] = parts(low, 2)
    high = mul(fxt, right[half:cells])
    corner = mul(fa.T, right[0:half, 0:half])
    high = jnp.concatenate([high[:, 0:half] + corner, high[:, half:cells]], axis=1)
    sf[0:half] = high
    sh[0:half], sl[0:half] = parts(high, 2)


def setup(cols, tiles, pivots):
    rows, _, bs, _ = tiles.shape
    cells = rows * bs
    shapes = [(3 * cells, cells)] * 3 + [(cells, cells)] * 6
    return pl.pallas_call(
        setup_kernel,
        out_shape=[jax.ShapeDtypeStruct(s, BF) for s in shapes] + [jax.ShapeDtypeStruct((cells, cells), F32)] * 2,
        in_specs=[SMEM, VMEM, VMEM],
        out_specs=[VMEM] * 11,
        scratch_shapes=[pltpu.VMEM((3 * cells, cells), F32), pltpu.VMEM((cells, cells), F32)],
        compiler_params=pltpu.CompilerParams(vmem_limit_bytes=40 * MIB),
    )(cols, tiles, pivots)


def mul_parts(a, b):
    (ah, al), (bh, bl) = a, b
    return dot(ah, bh) + (dot(ah, bl) + dot(al, bh))


def krylov_kernel(
    nr, nz,
    r, dh, dm, dl, nh, nl, th, tl, sh, sl, tf, sf,
    v_out, w_out, k_out, r_out,
    va, wa, c, sv, other, joint,
    u_src, u_dst, s_src, s_dst, k_src, k_dst, w_src, w_dst, far, above, below,
    red_x, red_y, red_z,
    link_send, link_recv, pair_send, pair_recv,
    z_send, z_recv, x_send, x_recv, y_send, y_recv, k_send, k_recv,
):
    me, mz = lax.axis_index("rows"), lax.axis_index("rhs")
    pos, where = lax.rem(me, SPAN), lax.div(me, SPAN)
    chip, odd = lax.div(pos, 2), lax.rem(pos, 2) == 1
    even = jnp.logical_not(odd)
    chips = SPAN // 2
    ny = nr // SPAN
    first, last = pos == 0, pos == SPAN - 1
    cells = r.shape[1]

    def x_peer(o):
        return (where * SPAN + lax.rem(pos + o, SPAN), mz)

    def y_peer(o):
        return (lax.rem(where + o, ny) * SPAN + pos, mz)

    def z_peer(o):
        return (me, lax.rem(mz + o, nz))

    barrier = pltpu.get_barrier_semaphore()

    def hello(device):
        pl.semaphore_signal(barrier, inc=1, device_id=device, device_id_type=pl.DeviceIdType.MESH)

    for o in range(1, SPAN):
        hello(x_peer(o))
    for o in range(1, ny):
        hello(y_peer(o))
    for o in range(1, nz):
        hello(z_peer(o))
    has_before, has_next = me > 0, me < nr - 1
    from_before, to_next = first & has_before, last & has_next

    @pl.when(from_before)
    def _():
        hello((me - 1, mz))

    @pl.when(to_next)
    def _():
        hello((me + 1, mz))

    edges = from_before.astype(jnp.int32) + to_next.astype(jnp.int32)
    pl.semaphore_wait(barrier, SPAN - 1 + ny - 1 + nz - 1 + edges)

    def copy(src, dst, send, recv, device):
        return pltpu.make_async_remote_copy(
            src_ref=src, dst_ref=dst, send_sem=send, recv_sem=recv,
            device_id=device, device_id_type=pl.DeviceIdType.MESH,
        )

    def link(kind, m, src, dst, device):
        return copy(src, dst.at[m], link_send.at[kind, m], link_recv.at[kind, m], (device, mz))

    def links(m):
        z = va.at[mz, m]
        return dict(
            u=link(0, m, u_src.at[m], u_dst, me + 1),
            s=link(1, m, s_src.at[m], s_dst, me - 1),
            k=link(2, m, k_src.at[m], k_dst, me + 2),
            w=link(3, m, w_src.at[m], w_dst, me + 1),
            far=link(4, m, z, far, me - 2),
            back=link(5, m, z, above, me - 1),
            on=link(6, m, z, below, me + 1),
        )

    def to_z(array, m, kind):
        return [
            copy(array.at[mz, m], array.at[mz, m], z_send.at[kind, o - 1], z_recv.at[kind, o - 1], z_peer(o))
            for o in range(1, nz)
        ]

    def spread(array, at, send, recv, peer, count):
        return [
            copy(array.at[at], array.at[at], send.at[o - 1], recv.at[o - 1], peer(o)) for o in range(1, count)
        ]

    begun = []

    def begin(copies):
        for s in copies:
            s.start()
        begun.extend(copies)

    pair = [
        copy(ref, other.at[i], pair_send.at[i], pair_recv.at[i], (me - 1, mz)) for i, ref in enumerate((tf, sf))
    ]

    @pl.when(odd)
    def _():
        for p in pair:
            p.start()

    @pl.when(me == 0)
    def _():
        below[...] = jnp.zeros(below.shape, F32)

    @pl.when(me == nr - 1)
    def _():
        above[...] = jnp.zeros(above.shape, F32)

    def values(refs, rows=slice(None)):
        return [ref[rows] for ref in refs]

    n_refs, t_refs, s_refs = (nh, nl), (th, tl), (sh, sl)
    kt_refs, k_refs, e_refs = ((joint.at[2 * i], joint.at[2 * i + 1]) for i in range(3))

    def product_of_two():
        pair[0].wait_recv()
        kt = mul_parts(values(t_refs), parts(other[0], 2))
        for ref, p in zip(kt_refs, parts(kt, 2)):
            ref[...] = p
        return kt

    def middle_of_two():
        pair[1].wait_recv()
        x = mul_parts(parts(other[1], 2), values(n_refs))
        e = sf[...] + mul_parts(values(t_refs), parts(x, 2))
        for ref, p in zip(e_refs, parts(e, 2)):
            ref[...] = p
        k = (kt_refs[0][...].astype(F32) + kt_refs[1][...].astype(F32)).T
        for ref, p in zip(k_refs, parts(k, 2)):
            ref[...] = p

    @pl.when(even)
    def _():
        product_of_two()

    for m in range(2):
        source = r if m == 0 else wa.at[mz, 0]
        at = links(m)

        def prepare():
            if m == 0:
                middle_of_two()
            at["s"].wait_recv()
            sv[...] = times(s_dst[m], values(n_refs))

        @pl.when(odd & (chip < chips - 1))
        def _():
            u_src[m] = times(source[...], values(t_refs))
            at["u"].start()

        @pl.when(odd)
        def _():
            s_src[m] = times(source[...], values(s_refs))
            at["s"].start()
            at["w"].wait_recv()
            c[...] = times(source[...] - w_dst[m], values(s_refs))

        @pl.when(odd & (chip < chips - 1))
        def _():
            at["back"].wait_recv()
            va[mz, m] = c[...] - times(above[m], values(n_refs))

        @pl.when(last)
        def _():
            va[mz, m] = c[...]

        @pl.when(first)
        def _():
            c[...] = source[...]

        @pl.when(even & (chip > 0))
        def _():
            prepare()
            at["u"].wait_recv()
            at["k"].wait_recv()
            c[...] = source[...] - u_dst[m] + k_dst[m]

        @pl.when(even & (chip < chips - 1))
        def _():
            k_src[m] = times(c[...], values(kt_refs))
            at["k"].start()

        @pl.when(even)
        def _():
            w_src[m] = times(c[...], values(t_refs))
            at["w"].start()

        @pl.when(first)
        def _():
            prepare()

        @pl.when(even)
        def _():
            c[...] = times(c[...], values(e_refs)) - sv[...]

        @pl.when(even & (chip < chips - 1))
        def _():
            at["far"].wait_recv()
            va[mz, m] = c[...] + times(far[m], values(k_refs))

        @pl.when(even & (chip == chips - 1))
        def _():
            va[mz, m] = c[...]

        @pl.when(even & (chip > 0))
        def _():
            at["far"].start()

        @pl.when(has_before)
        def _():
            at["back"].start()

        @pl.when(has_next)
        def _():
            at["on"].start()

        begin(to_z(va, m, 2 * m))

        d = (dh, dm, dl)

        def part(value, i):
            return times(value, values(d, slice(i * cells, (i + 1) * cells)))

        c[...] = part(va[mz, m], 1)

        @pl.when(from_before)
        def _():
            at["on"].wait_recv()

        @pl.when(first)
        def _():
            wa[mz, m] = part(below[m], 0)

        @pl.when(jnp.logical_not(odd) )
        def _():
            at["back"].wait_recv()

        @pl.when(jnp.logical_not(last))
        def _():
            sv[...] = part(above[m], 2)

        if m == 1:
            @pl.when(first)
            def _():
                far[0] = 0.5 * c[...] + sv[...] + wa[mz, m]

            @pl.when(jnp.logical_not(first | last))
            def _():
                far[0] = 0.5 * c[...] + sv[...]

            @pl.when(last)
            def _():
                far[0] = 0.5 * c[...]

            for kind in range(2):
                for s in to_z(va, kind, 2 * kind):
                    s.wait_recv()
            left = jnp.concatenate([wa[mz, 0], far[0], r[...]], axis=0)
            right = va[...].reshape(nz * 16, cells)
            red_x[pos] = lax.dot_general(
                left, right, (((1,), (1,)), ((), ())),
                precision=lax.Precision.HIGHEST, preferred_element_type=F32,
            )
            over_x = spread(red_x, pos, x_send, x_recv, x_peer, SPAN)
            begin(over_x)

        @pl.when(to_next)
        def _():
            at["back"].wait_recv()

        @pl.when(last)
        def _():
            sv[...] = part(above[m], 2)

        @pl.when(has_before & jnp.logical_not(first))
        def _():
            at["on"].wait_recv()

        @pl.when(jnp.logical_not(first))
        def _():
            wa[mz, m] = part(below[m], 0)

        wa[mz, m] = c[...] + sv[...] + wa[mz, m]
        begin(to_z(wa, m, 2 * m + 1))

    def total(array, count):
        value = array[0]
        for i in range(1, count):
            value = value + array[i]
        return value

    for s in over_x:
        s.wait_recv()
    red_y[where] = total(red_x, SPAN)
    over_y = spread(red_y, where, y_send, y_recv, y_peer, ny)
    begin(over_y)
    for s in over_y:
        s.wait_recv()
    whole = total(red_y, ny)
    r_out[...] = whole[16:24]
    red_z[mz] = whole[0:16]
    over_z = spread(red_z, mz, k_send, k_recv, z_peer, nz)
    begin(over_z)
    for m in range(2):
        for s in to_z(wa, m, 2 * m + 1):
            s.wait_recv()
    v_out[...] = va[...].reshape(nz * 16, cells)
    w_out[...] = wa[...].reshape(nz * 16, cells)
    for s in over_z:
        s.wait_recv()
    k_out[...] = red_z[...].reshape(nz * 16, nz * 16)
    for s in begun:
        s.wait_send()

    @pl.when(odd)
    def _():
        for p in pair:
            p.wait_send()

    for m in range(2):
        at = links(m)
        for name, started in (
            ("u", odd & (chip < chips - 1)),
            ("s", odd),
            ("k", even & (chip < chips - 1)),
            ("w", even),
            ("far", even & (chip > 0)),
            ("back", has_before),
            ("on", has_next),
        ):

            @pl.when(started)
            def _():
                at[name].wait_send()


def krylov(nr, nz, r, matrices):
    rhs, cells = r.shape
    ny = nr // SPAN
    dma = pltpu.SemaphoreType.DMA
    every = nz * 2 * rhs
    vector = pltpu.VMEM((rhs, cells), F32)
    vectors = pltpu.VMEM((2, rhs, cells), F32)
    return pl.pallas_call(
        functools.partial(krylov_kernel, nr, nz),
        out_shape=[
            jax.ShapeDtypeStruct((every, cells), F32),
            jax.ShapeDtypeStruct((every, cells), F32),
            jax.ShapeDtypeStruct((every, every), F32),
            jax.ShapeDtypeStruct((rhs, every), F32),
        ],
        in_specs=[VMEM] * 12,
        out_specs=[VMEM] * 4,
        scratch_shapes=[pltpu.VMEM((nz, 2, rhs, cells), F32)] * 2
        + [vector] * 2
        + [pltpu.VMEM((2, cells, cells), F32), pltpu.VMEM((6, cells, cells), BF)]
        + [vectors] * 11
        + [
            pltpu.VMEM((SPAN, 3 * rhs, every), F32),
            pltpu.VMEM((ny, 3 * rhs, every), F32),
            pltpu.VMEM((nz, 2 * rhs, every), F32),
        ]
        + [dma((7, 2))] * 2
        + [dma((2,))] * 2
        + [dma((4, max(nz - 1, 1)))] * 2
        + [dma((SPAN - 1,))] * 2
        + [dma((max(ny - 1, 1),))] * 2
        + [dma((max(nz - 1, 1),))] * 2,
        compiler_params=pltpu.CompilerParams(
            collective_id=0, has_side_effects=True, vmem_limit_bytes=32 * MIB
        ),
    )(r, *matrices)


def solve_kernel(k_in, rt, v, w, r, x_out, r_out):
    size = k_in.shape[0]
    k = k_in[...]
    kt = k.T
    row_of = lax.broadcasted_iota(jnp.int32, (size, 1), 0)
    col_of = lax.broadcasted_iota(jnp.int32, (1, size), 1)
    row_p, col_p = lax.rem(row_of // 8, 2) == 1, lax.rem(col_of // 8, 2) == 1
    both = k + kt
    k = jnp.where(row_p, jnp.where(col_p, both, kt), jnp.where(col_p, k, 0.5 * both))
    for i in range(0, size, 2):
        j = i + 1
        a, b, d = k[i : i + 1, i : i + 1], k[i : i + 1, j : j + 1], k[j : j + 1, j : j + 1]
        inv = 1.0 / (a * d - b * b)
        ra = jnp.where(col_of == i, 1.0, jnp.where(col_of == j, 0.0, k[i : i + 1, :]))
        rb = jnp.where(col_of == j, 1.0, jnp.where(col_of == i, 0.0, k[j : j + 1, :]))
        new_a, new_b = (d * ra - b * rb) * inv, (a * rb - b * ra) * inv
        ca = jnp.where(row_of == i, -1.0, jnp.where(row_of == j, 0.0, k[:, i : i + 1]))
        cb = jnp.where(row_of == j, -1.0, jnp.where(row_of == i, 0.0, k[:, j : j + 1]))
        gone = (row_of == i) | (row_of == j) | (col_of == i) | (col_of == j)
        k = jnp.where(gone, 0.0, k) - ca * new_a - cb * new_b
    high = lax.Precision.HIGHEST
    c = jnp.dot(rt[...], k, precision=high, preferred_element_type=F32)
    x_out[...] = jnp.dot(c, v[...], precision=high, preferred_element_type=F32)
    r_out[...] = r[...] - jnp.dot(c, w[...], precision=high, preferred_element_type=F32)


def solve(k, rt, v, w, r):
    return pl.pallas_call(
        solve_kernel,
        out_shape=[jax.ShapeDtypeStruct(r.shape, F32)] * 2,
        in_specs=[VMEM] * 5,
        out_specs=[VMEM] * 2,
        compiler_params=pltpu.CompilerParams(vmem_limit_bytes=16 * MIB),
    )(k, rt, v, w, r)


def solution(mesh):
    nr, nz = mesh.shape["rows"], mesh.shape["rhs"]

    def shards(right_side, tiles, pivots, columns):
        matrices = setup(columns, tiles, pivots)
        v, w, k, rt = krylov(nr, nz, right_side, matrices)
        return tuple(solve(k, rt, v, w, right_side))

    return jax.shard_map(
        shards,
        mesh=mesh,
        in_specs=(
            P("rhs", "rows"),
            P("rows", None, None, None),
            P("rows", None, None),
            P("rows", None),
        ),
        out_specs=(P("rhs", "rows"), P("rhs", "rows")),
        check_vma=False,
    )
```

```python
import functools

import jax
import jax.numpy as jnp
from jax import lax
from jax.experimental import pallas as pl
from jax.experimental.pallas import tpu as pltpu
from jax.sharding import PartitionSpec as P

SPAN = 8
BF, F32 = jnp.bfloat16, jnp.float32
MIB = 1 << 20
VMEM = pl.BlockSpec(memory_space=pltpu.VMEM)
SMEM = pl.BlockSpec(memory_space=pltpu.SMEM)


def parts(x, n):
    out = []
    for _ in range(n):
        high = x.astype(BF)
        out.append(high)
        x = x - high.astype(F32)
    return out


def dot(a, b):
    return jnp.dot(a, b, preferred_element_type=F32)


def mul(a, b):
    (ah, al), (bh, bl) = parts(a, 2), parts(b, 2)
    return dot(ah, bh) + (dot(ah, bl) + dot(al, bh))


def times(x, weights):
    n = x.shape[0]
    count = len(weights)
    stack = jnp.concatenate([p.astype(F32) for p in parts(x, count)], axis=0)
    if count * n % 16:
        stack = jnp.concatenate([stack, jnp.zeros((16 - count * n % 16, x.shape[1]), F32)], axis=0)
    stack = stack.astype(BF)
    total = None
    for w in reversed(weights):
        y = dot(stack, w)
        for i in reversed(range(count)):
            y_i = y[i * n : (i + 1) * n]
            total = y_i if total is None else total + y_i
    return total


def assemble_kernel(cols, tiles, dense, held, sems):
    rows, slots, bs = held.shape[0], held.shape[1], held.shape[2]
    start = lax.axis_index("rows") * rows
    copies = [pltpu.make_async_copy(tiles.at[i], held.at[i], sems.at[i]) for i in range(rows)]
    for c in copies:
        c.start()
    dense[...] = jnp.zeros(dense.shape, F32)
    for i in range(rows):
        copies[i].wait()
        for k in range(slots):
            j = cols[i, k] - start + rows
            at = (pl.ds(pl.multiple_of(j * bs, bs), bs), slice(i * bs, (i + 1) * bs))
            dense[at] = dense[at] + held[i, k].T


def assemble(cols, tiles):
    rows, _, bs, _ = tiles.shape
    cells = rows * bs
    return pl.pallas_call(
        assemble_kernel,
        out_shape=jax.ShapeDtypeStruct((3 * cells, cells), F32),
        in_specs=[SMEM, pl.BlockSpec(memory_space=pltpu.HBM)],
        out_specs=VMEM,
        scratch_shapes=[pltpu.VMEM(tiles.shape, F32), pltpu.SemaphoreType.DMA((rows,))],
        compiler_params=pltpu.CompilerParams(vmem_limit_bytes=16 * MIB),
    )(cols, tiles)


def mul_parts(a, b):
    (ah, al), (bh, bl) = a, b
    return dot(ah, bh) + (dot(ah, bl) + dot(al, bh))


def krylov_kernel(
    nr, nz,
    r, dense, pivots,
    v_out, w_out, k_out, r_out,
    dh, dm, dl, nh, nl, th, tl, sh, sl, tf, sf, pf,
    va, wa, c, sv, other, joint,
    u_src, u_dst, s_src, s_dst, k_src, k_dst, w_src, w_dst, far, above, below,
    red_x, red_y, red_z,
    link_send, link_recv, pair_send, pair_recv,
    z_send, z_recv, x_send, x_recv, y_send, y_recv, k_send, k_recv,
):
    me, mz = lax.axis_index("rows"), lax.axis_index("rhs")
    pos, where = lax.rem(me, SPAN), lax.div(me, SPAN)
    chip, odd = lax.div(pos, 2), lax.rem(pos, 2) == 1
    even = jnp.logical_not(odd)
    chips = SPAN // 2
    ny = nr // SPAN
    first, last = pos == 0, pos == SPAN - 1
    cells = r.shape[1]

    def x_peer(o):
        return (where * SPAN + lax.rem(pos + o, SPAN), mz)

    def y_peer(o):
        return (lax.rem(where + o, ny) * SPAN + pos, mz)

    def z_peer(o):
        return (me, lax.rem(mz + o, nz))

    barrier = pltpu.get_barrier_semaphore()

    def hello(device):
        pl.semaphore_signal(barrier, inc=1, device_id=device, device_id_type=pl.DeviceIdType.MESH)

    for o in range(1, SPAN):
        hello(x_peer(o))
    for o in range(1, ny):
        hello(y_peer(o))
    for o in range(1, nz):
        hello(z_peer(o))
    has_before, has_next = me > 0, me < nr - 1
    from_before, to_next = first & has_before, last & has_next

    @pl.when(from_before)
    def _():
        hello((me - 1, mz))

    @pl.when(to_next)
    def _():
        hello((me + 1, mz))

    bs = pivots.shape[1]
    half = cells // 2

    def block_diagonal(first_row):
        zero = jnp.zeros((bs, bs), F32)
        count = half // bs
        return jnp.concatenate(
            [
                jnp.concatenate([pivots[first_row + i] if i == j else zero for j in range(count)], axis=1)
                for i in range(count)
            ],
            axis=0,
        )

    pa, pb = block_diagonal(0), block_diagonal(half // bs)
    row = lax.broadcasted_iota(jnp.int32, (half, half), 0)
    col = lax.broadcasted_iota(jnp.int32, (half, half), 1)
    same_pair = row // (2 * bs) == col // (2 * bs)
    eye = (row == col).astype(F32)
    lower = row // bs > col // bs

    def inverse(block):
        within = jnp.where(same_pair, block, 0.0)
        f = eye - within
        return f - mul(mul(f, block - within), f)

    o = cells
    ga = mul(jnp.where(lower, dense[o : o + half, 0:half], 0.0), pa)
    gb = mul(jnp.where(lower, dense[o + half : o + cells, half:cells], 0.0), pb)
    gx = mul(dense[o + half : o + cells, 0:half], pa)
    fa, fb = inverse(ga), inverse(gb)
    fx = -mul(mul(fb, gx), fa)
    pf[0:half, 0:half] = mul(pa, fa)
    pf[0:half, half:cells] = jnp.zeros((half, half), F32)
    pf[half:cells, 0:half] = mul(pb, fx)
    pf[half:cells, half:cells] = mul(pb, fb)
    n = mul(dense[2 * cells : 3 * cells], pf[...])
    nh[...], nl[...] = parts(n, 2)
    nt = n.T
    tf[...] = nt
    th[...], tl[...] = parts(nt, 2)

    edges = from_before.astype(jnp.int32) + to_next.astype(jnp.int32)
    pl.semaphore_wait(barrier, SPAN - 1 + ny - 1 + nz - 1 + edges)

    def copy(src, dst, send, recv, device):
        return pltpu.make_async_remote_copy(
            src_ref=src, dst_ref=dst, send_sem=send, recv_sem=recv,
            device_id=device, device_id_type=pl.DeviceIdType.MESH,
        )

    def link(kind, m, src, dst, device):
        return copy(src, dst.at[m], link_send.at[kind, m], link_recv.at[kind, m], (device, mz))

    def links(m):
        z = va.at[mz, m]
        return dict(
            u=link(0, m, u_src.at[m], u_dst, me + 1),
            s=link(1, m, s_src.at[m], s_dst, me - 1),
            k=link(2, m, k_src.at[m], k_dst, me + 2),
            w=link(3, m, w_src.at[m], w_dst, me + 1),
            far=link(4, m, z, far, me - 2),
            back=link(5, m, z, above, me - 1),
            on=link(6, m, z, below, me + 1),
        )

    def to_z(array, m, kind):
        return [
            copy(array.at[mz, m], array.at[mz, m], z_send.at[kind, o - 1], z_recv.at[kind, o - 1], z_peer(o))
            for o in range(1, nz)
        ]

    def spread(array, at, send, recv, peer, count):
        return [
            copy(array.at[at], array.at[at], send.at[o - 1], recv.at[o - 1], peer(o)) for o in range(1, count)
        ]

    begun = []

    def begin(copies):
        for s in copies:
            s.start()
        begun.extend(copies)

    turn = chip == chips - 1
    ahead = chip < chips - 1
    pair_n = copy(tf, other, pair_send.at[0], pair_recv.at[0], (me - 1, mz))
    pair_s = copy(sf, other, pair_send.at[1], pair_recv.at[1], (me - 1, mz))

    @pl.when(odd & ahead)
    def _():
        pair_n.start()

    low = mul(fb.T, pf[half:cells])
    sf[half:cells] = low
    sh[half:cells], sl[half:cells] = parts(low, 2)
    high = mul(fx.T, pf[half:cells])
    corner = mul(fa.T, pf[0:half, 0:half])
    high = jnp.concatenate([high[:, 0:half] + corner, high[:, half:cells]], axis=1)
    sf[0:half] = high
    sh[0:half], sl[0:half] = parts(high, 2)

    @pl.when(last)
    def _():
        pair_s.start()

    @pl.when(me == 0)
    def _():
        below[...] = jnp.zeros(below.shape, F32)

    @pl.when(me == nr - 1)
    def _():
        above[...] = jnp.zeros(above.shape, F32)

    def values(refs, rows=slice(None)):
        return [ref[rows] for ref in refs]

    n_refs, t_refs, s_refs = (nh, nl), (th, tl), (sh, sl)
    kt_refs, k_refs = (joint.at[0], joint.at[1]), (joint.at[2], joint.at[3])

    def split_dense():
        for i in range(3):
            rows = slice(i * cells, (i + 1) * cells)
            for ref, p in zip((dh, dm, dl), parts(dense[rows], 3)):
                ref[rows] = p

    @pl.when(even & ahead)
    def _():
        pair_n.wait_recv()
        kt = mul_parts(values(t_refs), parts(other[...], 2))
        for ref, p in zip(kt_refs, parts(kt, 2)):
            ref[...] = p
        other[...] = kt

    @pl.when(even & turn)
    def _():
        pair_s.wait_recv()
        x = mul_parts(parts(other[...], 2), values(n_refs))
        e = sf[...] + mul_parts(values(t_refs), parts(x, 2))
        for ref, p in zip(s_refs, parts(e, 2)):
            ref[...] = p

    def back_product():
        for ref, p in zip(k_refs, parts(other[...].T, 2)):
            ref[...] = p

    for m in range(2):
        source = r if m == 0 else wa.at[mz, 0]
        at = links(m)
        begins = 1 if m == 0 else 0

        @pl.when(odd & ahead & (chip >= begins))
        def _():
            u_src[m] = times(source[...], values(t_refs))
            at["u"].start()

        @pl.when(last)
        def _():
            s_src[m] = times(source[...], values(s_refs))
            at["s"].start()

        if m == 0:

            @pl.when(jnp.logical_not(first) & (pos != 1))
            def _():
                split_dense()

        @pl.when(odd)
        def _():
            at["w"].wait_recv()
            c[...] = source[...] - w_dst[m]

        @pl.when(odd & (chip < begins))
        def _():
            u_src[m] = times(c[...], values(t_refs))
            at["u"].start()

        @pl.when(odd & ahead)
        def _():
            s_src[m] = times(c[...], values(s_refs))
            at["s"].start()

        if m == 0:

            @pl.when(pos == 1)
            def _():
                split_dense()

        @pl.when(odd & ahead)
        def _():
            at["back"].wait_recv()
            va[mz, m] = s_src[m] - times(above[m], values(n_refs))

        @pl.when(last)
        def _():
            va[mz, m] = times(c[...], values(s_refs))

        @pl.when(first)
        def _():
            c[...] = source[...]

        def other_half():
            at["s"].wait_recv()
            sv[...] = times(s_dst[m], values(n_refs))

        @pl.when(even & turn)
        def _():
            other_half()

        @pl.when(even & (chip > 0))
        def _():
            at["u"].wait_recv()
            c[...] = source[...] - u_dst[m]

        @pl.when(even & (chip > begins))
        def _():
            at["k"].wait_recv()
            c[...] = c[...] + k_dst[m]

        @pl.when(even & ahead & (chip >= begins))
        def _():
            k_src[m] = times(c[...], values(kt_refs))
            at["k"].start()

        @pl.when(even & ahead)
        def _():
            w_src[m] = times(c[...], values(t_refs))
            at["w"].start()

        if m == 0:

            @pl.when(even & ahead)
            def _():
                back_product()

            @pl.when(first)
            def _():
                split_dense()

        @pl.when(even & ahead)
        def _():
            other_half()
            c[...] = times(c[...], values(s_refs)) - sv[...]
            at["far"].wait_recv()
            va[mz, m] = c[...] + times(far[m], values(k_refs))

        @pl.when(even & turn)
        def _():
            va[mz, m] = times(c[...], values(s_refs)) - sv[...]

        @pl.when(even & (chip > 0))
        def _():
            at["far"].start()

        @pl.when(even & turn)
        def _():
            w_src[m] = times(c[...], values(t_refs))
            at["w"].start()

        @pl.when(has_before)
        def _():
            at["back"].start()

        @pl.when(has_next)
        def _():
            at["on"].start()

        begin(to_z(va, m, 2 * m))

        d = (dh, dm, dl)

        def part(value, i):
            return times(value, values(d, slice(i * cells, (i + 1) * cells)))

        c[...] = part(va[mz, m], 1)

        @pl.when(from_before)
        def _():
            at["on"].wait_recv()

        @pl.when(first)
        def _():
            wa[mz, m] = part(below[m], 0)

        @pl.when(jnp.logical_not(odd) )
        def _():
            at["back"].wait_recv()

        @pl.when(jnp.logical_not(last))
        def _():
            sv[...] = part(above[m], 2)

        if m == 1:
            @pl.when(first)
            def _():
                far[0] = 0.5 * c[...] + sv[...] + wa[mz, m]

            @pl.when(jnp.logical_not(first | last))
            def _():
                far[0] = 0.5 * c[...] + sv[...]

            @pl.when(last)
            def _():
                far[0] = 0.5 * c[...]

            for kind in range(2):
                for s in to_z(va, kind, 2 * kind):
                    s.wait_recv()
            left = jnp.concatenate([wa[mz, 0], far[0], r[...]], axis=0)
            right = va[...].reshape(nz * 16, cells)
            red_x[pos] = lax.dot_general(
                left, right, (((1,), (1,)), ((), ())),
                precision=lax.Precision.HIGHEST, preferred_element_type=F32,
            )
            over_x = spread(red_x, pos, x_send, x_recv, x_peer, SPAN)
            begin(over_x)

        @pl.when(to_next)
        def _():
            at["back"].wait_recv()

        @pl.when(last)
        def _():
            sv[...] = part(above[m], 2)

        @pl.when(has_before & jnp.logical_not(first))
        def _():
            at["on"].wait_recv()

        @pl.when(jnp.logical_not(first))
        def _():
            wa[mz, m] = part(below[m], 0)

        wa[mz, m] = c[...] + sv[...] + wa[mz, m]
        begin(to_z(wa, m, 2 * m + 1))

    def total(array, count):
        value = array[0]
        for i in range(1, count):
            value = value + array[i]
        return value

    for s in over_x:
        s.wait_recv()
    red_y[where] = total(red_x, SPAN)
    over_y = spread(red_y, where, y_send, y_recv, y_peer, ny)
    begin(over_y)
    for s in over_y:
        s.wait_recv()
    whole = total(red_y, ny)
    r_out[...] = whole[16:24]
    red_z[mz] = whole[0:16]
    over_z = spread(red_z, mz, k_send, k_recv, z_peer, nz)
    begin(over_z)
    for m in range(2):
        for s in to_z(wa, m, 2 * m + 1):
            s.wait_recv()
    v_out[...] = va[...].reshape(nz * 16, cells)
    w_out[...] = wa[...].reshape(nz * 16, cells)
    for s in over_z:
        s.wait_recv()
    k_out[...] = red_z[...].reshape(nz * 16, nz * 16)
    for s in begun:
        s.wait_send()

    @pl.when(odd & ahead)
    def _():
        pair_n.wait_send()

    @pl.when(last)
    def _():
        pair_s.wait_send()

    for m in range(2):
        at = links(m)
        for name, started in (
            ("u", odd & ahead),
            ("s", odd),
            ("k", even & ahead & (chip >= (1 if m == 0 else 0))),
            ("w", even),
            ("far", even & (chip > 0)),
            ("back", has_before),
            ("on", has_next),
        ):

            @pl.when(started)
            def _():
                at[name].wait_send()


def krylov(nr, nz, r, dense, pivots):
    rhs, cells = r.shape
    ny = nr // SPAN
    dma = pltpu.SemaphoreType.DMA
    every = nz * 2 * rhs
    vector = pltpu.VMEM((rhs, cells), F32)
    square, square_half = pltpu.VMEM((cells, cells), F32), pltpu.VMEM((cells, cells), BF)
    vectors = pltpu.VMEM((2, rhs, cells), F32)
    return pl.pallas_call(
        functools.partial(krylov_kernel, nr, nz),
        out_shape=[
            jax.ShapeDtypeStruct((every, cells), F32),
            jax.ShapeDtypeStruct((every, cells), F32),
            jax.ShapeDtypeStruct((every, every), F32),
            jax.ShapeDtypeStruct((rhs, every), F32),
        ],
        in_specs=[VMEM] * 3,
        out_specs=[VMEM] * 4,
        scratch_shapes=[pltpu.VMEM((3 * cells, cells), BF)] * 3
        + [square_half] * 6
        + [square] * 3
        + [pltpu.VMEM((nz, 2, rhs, cells), F32)] * 2
        + [vector] * 2
        + [square, pltpu.VMEM((4, cells, cells), BF)]
        + [vectors] * 11
        + [
            pltpu.VMEM((SPAN, 3 * rhs, every), F32),
            pltpu.VMEM((ny, 3 * rhs, every), F32),
            pltpu.VMEM((nz, 2 * rhs, every), F32),
        ]
        + [dma((7, 2))] * 2
        + [dma((2,))] * 2
        + [dma((4, max(nz - 1, 1)))] * 2
        + [dma((SPAN - 1,))] * 2
        + [dma((max(ny - 1, 1),))] * 2
        + [dma((max(nz - 1, 1),))] * 2,
        compiler_params=pltpu.CompilerParams(
            collective_id=0, has_side_effects=True, vmem_limit_bytes=44 * MIB
        ),
    )(r, dense, pivots)


def solve_kernel(k_in, rt, v, w, r, x_out, r_out):
    size = k_in.shape[0]
    k = k_in[...]
    kt = k.T
    row_of = lax.broadcasted_iota(jnp.int32, (size, 1), 0)
    col_of = lax.broadcasted_iota(jnp.int32, (1, size), 1)
    row_p, col_p = lax.rem(row_of // 8, 2) == 1, lax.rem(col_of // 8, 2) == 1
    both = k + kt
    k = jnp.where(row_p, jnp.where(col_p, both, kt), jnp.where(col_p, k, 0.5 * both))
    for i in range(0, size, 2):
        j = i + 1
        a, b, d = k[i : i + 1, i : i + 1], k[i : i + 1, j : j + 1], k[j : j + 1, j : j + 1]
        inv = 1.0 / (a * d - b * b)
        ra = jnp.where(col_of == i, 1.0, jnp.where(col_of == j, 0.0, k[i : i + 1, :]))
        rb = jnp.where(col_of == j, 1.0, jnp.where(col_of == i, 0.0, k[j : j + 1, :]))
        new_a, new_b = (d * ra - b * rb) * inv, (a * rb - b * ra) * inv
        ca = jnp.where(row_of == i, -1.0, jnp.where(row_of == j, 0.0, k[:, i : i + 1]))
        cb = jnp.where(row_of == j, -1.0, jnp.where(row_of == i, 0.0, k[:, j : j + 1]))
        gone = (row_of == i) | (row_of == j) | (col_of == i) | (col_of == j)
        k = jnp.where(gone, 0.0, k) - ca * new_a - cb * new_b
    high = lax.Precision.HIGHEST
    c = jnp.dot(rt[...], k, precision=high, preferred_element_type=F32)
    x_out[...] = jnp.dot(c, v[...], precision=high, preferred_element_type=F32)
    r_out[...] = r[...] - jnp.dot(c, w[...], precision=high, preferred_element_type=F32)


def solve(k, rt, v, w, r):
    return pl.pallas_call(
        solve_kernel,
        out_shape=[jax.ShapeDtypeStruct(r.shape, F32)] * 2,
        in_specs=[VMEM] * 5,
        out_specs=[VMEM] * 2,
        compiler_params=pltpu.CompilerParams(vmem_limit_bytes=16 * MIB),
    )(k, rt, v, w, r)


def solution(mesh):
    nr, nz = mesh.shape["rows"], mesh.shape["rhs"]

    def shards(right_side, tiles, pivots, columns):
        dense = assemble(columns, tiles)
        v, w, k, rt = krylov(nr, nz, right_side, dense, pivots)
        return tuple(solve(k, rt, v, w, right_side))

    return jax.shard_map(
        shards,
        mesh=mesh,
        in_specs=(
            P("rhs", "rows"),
            P("rows", None, None, None),
            P("rows", None, None),
            P("rows", None),
        ),
        out_specs=(P("rhs", "rows"), P("rhs", "rows")),
        check_vma=False,
    )
```

```python
import functools

import jax
import jax.numpy as jnp
from jax import lax
from jax.experimental import pallas as pl
from jax.experimental.pallas import tpu as pltpu
from jax.sharding import PartitionSpec as P

SPAN = 8
BF, F32 = jnp.bfloat16, jnp.float32
MIB = 1 << 20
VMEM = pl.BlockSpec(memory_space=pltpu.VMEM)
SMEM = pl.BlockSpec(memory_space=pltpu.SMEM)


def parts(x, n):
    out = []
    for _ in range(n):
        high = x.astype(BF)
        out.append(high)
        x = x - high.astype(F32)
    return out


def dot(a, b):
    return jnp.dot(a, b, preferred_element_type=F32)


def mul(a, b):
    (ah, al), (bh, bl) = parts(a, 2), parts(b, 2)
    return dot(ah, bh) + (dot(ah, bl) + dot(al, bh))


def times(x, weights):
    n = x.shape[0]
    count = len(weights)
    stack = jnp.concatenate([p.astype(F32) for p in parts(x, count)], axis=0)
    if count * n % 16:
        stack = jnp.concatenate([stack, jnp.zeros((16 - count * n % 16, x.shape[1]), F32)], axis=0)
    stack = stack.astype(BF)
    total = None
    for w in reversed(weights):
        y = dot(stack, w)
        for i in reversed(range(count)):
            y_i = y[i * n : (i + 1) * n]
            total = y_i if total is None else total + y_i
    return total


def mul_parts(a, b):
    (ah, al), (bh, bl) = a, b
    return dot(ah, bh) + (dot(ah, bl) + dot(al, bh))


def krylov_kernel(
    nr, nz,
    cols, tiles, r, pivots,
    v_out, w_out, k_out, r_out,
    held, dense, dh, dm, dl, nh, nl, th, tl, sh, sl, tf, sf, pf,
    va, wa, c, sv, other, joint,
    u_src, u_dst, s_src, s_dst, k_src, k_dst, w_src, w_dst, far, above, below,
    red_x, red_y, red_z,
    tile_sem, link_send, link_recv, pair_send, pair_recv,
    z_send, z_recv, x_send, x_recv, y_send, y_recv, k_send, k_recv,
):
    me, mz = lax.axis_index("rows"), lax.axis_index("rhs")
    pos, where = lax.rem(me, SPAN), lax.div(me, SPAN)
    chip, odd = lax.div(pos, 2), lax.rem(pos, 2) == 1
    even = jnp.logical_not(odd)
    chips = SPAN // 2
    ny = nr // SPAN
    first, last = pos == 0, pos == SPAN - 1
    cells = r.shape[1]

    def x_peer(o):
        return (where * SPAN + lax.rem(pos + o, SPAN), mz)

    def y_peer(o):
        return (lax.rem(where + o, ny) * SPAN + pos, mz)

    def z_peer(o):
        return (me, lax.rem(mz + o, nz))

    group, slots, bs = held.shape[0], held.shape[1], held.shape[2]
    fetch = [pltpu.make_async_copy(tiles.at[i], held.at[i], tile_sem.at[i]) for i in range(group)]
    for f in fetch:
        f.start()
    barrier = pltpu.get_barrier_semaphore()

    def hello(device):
        pl.semaphore_signal(barrier, inc=1, device_id=device, device_id_type=pl.DeviceIdType.MESH)

    for o in range(1, SPAN):
        hello(x_peer(o))
    for o in range(1, ny):
        hello(y_peer(o))
    for o in range(1, nz):
        hello(z_peer(o))
    has_before, has_next = me > 0, me < nr - 1
    from_before, to_next = first & has_before, last & has_next

    @pl.when(from_before)
    def _():
        hello((me - 1, mz))

    @pl.when(to_next)
    def _():
        hello((me + 1, mz))

    half = cells // 2

    def block(i, j):
        return (slice(i * bs, (i + 1) * bs), slice(j * bs, (j + 1) * bs))

    nothing = jnp.zeros((bs, bs), F32)
    for i in range(group):
        fetch[i].wait()
        away = [cols[i, k] - cols[i, 0] for k in range(1, slots)]
        for delta in range(-group, group + 1):
            tile = held[i, 0] if delta == 0 else None
            for k in range(1, slots):
                term = held[i, k] * (away[k - 1] == delta).astype(F32)
                tile = term if tile is None else tile + term
            j = i + delta
            if 0 <= j < group:
                dense[block(group + i, j)] = tile
            else:
                dense[block(group + j, i)] = tile.T
        for j in range(group):
            if j < i:
                dense[block(j, i)] = nothing
            if j > i:
                dense[block(2 * group + j, i)] = nothing

    def block_diagonal(first_row):
        zero = jnp.zeros((bs, bs), F32)
        count = half // bs
        return jnp.concatenate(
            [
                jnp.concatenate([pivots[first_row + i] if i == j else zero for j in range(count)], axis=1)
                for i in range(count)
            ],
            axis=0,
        )

    pa, pb = block_diagonal(0), block_diagonal(half // bs)
    row = lax.broadcasted_iota(jnp.int32, (half, half), 0)
    col = lax.broadcasted_iota(jnp.int32, (half, half), 1)
    same_pair = row // (2 * bs) == col // (2 * bs)
    eye = (row == col).astype(F32)
    lower = row // bs > col // bs

    def inverse(block):
        within = jnp.where(same_pair, block, 0.0)
        f = eye - within
        return f - mul(mul(f, block - within), f)

    o = cells
    ga = mul(jnp.where(lower, dense[o : o + half, 0:half], 0.0), pa)
    gb = mul(jnp.where(lower, dense[o + half : o + cells, half:cells], 0.0), pb)
    gx = mul(dense[o + half : o + cells, 0:half], pa)
    fa, fb = inverse(ga), inverse(gb)
    fx = -mul(mul(fb, gx), fa)
    pf[0:half, 0:half] = mul(pa, fa)
    pf[0:half, half:cells] = jnp.zeros((half, half), F32)
    pf[half:cells, 0:half] = mul(pb, fx)
    pf[half:cells, half:cells] = mul(pb, fb)
    n = mul(dense[2 * cells : 3 * cells], pf[...])
    nh[...], nl[...] = parts(n, 2)
    nt = n.T
    tf[...] = nt
    th[...], tl[...] = parts(nt, 2)

    edges = from_before.astype(jnp.int32) + to_next.astype(jnp.int32)
    pl.semaphore_wait(barrier, SPAN - 1 + ny - 1 + nz - 1 + edges)

    def copy(src, dst, send, recv, device):
        return pltpu.make_async_remote_copy(
            src_ref=src, dst_ref=dst, send_sem=send, recv_sem=recv,
            device_id=device, device_id_type=pl.DeviceIdType.MESH,
        )

    def link(kind, m, src, dst, device):
        return copy(src, dst.at[m], link_send.at[kind, m], link_recv.at[kind, m], (device, mz))

    def links(m):
        z = va.at[mz, m]
        return dict(
            u=link(0, m, u_src.at[m], u_dst, me + 1),
            s=link(1, m, s_src.at[m], s_dst, me - 1),
            k=link(2, m, k_src.at[m], k_dst, me + 2),
            w=link(3, m, w_src.at[m], w_dst, me + 1),
            far=link(4, m, z, far, me - 2),
            back=link(5, m, z, above, me - 1),
            on=link(6, m, z, below, me + 1),
        )

    def to_z(array, m, kind):
        return [
            copy(array.at[mz, m], array.at[mz, m], z_send.at[kind, o - 1], z_recv.at[kind, o - 1], z_peer(o))
            for o in range(1, nz)
        ]

    def spread(array, at, send, recv, peer, count):
        return [
            copy(array.at[at], array.at[at], send.at[o - 1], recv.at[o - 1], peer(o)) for o in range(1, count)
        ]

    begun = []

    def begin(copies):
        for s in copies:
            s.start()
        begun.extend(copies)

    def values(refs, rows=slice(None)):
        return [ref[rows] for ref in refs]

    n_refs, t_refs, s_refs = (nh, nl), (th, tl), (sh, sl)
    turn = chip == chips - 1
    ahead = chip < chips - 1
    pair_n = copy(tf, other, pair_send.at[0], pair_recv.at[0], (me - 1, mz))
    pair_s = copy(sf, other, pair_send.at[1], pair_recv.at[1], (me - 1, mz))

    @pl.when(odd & ahead)
    def _():
        pair_n.start()

    at_once = links(0)

    @pl.when(first)
    def _():
        w_src[0] = times(r[...], values(t_refs))
        at_once["w"].start()

    @pl.when(pos == 1)
    def _():
        at_once["w"].wait_recv()
        c[...] = r[...] - w_dst[0]
        u_src[0] = times(c[...], values(t_refs))
        at_once["u"].start()

    low = mul(fb.T, pf[half:cells])
    sf[half:cells] = low
    sh[half:cells], sl[half:cells] = parts(low, 2)
    high = mul(fx.T, pf[half:cells])
    corner = mul(fa.T, pf[0:half, 0:half])
    high = jnp.concatenate([high[:, 0:half] + corner, high[:, half:cells]], axis=1)
    sf[0:half] = high
    sh[0:half], sl[0:half] = parts(high, 2)

    @pl.when(last)
    def _():
        pair_s.start()

    @pl.when(me == 0)
    def _():
        below[...] = jnp.zeros(below.shape, F32)

    @pl.when(me == nr - 1)
    def _():
        above[...] = jnp.zeros(above.shape, F32)

    kt_refs, k_refs = (joint.at[0], joint.at[1]), (joint.at[2], joint.at[3])

    def split_dense():
        for i in range(3):
            rows = slice(i * cells, (i + 1) * cells)
            for ref, p in zip((dh, dm, dl), parts(dense[rows], 3)):
                ref[rows] = p

    @pl.when(even & ahead)
    def _():
        pair_n.wait_recv()
        kt = mul_parts(values(t_refs), parts(other[...], 2))
        for ref, p in zip(kt_refs, parts(kt, 2)):
            ref[...] = p
        other[...] = kt

    @pl.when(even & turn)
    def _():
        pair_s.wait_recv()
        x = mul_parts(parts(other[...], 2), values(n_refs))
        e = sf[...] + mul_parts(values(t_refs), parts(x, 2))
        for ref, p in zip(s_refs, parts(e, 2)):
            ref[...] = p

    def back_product():
        for ref, p in zip(k_refs, parts(other[...].T, 2)):
            ref[...] = p

    for m in range(2):
        source = r if m == 0 else wa.at[mz, 0]
        at = links(m)
        begins = 1 if m == 0 else 0

        @pl.when(odd & ahead & (chip >= begins))
        def _():
            u_src[m] = times(source[...], values(t_refs))
            at["u"].start()

        @pl.when(last)
        def _():
            s_src[m] = times(source[...], values(s_refs))
            at["s"].start()

        if m == 0:

            @pl.when(jnp.logical_not(first) & (pos != 1))
            def _():
                split_dense()

        @pl.when(odd & (chip >= begins))
        def _():
            at["w"].wait_recv()
            c[...] = source[...] - w_dst[m]

        @pl.when(odd & ahead)
        def _():
            s_src[m] = times(c[...], values(s_refs))
            at["s"].start()

        if m == 0:

            @pl.when(pos == 1)
            def _():
                split_dense()

        @pl.when(odd & ahead)
        def _():
            at["back"].wait_recv()
            va[mz, m] = s_src[m] - times(above[m], values(n_refs))

        @pl.when(last)
        def _():
            va[mz, m] = times(c[...], values(s_refs))

        @pl.when(first)
        def _():
            c[...] = source[...]

        def other_half():
            at["s"].wait_recv()
            sv[...] = times(s_dst[m], values(n_refs))

        @pl.when(even & turn)
        def _():
            other_half()

        @pl.when(even & (chip > 0))
        def _():
            at["u"].wait_recv()
            c[...] = source[...] - u_dst[m]

        @pl.when(even & (chip > begins))
        def _():
            at["k"].wait_recv()
            c[...] = c[...] + k_dst[m]

        @pl.when(even & ahead & (chip >= begins))
        def _():
            k_src[m] = times(c[...], values(kt_refs))
            at["k"].start()

        @pl.when(even & ahead & (chip >= begins))
        def _():
            w_src[m] = times(c[...], values(t_refs))
            at["w"].start()

        if m == 0:

            @pl.when(even & ahead)
            def _():
                back_product()

            @pl.when(first)
            def _():
                split_dense()

        @pl.when(even & ahead)
        def _():
            other_half()
            c[...] = times(c[...], values(s_refs)) - sv[...]
            at["far"].wait_recv()
            va[mz, m] = c[...] + times(far[m], values(k_refs))

        @pl.when(even & turn)
        def _():
            va[mz, m] = times(c[...], values(s_refs)) - sv[...]

        @pl.when(even & (chip > 0))
        def _():
            at["far"].start()

        @pl.when(even & turn)
        def _():
            w_src[m] = times(c[...], values(t_refs))
            at["w"].start()

        @pl.when(has_before)
        def _():
            at["back"].start()

        @pl.when(has_next)
        def _():
            at["on"].start()

        begin(to_z(va, m, 2 * m))

        d = (dh, dm, dl)

        def part(value, i):
            return times(value, values(d, slice(i * cells, (i + 1) * cells)))

        c[...] = part(va[mz, m], 1)

        @pl.when(from_before)
        def _():
            at["on"].wait_recv()

        @pl.when(first)
        def _():
            wa[mz, m] = part(below[m], 0)

        @pl.when(jnp.logical_not(odd) )
        def _():
            at["back"].wait_recv()

        @pl.when(jnp.logical_not(last))
        def _():
            sv[...] = part(above[m], 2)

        if m == 1:
            @pl.when(first)
            def _():
                far[0] = 0.5 * c[...] + sv[...] + wa[mz, m]

            @pl.when(jnp.logical_not(first | last))
            def _():
                far[0] = 0.5 * c[...] + sv[...]

            @pl.when(last)
            def _():
                far[0] = 0.5 * c[...]

            for kind in range(2):
                for s in to_z(va, kind, 2 * kind):
                    s.wait_recv()
            left = jnp.concatenate([wa[mz, 0], far[0], r[...]], axis=0)
            right = va[...].reshape(nz * 16, cells)
            red_x[pos] = lax.dot_general(
                left, right, (((1,), (1,)), ((), ())),
                precision=lax.Precision.HIGHEST, preferred_element_type=F32,
            )
            over_x = spread(red_x, pos, x_send, x_recv, x_peer, SPAN)
            begin(over_x)

        @pl.when(to_next)
        def _():
            at["back"].wait_recv()

        @pl.when(last)
        def _():
            sv[...] = part(above[m], 2)

        @pl.when(has_before & jnp.logical_not(first))
        def _():
            at["on"].wait_recv()

        @pl.when(jnp.logical_not(first))
        def _():
            wa[mz, m] = part(below[m], 0)

        wa[mz, m] = c[...] + sv[...] + wa[mz, m]
        begin(to_z(wa, m, 2 * m + 1))

    def total(array, count):
        value = array[0]
        for i in range(1, count):
            value = value + array[i]
        return value

    for s in over_x:
        s.wait_recv()
    red_y[where] = total(red_x, SPAN)
    over_y = spread(red_y, where, y_send, y_recv, y_peer, ny)
    begin(over_y)
    for s in over_y:
        s.wait_recv()
    whole = total(red_y, ny)
    r_out[...] = whole[16:24]
    red_z[mz] = whole[0:16]
    over_z = spread(red_z, mz, k_send, k_recv, z_peer, nz)
    begin(over_z)
    for m in range(2):
        for s in to_z(wa, m, 2 * m + 1):
            s.wait_recv()
    v_out[...] = va[...].reshape(nz * 16, cells)
    w_out[...] = wa[...].reshape(nz * 16, cells)
    for s in over_z:
        s.wait_recv()
    k_out[...] = red_z[...].reshape(nz * 16, nz * 16)
    for s in begun:
        s.wait_send()

    @pl.when(odd & ahead)
    def _():
        pair_n.wait_send()

    @pl.when(last)
    def _():
        pair_s.wait_send()

    for m in range(2):
        at = links(m)
        for name, started in (
            ("u", odd & ahead),
            ("s", odd),
            ("k", even & ahead & (chip >= (1 if m == 0 else 0))),
            ("w", even),
            ("far", even & (chip > 0)),
            ("back", has_before),
            ("on", has_next),
        ):

            @pl.when(started)
            def _():
                at[name].wait_send()


def krylov(nr, nz, cols, tiles, r, pivots):
    rhs, cells = r.shape
    ny = nr // SPAN
    dma = pltpu.SemaphoreType.DMA
    every = nz * 2 * rhs
    vector = pltpu.VMEM((rhs, cells), F32)
    square, square_half = pltpu.VMEM((cells, cells), F32), pltpu.VMEM((cells, cells), BF)
    vectors = pltpu.VMEM((2, rhs, cells), F32)
    return pl.pallas_call(
        functools.partial(krylov_kernel, nr, nz),
        out_shape=[
            jax.ShapeDtypeStruct((every, cells), F32),
            jax.ShapeDtypeStruct((every, cells), F32),
            jax.ShapeDtypeStruct((every, every), F32),
            jax.ShapeDtypeStruct((rhs, every), F32),
        ],
        in_specs=[SMEM, pl.BlockSpec(memory_space=pltpu.HBM), VMEM, VMEM],
        out_specs=[VMEM] * 4,
        scratch_shapes=[pltpu.VMEM(tiles.shape, F32), pltpu.VMEM((3 * cells, cells), F32)]
        + [pltpu.VMEM((3 * cells, cells), BF)] * 3
        + [square_half] * 6
        + [square] * 3
        + [pltpu.VMEM((nz, 2, rhs, cells), F32)] * 2
        + [vector] * 2
        + [square, pltpu.VMEM((4, cells, cells), BF)]
        + [vectors] * 11
        + [
            pltpu.VMEM((SPAN, 3 * rhs, every), F32),
            pltpu.VMEM((ny, 3 * rhs, every), F32),
            pltpu.VMEM((nz, 2 * rhs, every), F32),
        ]
        + [dma((tiles.shape[0],))]
        + [dma((7, 2))] * 2
        + [dma((2,))] * 2
        + [dma((4, max(nz - 1, 1)))] * 2
        + [dma((SPAN - 1,))] * 2
        + [dma((max(ny - 1, 1),))] * 2
        + [dma((max(nz - 1, 1),))] * 2,
        compiler_params=pltpu.CompilerParams(
            collective_id=0, has_side_effects=True, vmem_limit_bytes=44 * MIB
        ),
    )(cols, tiles, r, pivots)


def spd_inverse(k, block):
    size = k.shape[0]
    row_of = lax.broadcasted_iota(jnp.int32, (size, 1), 0)
    col_of = lax.broadcasted_iota(jnp.int32, (1, size), 1)
    span = range(block)
    for b in range(0, size, block):
        d = [[jnp.broadcast_to(k[b + i : b + i + 1, b + j : b + j + 1], (1, size)) for j in span] for i in span]
        for p in span:
            inv = 1.0 / d[p][p]
            row = [inv if j == p else d[p][j] * inv for j in span]
            for i in span:
                if i != p:
                    f = d[i][p]
                    d[i] = [-f * row[p] if j == p else d[i][j] - f * row[j] for j in span]
            d[p] = row
        in_cols = (col_of >= b) & (col_of < b + block)
        in_rows = (row_of >= b) & (row_of < b + block)
        base = jnp.where(in_rows | in_cols, 0.0, k)
        for i in span:
            row, corner = d[i][0] * k[b : b + 1, :], d[i][0]
            for j in range(1, block):
                row = row + d[i][j] * k[b + j : b + j + 1, :]
                corner = jnp.where(col_of == b + j, d[i][j], corner)
            row = jnp.where(in_cols, corner, row)
            col = jnp.where(in_rows, jnp.where(row_of == b + i, -1.0, 0.0), k[:, b + i : b + i + 1])
            base = base - col * row
        k = base
    return k


def solve_kernel(k_in, rt, v, w, r, x_out, r_out):
    size = k_in.shape[0]
    k = k_in[...]
    kt = k.T
    row_of = lax.broadcasted_iota(jnp.int32, (size, 1), 0)
    col_of = lax.broadcasted_iota(jnp.int32, (1, size), 1)
    row_p, col_p = lax.rem(row_of // 8, 2) == 1, lax.rem(col_of // 8, 2) == 1
    both = k + kt
    k = jnp.where(row_p, jnp.where(col_p, both, kt), jnp.where(col_p, k, 0.5 * both))
    high = lax.Precision.HIGHEST
    c = jnp.dot(rt[...], spd_inverse(k, 4), precision=high, preferred_element_type=F32)
    x_out[...] = jnp.dot(c, v[...], precision=high, preferred_element_type=F32)
    r_out[...] = r[...] - jnp.dot(c, w[...], precision=high, preferred_element_type=F32)


def solve(k, rt, v, w, r):
    return pl.pallas_call(
        solve_kernel,
        out_shape=[jax.ShapeDtypeStruct(r.shape, F32)] * 2,
        in_specs=[VMEM] * 5,
        out_specs=[VMEM] * 2,
        compiler_params=pltpu.CompilerParams(vmem_limit_bytes=16 * MIB),
    )(k, rt, v, w, r)


def solution(mesh):
    nr, nz = mesh.shape["rows"], mesh.shape["rhs"]

    def shards(right_side, tiles, pivots, columns):
        v, w, k, rt = krylov(nr, nz, columns, tiles, right_side, pivots)
        return tuple(solve(k, rt, v, w, right_side))

    return jax.shard_map(
        shards,
        mesh=mesh,
        in_specs=(
            P("rhs", "rows"),
            P("rows", None, None, None),
            P("rows", None, None),
            P("rows", None),
        ),
        out_specs=(P("rhs", "rows"), P("rhs", "rows")),
        check_vma=False,
    )
```

```python
import functools

import jax
import jax.numpy as jnp
from jax import lax
from jax.experimental import pallas as pl
from jax.experimental.pallas import tpu as pltpu
from jax.sharding import PartitionSpec as P

SPAN = 8
BF, F32 = jnp.bfloat16, jnp.float32
MIB = 1 << 20
VMEM = pl.BlockSpec(memory_space=pltpu.VMEM)
SMEM = pl.BlockSpec(memory_space=pltpu.SMEM)


def parts(x, n):
    out = []
    for _ in range(n):
        high = x.astype(BF)
        out.append(high)
        x = x - high.astype(F32)
    return out


def dot(a, b):
    return jnp.dot(a, b, preferred_element_type=F32)


def mul(a, b):
    (ah, al), (bh, bl) = parts(a, 2), parts(b, 2)
    return dot(ah, bh) + (dot(ah, bl) + dot(al, bh))


def times(x, weights):
    n = x.shape[0]
    count = len(weights)
    stack = jnp.concatenate([p.astype(F32) for p in parts(x, count)], axis=0)
    if count * n % 16:
        stack = jnp.concatenate([stack, jnp.zeros((16 - count * n % 16, x.shape[1]), F32)], axis=0)
    stack = stack.astype(BF)
    total = None
    for w in reversed(weights):
        y = dot(stack, w)
        for i in reversed(range(count)):
            y_i = y[i * n : (i + 1) * n]
            total = y_i if total is None else total + y_i
    return total


def mul_parts(a, b):
    (ah, al), (bh, bl) = a, b
    return dot(ah, bh) + (dot(ah, bl) + dot(al, bh))


def krylov_kernel(
    nr, nz,
    cols_in, tiles, r_in, pivots_in,
    v_out, w_out, k_out, r_out,
    cols, r, pivots, held, dense, dh, dm, dl, nh, nl, th, tl, sh, sl, tf, sf, pf,
    va, wa, c, sv, other, joint,
    u_src, u_dst, s_src, s_dst, k_src, k_dst, w_src, w_dst, far, above, below,
    red_x, red_y, red_z,
    tile_sem, in_sem, link_send, link_recv, pair_send, pair_recv,
    z_send, z_recv, x_send, x_recv, y_send, y_recv, k_send, k_recv,
):
    me, mz = lax.axis_index("rows"), lax.axis_index("rhs")
    pos, where = lax.rem(me, SPAN), lax.div(me, SPAN)
    chip, odd = lax.div(pos, 2), lax.rem(pos, 2) == 1
    even = jnp.logical_not(odd)
    chips = SPAN // 2
    ny = nr // SPAN
    first, last = pos == 0, pos == SPAN - 1
    cells = r.shape[1]

    def x_peer(o):
        return (where * SPAN + lax.rem(pos + o, SPAN), mz)

    def y_peer(o):
        return (lax.rem(where + o, ny) * SPAN + pos, mz)

    def z_peer(o):
        return (me, lax.rem(mz + o, nz))

    group, slots, bs = held.shape[0], held.shape[1], held.shape[2]
    fetch = [pltpu.make_async_copy(tiles.at[i], held.at[i], tile_sem.at[i]) for i in range(group)]
    whole = ((cols_in, cols), (pivots_in, pivots), (r_in, r))
    fetch += [pltpu.make_async_copy(src, dst, in_sem.at[i]) for i, (src, dst) in enumerate(whole)]
    for f in fetch[group:] + fetch[:group]:
        f.start()
    barrier = pltpu.get_barrier_semaphore()

    def hello(device):
        pl.semaphore_signal(barrier, inc=1, device_id=device, device_id_type=pl.DeviceIdType.MESH)

    for o in range(1, SPAN):
        hello(x_peer(o))
    for o in range(1, ny):
        hello(y_peer(o))
    for o in range(1, nz):
        hello(z_peer(o))
    has_before, has_next = me > 0, me < nr - 1
    from_before, to_next = first & has_before, last & has_next

    @pl.when(from_before)
    def _():
        hello((me - 1, mz))

    @pl.when(to_next)
    def _():
        hello((me + 1, mz))

    half = cells // 2

    def block(i, j):
        return (slice(i * bs, (i + 1) * bs), slice(j * bs, (j + 1) * bs))

    nothing = jnp.zeros((bs, bs), F32)
    for f in fetch[group:]:
        f.wait()
    for i in range(group):
        fetch[i].wait()
        away = [cols[i, k] - cols[i, 0] for k in range(1, slots)]
        for delta in range(-group, group + 1):
            tile = held[i, 0] if delta == 0 else None
            for k in range(1, slots):
                term = held[i, k] * (away[k - 1] == delta).astype(F32)
                tile = term if tile is None else tile + term
            j = i + delta
            if 0 <= j < group:
                dense[block(group + i, j)] = tile
            else:
                dense[block(group + j, i)] = tile.T
        for j in range(group):
            if j < i:
                dense[block(j, i)] = nothing
            if j > i:
                dense[block(2 * group + j, i)] = nothing

    def block_diagonal(first_row):
        zero = jnp.zeros((bs, bs), F32)
        count = half // bs
        return jnp.concatenate(
            [
                jnp.concatenate([pivots[first_row + i] if i == j else zero for j in range(count)], axis=1)
                for i in range(count)
            ],
            axis=0,
        )

    pa, pb = block_diagonal(0), block_diagonal(half // bs)
    row = lax.broadcasted_iota(jnp.int32, (half, half), 0)
    col = lax.broadcasted_iota(jnp.int32, (half, half), 1)
    same_pair = row // (2 * bs) == col // (2 * bs)
    eye = (row == col).astype(F32)
    lower = row // bs > col // bs

    def inverse(block):
        within = jnp.where(same_pair, block, 0.0)
        f = eye - within
        return f - mul(mul(f, block - within), f)

    o = cells
    ga = mul(jnp.where(lower, dense[o : o + half, 0:half], 0.0), pa)
    gb = mul(jnp.where(lower, dense[o + half : o + cells, half:cells], 0.0), pb)
    gx = mul(dense[o + half : o + cells, 0:half], pa)
    fa, fb = inverse(ga), inverse(gb)
    fx = -mul(mul(fb, gx), fa)
    pf[0:half, 0:half] = mul(pa, fa)
    pf[0:half, half:cells] = jnp.zeros((half, half), F32)
    pf[half:cells, 0:half] = mul(pb, fx)
    pf[half:cells, half:cells] = mul(pb, fb)
    n = mul(dense[2 * cells : 3 * cells], pf[...])
    nh[...], nl[...] = parts(n, 2)
    nt = n.T
    tf[...] = nt
    th[...], tl[...] = parts(nt, 2)

    edges = from_before.astype(jnp.int32) + to_next.astype(jnp.int32)
    pl.semaphore_wait(barrier, SPAN - 1 + ny - 1 + nz - 1 + edges)

    def copy(src, dst, send, recv, device):
        return pltpu.make_async_remote_copy(
            src_ref=src, dst_ref=dst, send_sem=send, recv_sem=recv,
            device_id=device, device_id_type=pl.DeviceIdType.MESH,
        )

    def link(kind, m, src, dst, device):
        return copy(src, dst.at[m], link_send.at[kind, m], link_recv.at[kind, m], (device, mz))

    def links(m):
        z = va.at[mz, m]
        return dict(
            u=link(0, m, u_src.at[m], u_dst, me + 1),
            s=link(1, m, s_src.at[m], s_dst, me - 1),
            k=link(2, m, k_src.at[m], k_dst, me + 2),
            w=link(3, m, w_src.at[m], w_dst, me + 1),
            far=link(4, m, z, far, me - 2),
            back=link(5, m, z, above, me - 1),
            on=link(6, m, z, below, me + 1),
        )

    def to_z(array, m, kind):
        return [
            copy(array.at[mz, m], array.at[mz, m], z_send.at[kind, o - 1], z_recv.at[kind, o - 1], z_peer(o))
            for o in range(1, nz)
        ]

    def spread(array, at, send, recv, peer, count):
        return [
            copy(array.at[at], array.at[at], send.at[o - 1], recv.at[o - 1], peer(o)) for o in range(1, count)
        ]

    begun = []

    def begin(copies):
        for s in copies:
            s.start()
        begun.extend(copies)

    def values(refs, rows=slice(None)):
        return [ref[rows] for ref in refs]

    n_refs, t_refs, s_refs = (nh, nl), (th, tl), (sh, sl)
    turn = chip == chips - 1
    ahead = chip < chips - 1
    pair_n = copy(tf, other, pair_send.at[0], pair_recv.at[0], (me - 1, mz))
    pair_s = copy(sf, other, pair_send.at[1], pair_recv.at[1], (me - 1, mz))

    @pl.when(odd & ahead)
    def _():
        pair_n.start()

    at_once = links(0)

    @pl.when(first)
    def _():
        w_src[0] = times(r[...], values(t_refs))
        at_once["w"].start()

    @pl.when(pos == 1)
    def _():
        at_once["w"].wait_recv()
        c[...] = r[...] - w_dst[0]
        u_src[0] = times(c[...], values(t_refs))
        at_once["u"].start()

    low = mul(fb.T, pf[half:cells])
    sf[half:cells] = low
    sh[half:cells], sl[half:cells] = parts(low, 2)
    high = mul(fx.T, pf[half:cells])
    corner = mul(fa.T, pf[0:half, 0:half])
    high = jnp.concatenate([high[:, 0:half] + corner, high[:, half:cells]], axis=1)
    sf[0:half] = high
    sh[0:half], sl[0:half] = parts(high, 2)

    @pl.when(last)
    def _():
        pair_s.start()

    @pl.when(me == 0)
    def _():
        below[...] = jnp.zeros(below.shape, F32)

    @pl.when(me == nr - 1)
    def _():
        above[...] = jnp.zeros(above.shape, F32)

    kt_refs, k_refs = (joint.at[0], joint.at[1]), (joint.at[2], joint.at[3])

    def split_dense():
        for i in range(3):
            rows = slice(i * cells, (i + 1) * cells)
            for ref, p in zip((dh, dm, dl), parts(dense[rows], 3)):
                ref[rows] = p

    @pl.when(even & ahead)
    def _():
        pair_n.wait_recv()
        kt = mul_parts(values(t_refs), parts(other[...], 2))
        for ref, p in zip(kt_refs, parts(kt, 2)):
            ref[...] = p
        other[...] = kt

    @pl.when(even & turn)
    def _():
        pair_s.wait_recv()
        x = mul_parts(parts(other[...], 2), values(n_refs))
        e = sf[...] + mul_parts(values(t_refs), parts(x, 2))
        for ref, p in zip(s_refs, parts(e, 2)):
            ref[...] = p

    def back_product():
        for ref, p in zip(k_refs, parts(other[...].T, 2)):
            ref[...] = p

    for m in range(2):
        source = r if m == 0 else wa.at[mz, 0]
        at = links(m)
        begins = 1 if m == 0 else 0

        @pl.when(odd & ahead & (chip >= begins))
        def _():
            u_src[m] = times(source[...], values(t_refs))
            at["u"].start()

        @pl.when(last)
        def _():
            s_src[m] = times(source[...], values(s_refs))
            at["s"].start()

        if m == 0:

            @pl.when(jnp.logical_not(first) & (pos != 1))
            def _():
                split_dense()

        @pl.when(odd & (chip >= begins))
        def _():
            at["w"].wait_recv()
            c[...] = source[...] - w_dst[m]

        @pl.when(odd & ahead)
        def _():
            s_src[m] = times(c[...], values(s_refs))
            at["s"].start()

        if m == 0:

            @pl.when(pos == 1)
            def _():
                split_dense()

        @pl.when(odd & ahead)
        def _():
            at["back"].wait_recv()
            va[mz, m] = s_src[m] - times(above[m], values(n_refs))

        @pl.when(last)
        def _():
            va[mz, m] = times(c[...], values(s_refs))

        @pl.when(first)
        def _():
            c[...] = source[...]

        def other_half():
            at["s"].wait_recv()
            sv[...] = times(s_dst[m], values(n_refs))

        @pl.when(even & turn)
        def _():
            other_half()

        @pl.when(even & (chip > 0))
        def _():
            at["u"].wait_recv()
            c[...] = source[...] - u_dst[m]

        @pl.when(even & (chip > begins))
        def _():
            at["k"].wait_recv()
            c[...] = c[...] + k_dst[m]

        @pl.when(even & ahead & (chip >= begins))
        def _():
            k_src[m] = times(c[...], values(kt_refs))
            at["k"].start()

        @pl.when(even & ahead & (chip >= begins))
        def _():
            w_src[m] = times(c[...], values(t_refs))
            at["w"].start()

        if m == 0:

            @pl.when(even & ahead)
            def _():
                back_product()

            @pl.when(first)
            def _():
                split_dense()

        @pl.when(even & ahead)
        def _():
            other_half()
            c[...] = times(c[...], values(s_refs)) - sv[...]
            at["far"].wait_recv()
            va[mz, m] = c[...] + times(far[m], values(k_refs))

        @pl.when(even & turn)
        def _():
            va[mz, m] = times(c[...], values(s_refs)) - sv[...]

        @pl.when(even & (chip > 0))
        def _():
            at["far"].start()

        @pl.when(even & turn)
        def _():
            w_src[m] = times(c[...], values(t_refs))
            at["w"].start()

        @pl.when(has_before)
        def _():
            at["back"].start()

        @pl.when(has_next)
        def _():
            at["on"].start()

        begin(to_z(va, m, 2 * m))

        d = (dh, dm, dl)

        def part(value, i):
            return times(value, values(d, slice(i * cells, (i + 1) * cells)))

        c[...] = part(va[mz, m], 1)

        @pl.when(from_before)
        def _():
            at["on"].wait_recv()

        @pl.when(first)
        def _():
            wa[mz, m] = part(below[m], 0)

        @pl.when(jnp.logical_not(odd) )
        def _():
            at["back"].wait_recv()

        @pl.when(jnp.logical_not(last))
        def _():
            sv[...] = part(above[m], 2)

        if m == 1:
            @pl.when(first)
            def _():
                far[0] = 0.5 * c[...] + sv[...] + wa[mz, m]

            @pl.when(jnp.logical_not(first | last))
            def _():
                far[0] = 0.5 * c[...] + sv[...]

            @pl.when(last)
            def _():
                far[0] = 0.5 * c[...]

            for kind in range(2):
                for s in to_z(va, kind, 2 * kind):
                    s.wait_recv()
            left = jnp.concatenate([wa[mz, 0], far[0], r[...]], axis=0)
            right = va[...].reshape(nz * 16, cells)
            red_x[pos] = lax.dot_general(
                left, right, (((1,), (1,)), ((), ())),
                precision=lax.Precision.HIGHEST, preferred_element_type=F32,
            )
            over_x = spread(red_x, pos, x_send, x_recv, x_peer, SPAN)
            begin(over_x)

        @pl.when(to_next)
        def _():
            at["back"].wait_recv()

        @pl.when(last)
        def _():
            sv[...] = part(above[m], 2)

        @pl.when(has_before & jnp.logical_not(first))
        def _():
            at["on"].wait_recv()

        @pl.when(jnp.logical_not(first))
        def _():
            wa[mz, m] = part(below[m], 0)

        wa[mz, m] = c[...] + sv[...] + wa[mz, m]
        begin(to_z(wa, m, 2 * m + 1))

    def total(array, count):
        value = array[0]
        for i in range(1, count):
            value = value + array[i]
        return value

    for s in over_x:
        s.wait_recv()
    red_y[where] = total(red_x, SPAN)
    over_y = spread(red_y, where, y_send, y_recv, y_peer, ny)
    begin(over_y)
    for s in over_y:
        s.wait_recv()
    both = total(red_y, ny)
    r_out[...] = both[16:24]
    red_z[mz] = both[0:16]
    over_z = spread(red_z, mz, k_send, k_recv, z_peer, nz)
    begin(over_z)
    for m in range(2):
        for s in to_z(wa, m, 2 * m + 1):
            s.wait_recv()
    v_out[...] = va[...].reshape(nz * 16, cells)
    w_out[...] = wa[...].reshape(nz * 16, cells)
    for s in over_z:
        s.wait_recv()
    k_out[...] = red_z[...].reshape(nz * 16, nz * 16)
    for s in begun:
        s.wait_send()

    @pl.when(odd & ahead)
    def _():
        pair_n.wait_send()

    @pl.when(last)
    def _():
        pair_s.wait_send()

    for m in range(2):
        at = links(m)
        for name, started in (
            ("u", odd & ahead),
            ("s", odd),
            ("k", even & ahead & (chip >= (1 if m == 0 else 0))),
            ("w", even),
            ("far", even & (chip > 0)),
            ("back", has_before),
            ("on", has_next),
        ):

            @pl.when(started)
            def _():
                at[name].wait_send()


def krylov(nr, nz, cols, tiles, r, pivots):
    rhs, cells = r.shape
    ny = nr // SPAN
    dma = pltpu.SemaphoreType.DMA
    every = nz * 2 * rhs
    vector = pltpu.VMEM((rhs, cells), F32)
    square, square_half = pltpu.VMEM((cells, cells), F32), pltpu.VMEM((cells, cells), BF)
    vectors = pltpu.VMEM((2, rhs, cells), F32)
    return pl.pallas_call(
        functools.partial(krylov_kernel, nr, nz),
        out_shape=[
            jax.ShapeDtypeStruct((every, cells), F32),
            jax.ShapeDtypeStruct((every, cells), F32),
            jax.ShapeDtypeStruct((every, every), F32),
            jax.ShapeDtypeStruct((rhs, every), F32),
        ],
        in_specs=[pl.BlockSpec(memory_space=pltpu.HBM)] * 4,
        out_specs=[VMEM] * 4,
        scratch_shapes=[pltpu.SMEM(cols.shape, jnp.int32), vector, pltpu.VMEM(pivots.shape, F32)]
        + [pltpu.VMEM(tiles.shape, F32), pltpu.VMEM((3 * cells, cells), F32)]
        + [pltpu.VMEM((3 * cells, cells), BF)] * 3
        + [square_half] * 6
        + [square] * 3
        + [pltpu.VMEM((nz, 2, rhs, cells), F32)] * 2
        + [vector] * 2
        + [square, pltpu.VMEM((4, cells, cells), BF)]
        + [vectors] * 11
        + [
            pltpu.VMEM((SPAN, 3 * rhs, every), F32),
            pltpu.VMEM((ny, 3 * rhs, every), F32),
            pltpu.VMEM((nz, 2 * rhs, every), F32),
        ]
        + [dma((tiles.shape[0],)), dma((3,))]
        + [dma((7, 2))] * 2
        + [dma((2,))] * 2
        + [dma((4, max(nz - 1, 1)))] * 2
        + [dma((SPAN - 1,))] * 2
        + [dma((max(ny - 1, 1),))] * 2
        + [dma((max(nz - 1, 1),))] * 2,
        compiler_params=pltpu.CompilerParams(
            collective_id=0, has_side_effects=True, vmem_limit_bytes=60 * MIB
        ),
    )(cols, tiles, r, pivots)


def spd_inverse(k, block):
    size = k.shape[0]
    row_of = lax.broadcasted_iota(jnp.int32, (size, 1), 0)
    col_of = lax.broadcasted_iota(jnp.int32, (1, size), 1)
    span = range(block)
    for b in range(0, size, block):
        d = [[jnp.broadcast_to(k[b + i : b + i + 1, b + j : b + j + 1], (1, size)) for j in span] for i in span]
        for p in span:
            inv = 1.0 / d[p][p]
            row = [inv if j == p else d[p][j] * inv for j in span]
            for i in span:
                if i != p:
                    f = d[i][p]
                    d[i] = [-f * row[p] if j == p else d[i][j] - f * row[j] for j in span]
            d[p] = row
        in_cols = (col_of >= b) & (col_of < b + block)
        in_rows = (row_of >= b) & (row_of < b + block)
        base = jnp.where(in_rows | in_cols, 0.0, k)
        for i in span:
            row, corner = d[i][0] * k[b : b + 1, :], d[i][0]
            for j in range(1, block):
                row = row + d[i][j] * k[b + j : b + j + 1, :]
                corner = jnp.where(col_of == b + j, d[i][j], corner)
            row = jnp.where(in_cols, corner, row)
            col = jnp.where(in_rows, jnp.where(row_of == b + i, -1.0, 0.0), k[:, b + i : b + i + 1])
            base = base - col * row
        k = base
    return k


def solve_kernel(k_in, rt_in, v_in, w_in, r_in, x_out, r_out, k_buf, rt, v, w, r, sems):
    whole = ((k_in, k_buf), (rt_in, rt), (v_in, v), (w_in, w), (r_in, r))
    fetch = [pltpu.make_async_copy(src, dst, sems.at[i]) for i, (src, dst) in enumerate(whole)]
    for f in fetch:
        f.start()
    fetch[0].wait()
    size = k_buf.shape[0]
    k = k_buf[...]
    kt = k.T
    row_of = lax.broadcasted_iota(jnp.int32, (size, 1), 0)
    col_of = lax.broadcasted_iota(jnp.int32, (1, size), 1)
    row_p, col_p = lax.rem(row_of // 8, 2) == 1, lax.rem(col_of // 8, 2) == 1
    both = k + kt
    k = jnp.where(row_p, jnp.where(col_p, both, kt), jnp.where(col_p, k, 0.5 * both))
    high = lax.Precision.HIGHEST
    inverse = spd_inverse(k, 4)
    for f in fetch[1:]:
        f.wait()
    c = jnp.dot(rt[...], inverse, precision=high, preferred_element_type=F32)
    x_out[...] = jnp.dot(c, v[...], precision=high, preferred_element_type=F32)
    r_out[...] = r[...] - jnp.dot(c, w[...], precision=high, preferred_element_type=F32)


def solve(k, rt, v, w, r):
    operands = (k, rt, v, w, r)
    return pl.pallas_call(
        solve_kernel,
        out_shape=[jax.ShapeDtypeStruct(r.shape, F32)] * 2,
        in_specs=[pl.BlockSpec(memory_space=pltpu.HBM)] * 5,
        out_specs=[VMEM] * 2,
        scratch_shapes=[pltpu.VMEM(o.shape, F32) for o in operands] + [pltpu.SemaphoreType.DMA((5,))],
        compiler_params=pltpu.CompilerParams(vmem_limit_bytes=60 * MIB),
    )(*operands)


def solution(mesh):
    nr, nz = mesh.shape["rows"], mesh.shape["rhs"]

    def shards(right_side, tiles, pivots, columns):
        v, w, k, rt = krylov(nr, nz, columns, tiles, right_side, pivots)
        return tuple(solve(k, rt, v, w, right_side))

    return jax.shard_map(
        shards,
        mesh=mesh,
        in_specs=(
            P("rhs", "rows"),
            P("rows", None, None, None),
            P("rows", None, None),
            P("rows", None),
        ),
        out_specs=(P("rhs", "rows"), P("rhs", "rows")),
        check_vma=False,
    )
```

```python
import functools

import jax
import jax.numpy as jnp
from jax import lax
from jax.experimental import pallas as pl
from jax.experimental.pallas import tpu as pltpu
from jax.sharding import PartitionSpec as P

SPAN = 8
BF, F32 = jnp.bfloat16, jnp.float32
MIB = 1 << 20
VMEM = pl.BlockSpec(memory_space=pltpu.VMEM)
SMEM = pl.BlockSpec(memory_space=pltpu.SMEM)


def parts(x, n):
    out = []
    for _ in range(n):
        high = x.astype(BF)
        out.append(high)
        x = x - high.astype(F32)
    return out


def dot(a, b):
    return jnp.dot(a, b, preferred_element_type=F32)


def mul(a, b):
    (ah, al), (bh, bl) = parts(a, 2), parts(b, 2)
    return dot(ah, bh) + (dot(ah, bl) + dot(al, bh))


def times(x, weights):
    n = x.shape[0]
    count = len(weights)
    stack = jnp.concatenate([p.astype(F32) for p in parts(x, count)], axis=0)
    if count * n % 16:
        stack = jnp.concatenate([stack, jnp.zeros((16 - count * n % 16, x.shape[1]), F32)], axis=0)
    stack = stack.astype(BF)
    total = None
    for w in reversed(weights):
        y = dot(stack, w)
        for i in reversed(range(count)):
            y_i = y[i * n : (i + 1) * n]
            total = y_i if total is None else total + y_i
    return total


def mul_parts(a, b):
    (ah, al), (bh, bl) = a, b
    return dot(ah, bh) + (dot(ah, bl) + dot(al, bh))


def krylov_kernel(
    nr, nz,
    cols_in, tiles, r_in, pivots_in,
    v_out, w_out, k_out, r_out,
    cols, r, pivots, held, dense, dh, dm, dl, nh, nl, th, tl, sh, sl, tf, sf, pf,
    va, wa, c, sv, other, third, joint,
    u_src, u_dst, s_src, s_dst, k_src, k_dst, w_src, w_dst, far, above, below,
    g_src, g_dst, h_dst, e_src, e_dst,
    red_x, red_y, red_z,
    tile_sem, in_sem, link_send, link_recv, pair_send, pair_recv,
    z_send, z_recv, x_send, x_recv, y_send, y_recv, k_send, k_recv,
):
    me, mz = lax.axis_index("rows"), lax.axis_index("rhs")
    pos, where = lax.rem(me, SPAN), lax.div(me, SPAN)
    chip, odd = lax.div(pos, 2), lax.rem(pos, 2) == 1
    even = jnp.logical_not(odd)
    chips = SPAN // 2
    ny = nr // SPAN
    first, last = pos == 0, pos == SPAN - 1
    cells = r.shape[1]

    def x_peer(o):
        return (where * SPAN + lax.rem(pos + o, SPAN), mz)

    def y_peer(o):
        return (lax.rem(where + o, ny) * SPAN + pos, mz)

    def z_peer(o):
        return (me, lax.rem(mz + o, nz))

    group, slots, bs = held.shape[0], held.shape[1], held.shape[2]
    fetch = [pltpu.make_async_copy(tiles.at[i], held.at[i], tile_sem.at[i]) for i in range(group)]
    whole = ((cols_in, cols), (pivots_in, pivots), (r_in, r))
    fetch += [pltpu.make_async_copy(src, dst, in_sem.at[i]) for i, (src, dst) in enumerate(whole)]
    for f in fetch[group:] + fetch[:group]:
        f.start()
    barrier = pltpu.get_barrier_semaphore()

    def hello(device):
        pl.semaphore_signal(barrier, inc=1, device_id=device, device_id_type=pl.DeviceIdType.MESH)

    for o in range(1, SPAN):
        hello(x_peer(o))
    for o in range(1, ny):
        hello(y_peer(o))
    for o in range(1, nz):
        hello(z_peer(o))
    has_before, has_next = me > 0, me < nr - 1
    from_before, to_next = first & has_before, last & has_next

    @pl.when(from_before)
    def _():
        hello((me - 1, mz))

    @pl.when(to_next)
    def _():
        hello((me + 1, mz))

    half = cells // 2

    def block(i, j):
        return (slice(i * bs, (i + 1) * bs), slice(j * bs, (j + 1) * bs))

    nothing = jnp.zeros((bs, bs), F32)
    for f in fetch[group:]:
        f.wait()
    for i in range(group):
        fetch[i].wait()
        away = [cols[i, k] - cols[i, 0] for k in range(1, slots)]
        for delta in range(-group, group + 1):
            tile = held[i, 0] if delta == 0 else None
            for k in range(1, slots):
                term = held[i, k] * (away[k - 1] == delta).astype(F32)
                tile = term if tile is None else tile + term
            j = i + delta
            if 0 <= j < group:
                dense[block(group + i, j)] = tile
            else:
                dense[block(group + j, i)] = tile.T
        for j in range(group):
            if j < i:
                dense[block(j, i)] = nothing
            if j > i:
                dense[block(2 * group + j, i)] = nothing

    def block_diagonal(first_row):
        zero = jnp.zeros((bs, bs), F32)
        count = half // bs
        return jnp.concatenate(
            [
                jnp.concatenate([pivots[first_row + i] if i == j else zero for j in range(count)], axis=1)
                for i in range(count)
            ],
            axis=0,
        )

    pa, pb = block_diagonal(0), block_diagonal(half // bs)
    row = lax.broadcasted_iota(jnp.int32, (half, half), 0)
    col = lax.broadcasted_iota(jnp.int32, (half, half), 1)
    same_pair = row // (2 * bs) == col // (2 * bs)
    eye = (row == col).astype(F32)
    lower = row // bs > col // bs

    def inverse(block):
        within = jnp.where(same_pair, block, 0.0)
        f = eye - within
        return f - mul(mul(f, block - within), f)

    o = cells
    ga = mul(jnp.where(lower, dense[o : o + half, 0:half], 0.0), pa)
    gb = mul(jnp.where(lower, dense[o + half : o + cells, half:cells], 0.0), pb)
    gx = mul(dense[o + half : o + cells, 0:half], pa)
    fa, fb = inverse(ga), inverse(gb)
    fx = -mul(mul(fb, gx), fa)
    pf[0:half, 0:half] = mul(pa, fa)
    pf[0:half, half:cells] = jnp.zeros((half, half), F32)
    pf[half:cells, 0:half] = mul(pb, fx)
    pf[half:cells, half:cells] = mul(pb, fb)
    n = mul(dense[2 * cells : 3 * cells], pf[...])
    nh[...], nl[...] = parts(n, 2)
    nt = n.T
    tf[...] = nt
    th[...], tl[...] = parts(nt, 2)

    edges = from_before.astype(jnp.int32) + to_next.astype(jnp.int32)
    pl.semaphore_wait(barrier, SPAN - 1 + ny - 1 + nz - 1 + edges)

    def copy(src, dst, send, recv, device):
        return pltpu.make_async_remote_copy(
            src_ref=src, dst_ref=dst, send_sem=send, recv_sem=recv,
            device_id=device, device_id_type=pl.DeviceIdType.MESH,
        )

    def link(kind, m, src, dst, device):
        return copy(src, dst.at[m], link_send.at[kind, m], link_recv.at[kind, m], (device, mz))

    def links(m):
        z = va.at[mz, m]
        return dict(
            u=link(0, m, u_src.at[m], u_dst, me + 1),
            s=link(1, m, s_src.at[m], s_dst, me - 1),
            k=link(2, m, k_src.at[m], k_dst, me + 2),
            w=link(3, m, w_src.at[m], w_dst, me + 1),
            far=link(4, m, z, far, me - 2),
            back=link(5, m, z, above, me - 1),
            on=link(6, m, z, below, me + 1),
            g=link(7, m, g_src.at[m], g_dst, me + 4),
            h=link(8, m, z, h_dst, me - 4),
            e=link(9, m, e_src.at[m], e_dst, me - 2),
        )

    def to_z(array, m, kind):
        return [
            copy(array.at[mz, m], array.at[mz, m], z_send.at[kind, o - 1], z_recv.at[kind, o - 1], z_peer(o))
            for o in range(1, nz)
        ]

    def spread(array, at, send, recv, peer, count):
        return [
            copy(array.at[at], array.at[at], send.at[o - 1], recv.at[o - 1], peer(o)) for o in range(1, count)
        ]

    begun = []

    def begin(copies):
        for s in copies:
            s.start()
        begun.extend(copies)

    def values(refs, rows=slice(None)):
        return [ref[rows] for ref in refs]

    n_refs, t_refs, s_refs = (nh, nl), (th, tl), (sh, sl)
    turn = chip == chips - 1
    ahead = chip < chips - 1
    pair_n = copy(tf, other, pair_send.at[0], pair_recv.at[0], (me - 1, mz))
    pair_s = copy(sf, other, pair_send.at[1], pair_recv.at[1], (me - 1, mz))

    @pl.when(odd & ahead)
    def _():
        pair_n.start()

    pair_k = copy(other, third, pair_send.at[2], pair_recv.at[2], (me - 2, mz))
    at_once = links(0)

    @pl.when(first)
    def _():
        w_src[0] = times(r[...], values(t_refs))
        at_once["w"].start()

    @pl.when(pos == 1)
    def _():
        at_once["w"].wait_recv()
        c[...] = r[...] - w_dst[0]
        u_src[0] = times(c[...], values(t_refs))
        at_once["u"].start()

    def middle():
        low = mul(fb.T, pf[half:cells])
        sf[half:cells] = low
        sh[half:cells], sl[half:cells] = parts(low, 2)
        high = mul(fx.T, pf[half:cells])
        corner = mul(fa.T, pf[0:half, 0:half])
        high = jnp.concatenate([high[:, 0:half] + corner, high[:, half:cells]], axis=1)
        sf[0:half] = high
        sh[0:half], sl[0:half] = parts(high, 2)

    kt_refs, k_refs = (joint.at[0], joint.at[1]), (joint.at[2], joint.at[3])
    two_t, two = (joint.at[4], joint.at[5]), (joint.at[6], joint.at[7])

    @pl.when(even & ahead)
    def _():
        pair_n.wait_recv()
        kt = mul_parts(values(t_refs), parts(other[...], 2))
        for ref, p in zip(kt_refs, parts(kt, 2)):
            ref[...] = p
        other[...] = kt

    @pl.when(pos == 4)
    def _():
        pair_k.start()

    @pl.when(pos != 2)
    def _():
        middle()

    @pl.when(last)
    def _():
        pair_s.start()

    @pl.when(me == 0)
    def _():
        below[...] = jnp.zeros(below.shape, F32)

    @pl.when(me == nr - 1)
    def _():
        above[...] = jnp.zeros(above.shape, F32)


    def split_dense():
        for i in range(3):
            rows = slice(i * cells, (i + 1) * cells)
            for ref, p in zip((dh, dm, dl), parts(dense[rows], 3)):
                ref[rows] = p

    @pl.when(even & turn)
    def _():
        pair_s.wait_recv()
        x = mul_parts(parts(other[...], 2), values(n_refs))
        e = sf[...] + mul_parts(values(t_refs), parts(x, 2))
        for ref, p in zip(s_refs, parts(e, 2)):
            ref[...] = p

    def back_product():
        for ref, p in zip(k_refs, parts(other[...].T, 2)):
            ref[...] = p

    for m in range(2):
        source = r if m == 0 else wa.at[mz, 0]
        at = links(m)
        begins = 1 if m == 0 else 0

        @pl.when(odd & ahead & (chip >= begins))
        def _():
            u_src[m] = times(source[...], values(t_refs))
            at["u"].start()

        @pl.when(last)
        def _():
            s_src[m] = times(source[...], values(s_refs))
            at["s"].start()

        if m == 0:

            @pl.when((pos > 2))
            def _():
                split_dense()

        @pl.when(odd & (chip >= begins))
        def _():
            at["w"].wait_recv()
            c[...] = source[...] - w_dst[m]

        @pl.when(odd & ahead)
        def _():
            s_src[m] = times(c[...], values(s_refs))
            at["s"].start()

        if m == 0:

            @pl.when(pos == 1)
            def _():
                split_dense()

        @pl.when(odd & ahead)
        def _():
            at["back"].wait_recv()
            va[mz, m] = s_src[m] - times(above[m], values(n_refs))

        @pl.when(last)
        def _():
            va[mz, m] = times(c[...], values(s_refs))

        @pl.when(first)
        def _():
            c[...] = source[...]

        def other_half():
            at["s"].wait_recv()
            sv[...] = times(s_dst[m], values(n_refs))

        @pl.when(even & turn)
        def _():
            other_half()

        @pl.when(even & (chip > 0))
        def _():
            at["u"].wait_recv()
            c[...] = source[...] - u_dst[m]

        direct = m == 1
        if direct:

            @pl.when(pos == 4)
            def _():
                k_src[m] = times(c[...], values(kt_refs))
                at["k"].start()

        @pl.when(even & (chip > begins))
        def _():
            at["k"].wait_recv()
            c[...] = c[...] + k_dst[m]

        if direct:

            @pl.when(pos == 6)
            def _():
                at["g"].wait_recv()
                c[...] = c[...] + g_dst[m]

            @pl.when(pos == 2)
            def _():
                g_src[m] = times(c[...], values(two_t))
                at["g"].start()

        @pl.when(even & ahead & (chip >= begins) & ((pos != 4) if direct else (pos >= 0)))
        def _():
            k_src[m] = times(c[...], values(kt_refs))
            at["k"].start()

        @pl.when(even & ahead & (chip >= begins))
        def _():
            w_src[m] = times(c[...], values(t_refs))
            at["w"].start()

        if m == 0:

            @pl.when(pos == 2)
            def _():
                middle()

            @pl.when(even & ahead)
            def _():
                back_product()

            @pl.when(even & (pos <= 2))
            def _():
                split_dense()

        @pl.when(even & ahead)
        def _():
            other_half()
            c[...] = times(c[...], values(s_refs)) - sv[...]

        if direct:

            @pl.when(pos == 4)
            def _():
                e_src[m] = c[...]
                at["e"].start()

            @pl.when(pos == 2)
            def _():
                at["e"].wait_recv()
                c[...] = c[...] + times(e_dst[m], values(k_refs))
                at["h"].wait_recv()
                va[mz, m] = c[...] + times(h_dst[m], values(two))

        @pl.when(even & ahead & ((pos != 2) if direct else (pos >= 0)))
        def _():
            at["far"].wait_recv()
            va[mz, m] = c[...] + times(far[m], values(k_refs))

        @pl.when(even & turn)
        def _():
            va[mz, m] = times(c[...], values(s_refs)) - sv[...]

        if direct:

            @pl.when(pos == 6)
            def _():
                at["h"].start()

        @pl.when(even & (chip > 0) & ((pos != 4) if direct else (pos >= 0)))
        def _():
            at["far"].start()

        @pl.when(even & turn)
        def _():
            w_src[m] = times(c[...], values(t_refs))
            at["w"].start()

        @pl.when(has_before)
        def _():
            at["back"].start()

        @pl.when(has_next)
        def _():
            at["on"].start()

        begin(to_z(va, m, 2 * m))

        if m == 0:

            @pl.when(pos == 2)
            def _():
                pair_k.wait_recv()
                t = mul_parts(values(kt_refs), parts(third[...], 2))
                for ref, p in zip(two_t, parts(t, 2)):
                    ref[...] = p
                for ref, p in zip(two, parts(t.T, 2)):
                    ref[...] = p

        d = (dh, dm, dl)

        def part(value, i):
            return times(value, values(d, slice(i * cells, (i + 1) * cells)))

        c[...] = part(va[mz, m], 1)

        @pl.when(from_before)
        def _():
            at["on"].wait_recv()

        @pl.when(first)
        def _():
            wa[mz, m] = part(below[m], 0)

        @pl.when(jnp.logical_not(odd) )
        def _():
            at["back"].wait_recv()

        @pl.when(jnp.logical_not(last))
        def _():
            sv[...] = part(above[m], 2)

        if m == 1:
            @pl.when(first)
            def _():
                far[0] = 0.5 * c[...] + sv[...] + wa[mz, m]

            @pl.when(jnp.logical_not(first | last))
            def _():
                far[0] = 0.5 * c[...] + sv[...]

            @pl.when(last)
            def _():
                far[0] = 0.5 * c[...]

            for kind in range(2):
                for s in to_z(va, kind, 2 * kind):
                    s.wait_recv()
            left = jnp.concatenate([wa[mz, 0], far[0], r[...]], axis=0)
            right = va[...].reshape(nz * 16, cells)
            red_x[pos] = lax.dot_general(
                left, right, (((1,), (1,)), ((), ())),
                precision=lax.Precision.HIGHEST, preferred_element_type=F32,
            )
            over_x = spread(red_x, pos, x_send, x_recv, x_peer, SPAN)
            begin(over_x)

        @pl.when(to_next)
        def _():
            at["back"].wait_recv()

        @pl.when(last)
        def _():
            sv[...] = part(above[m], 2)

        @pl.when(has_before & jnp.logical_not(first))
        def _():
            at["on"].wait_recv()

        @pl.when(jnp.logical_not(first))
        def _():
            wa[mz, m] = part(below[m], 0)

        wa[mz, m] = c[...] + sv[...] + wa[mz, m]
        begin(to_z(wa, m, 2 * m + 1))

    def total(array, count):
        value = array[0]
        for i in range(1, count):
            value = value + array[i]
        return value

    for s in over_x:
        s.wait_recv()
    red_y[where] = total(red_x, SPAN)
    over_y = spread(red_y, where, y_send, y_recv, y_peer, ny)
    begin(over_y)
    for s in over_y:
        s.wait_recv()
    both = total(red_y, ny)
    r_out[...] = both[16:24]
    red_z[mz] = both[0:16]
    over_z = spread(red_z, mz, k_send, k_recv, z_peer, nz)
    begin(over_z)
    for m in range(2):
        for s in to_z(wa, m, 2 * m + 1):
            s.wait_recv()
    v_out[...] = va[...].reshape(nz * 16, cells)
    w_out[...] = wa[...].reshape(nz * 16, cells)
    for s in over_z:
        s.wait_recv()
    k_out[...] = red_z[...].reshape(nz * 16, nz * 16)
    for s in begun:
        s.wait_send()

    @pl.when(odd & ahead)
    def _():
        pair_n.wait_send()

    @pl.when(last)
    def _():
        pair_s.wait_send()

    @pl.when(pos == 4)
    def _():
        pair_k.wait_send()

    for m in range(2):
        at = links(m)
        for name, started in (
            ("u", odd & ahead),
            ("s", odd),
            ("k", even & ahead & (chip >= (1 if m == 0 else 0))),
            ("w", even),
            ("far", even & (chip > 0) & ((pos != 4) if m == 1 else (pos >= 0))),
            ("g", (pos == 2) & (m == 1)),
            ("h", (pos == 6) & (m == 1)),
            ("e", (pos == 4) & (m == 1)),
            ("back", has_before),
            ("on", has_next),
        ):

            @pl.when(started)
            def _():
                at[name].wait_send()


def krylov(nr, nz, cols, tiles, r, pivots):
    rhs, cells = r.shape
    ny = nr // SPAN
    dma = pltpu.SemaphoreType.DMA
    every = nz * 2 * rhs
    vector = pltpu.VMEM((rhs, cells), F32)
    square, square_half = pltpu.VMEM((cells, cells), F32), pltpu.VMEM((cells, cells), BF)
    vectors = pltpu.VMEM((2, rhs, cells), F32)
    return pl.pallas_call(
        functools.partial(krylov_kernel, nr, nz),
        out_shape=[
            jax.ShapeDtypeStruct((every, cells), F32),
            jax.ShapeDtypeStruct((every, cells), F32),
            jax.ShapeDtypeStruct((every, every), F32),
            jax.ShapeDtypeStruct((rhs, every), F32),
        ],
        in_specs=[pl.BlockSpec(memory_space=pltpu.HBM)] * 4,
        out_specs=[VMEM] * 4,
        scratch_shapes=[pltpu.SMEM(cols.shape, jnp.int32), vector, pltpu.VMEM(pivots.shape, F32)]
        + [pltpu.VMEM(tiles.shape, F32), pltpu.VMEM((3 * cells, cells), F32)]
        + [pltpu.VMEM((3 * cells, cells), BF)] * 3
        + [square_half] * 6
        + [square] * 3
        + [pltpu.VMEM((nz, 2, rhs, cells), F32)] * 2
        + [vector] * 2
        + [square, square, pltpu.VMEM((8, cells, cells), BF)]
        + [vectors] * 16
        + [
            pltpu.VMEM((SPAN, 3 * rhs, every), F32),
            pltpu.VMEM((ny, 3 * rhs, every), F32),
            pltpu.VMEM((nz, 2 * rhs, every), F32),
        ]
        + [dma((tiles.shape[0],)), dma((3,))]
        + [dma((10, 2))] * 2
        + [dma((3,))] * 2
        + [dma((4, max(nz - 1, 1)))] * 2
        + [dma((SPAN - 1,))] * 2
        + [dma((max(ny - 1, 1),))] * 2
        + [dma((max(nz - 1, 1),))] * 2,
        compiler_params=pltpu.CompilerParams(
            collective_id=0, has_side_effects=True, vmem_limit_bytes=60 * MIB
        ),
    )(cols, tiles, r, pivots)


def spd_inverse(k, block):
    size = k.shape[0]
    row_of = lax.broadcasted_iota(jnp.int32, (size, 1), 0)
    col_of = lax.broadcasted_iota(jnp.int32, (1, size), 1)
    span = range(block)
    for b in range(0, size, block):
        d = [[jnp.broadcast_to(k[b + i : b + i + 1, b + j : b + j + 1], (1, size)) for j in span] for i in span]
        for p in span:
            inv = 1.0 / d[p][p]
            row = [inv if j == p else d[p][j] * inv for j in span]
            for i in span:
                if i != p:
                    f = d[i][p]
                    d[i] = [-f * row[p] if j == p else d[i][j] - f * row[j] for j in span]
            d[p] = row
        in_cols = (col_of >= b) & (col_of < b + block)
        in_rows = (row_of >= b) & (row_of < b + block)
        base = jnp.where(in_rows | in_cols, 0.0, k)
        for i in span:
            row, corner = d[i][0] * k[b : b + 1, :], d[i][0]
            for j in range(1, block):
                row = row + d[i][j] * k[b + j : b + j + 1, :]
                corner = jnp.where(col_of == b + j, d[i][j], corner)
            row = jnp.where(in_cols, corner, row)
            col = jnp.where(in_rows, jnp.where(row_of == b + i, -1.0, 0.0), k[:, b + i : b + i + 1])
            base = base - col * row
        k = base
    return k


def solve_kernel(k_in, rt_in, v_in, w_in, r_in, x_out, r_out, k_buf, rt, v, w, r, sems):
    whole = ((k_in, k_buf), (rt_in, rt), (v_in, v), (w_in, w), (r_in, r))
    fetch = [pltpu.make_async_copy(src, dst, sems.at[i]) for i, (src, dst) in enumerate(whole)]
    for f in fetch:
        f.start()
    fetch[0].wait()
    size = k_buf.shape[0]
    k = k_buf[...]
    kt = k.T
    row_of = lax.broadcasted_iota(jnp.int32, (size, 1), 0)
    col_of = lax.broadcasted_iota(jnp.int32, (1, size), 1)
    row_p, col_p = lax.rem(row_of // 8, 2) == 1, lax.rem(col_of // 8, 2) == 1
    both = k + kt
    k = jnp.where(row_p, jnp.where(col_p, both, kt), jnp.where(col_p, k, 0.5 * both))
    high = lax.Precision.HIGHEST
    inverse = spd_inverse(k, 4)
    for f in fetch[1:]:
        f.wait()
    c = jnp.dot(rt[...], inverse, precision=high, preferred_element_type=F32)
    x_out[...] = jnp.dot(c, v[...], precision=high, preferred_element_type=F32)
    r_out[...] = r[...] - jnp.dot(c, w[...], precision=high, preferred_element_type=F32)


def solve(k, rt, v, w, r):
    operands = (k, rt, v, w, r)
    return pl.pallas_call(
        solve_kernel,
        out_shape=[jax.ShapeDtypeStruct(r.shape, F32)] * 2,
        in_specs=[pl.BlockSpec(memory_space=pltpu.HBM)] * 5,
        out_specs=[VMEM] * 2,
        scratch_shapes=[pltpu.VMEM(o.shape, F32) for o in operands] + [pltpu.SemaphoreType.DMA((5,))],
        compiler_params=pltpu.CompilerParams(vmem_limit_bytes=60 * MIB),
    )(*operands)


def solution(mesh):
    nr, nz = mesh.shape["rows"], mesh.shape["rhs"]

    def shards(right_side, tiles, pivots, columns):
        v, w, k, rt = krylov(nr, nz, columns, tiles, right_side, pivots)
        return tuple(solve(k, rt, v, w, right_side))

    return jax.shard_map(
        shards,
        mesh=mesh,
        in_specs=(
            P("rhs", "rows"),
            P("rows", None, None, None),
            P("rows", None, None),
            P("rows", None),
        ),
        out_specs=(P("rhs", "rows"), P("rhs", "rows")),
        check_vma=False,
    )
```

```python
import functools

import jax
import jax.numpy as jnp
from jax import lax
from jax.experimental import pallas as pl
from jax.experimental.pallas import tpu as pltpu
from jax.sharding import PartitionSpec as P

SPAN = 8
BF, F32 = jnp.bfloat16, jnp.float32
MIB = 1 << 20
VMEM = pl.BlockSpec(memory_space=pltpu.VMEM)
SMEM = pl.BlockSpec(memory_space=pltpu.SMEM)


def parts(x, n):
    out = []
    for _ in range(n):
        high = x.astype(BF)
        out.append(high)
        x = x - high.astype(F32)
    return out


def dot(a, b):
    return jnp.dot(a, b, preferred_element_type=F32)


def mul(a, b):
    (ah, al), (bh, bl) = parts(a, 2), parts(b, 2)
    return dot(ah, bh) + (dot(ah, bl) + dot(al, bh))


def times(x, weights):
    n = x.shape[0]
    count = len(weights)
    stack = jnp.concatenate([p.astype(F32) for p in parts(x, count)], axis=0)
    if count * n % 16:
        stack = jnp.concatenate([stack, jnp.zeros((16 - count * n % 16, x.shape[1]), F32)], axis=0)
    stack = stack.astype(BF)
    total = None
    for w in reversed(weights):
        y = dot(stack, w)
        for i in reversed(range(count)):
            y_i = y[i * n : (i + 1) * n]
            total = y_i if total is None else total + y_i
    return total


def mul_parts(a, b):
    (ah, al), (bh, bl) = a, b
    return dot(ah, bh) + (dot(ah, bl) + dot(al, bh))


def krylov_kernel(
    nr, nz,
    cols_in, tiles, r_in, pivots_in,
    v_out, w_out, k_out, r_out,
    cols, r, pivots, held, dense, dh, dm, dl, nh, nl, th, tl, sh, sl, tf, sf, pf,
    va, wa, c, sv, other, third, joint,
    u_src, u_dst, s_src, s_dst, k_src, k_dst, w_src, w_dst, far, above, below,
    g_src, g_dst, h_dst, e_src, e_dst,
    red_x, red_y, red_z,
    tile_sem, in_sem, link_send, link_recv, pair_send, pair_recv,
    z_send, z_recv, x_send, x_recv, y_send, y_recv, k_send, k_recv,
):
    me, mz = lax.axis_index("rows"), lax.axis_index("rhs")
    pos, where = lax.rem(me, SPAN), lax.div(me, SPAN)
    chip, odd = lax.div(pos, 2), lax.rem(pos, 2) == 1
    even = jnp.logical_not(odd)
    chips = SPAN // 2
    ny = nr // SPAN
    first, last = pos == 0, pos == SPAN - 1
    cells = r.shape[1]

    def x_peer(o):
        return (where * SPAN + lax.rem(pos + o, SPAN), mz)

    def y_peer(o):
        return (lax.rem(where + o, ny) * SPAN + pos, mz)

    def z_peer(o):
        return (me, lax.rem(mz + o, nz))

    group, slots, bs = held.shape[0], held.shape[1], held.shape[2]
    fetch = [pltpu.make_async_copy(tiles.at[i], held.at[i], tile_sem.at[i]) for i in range(group)]
    whole = ((cols_in, cols), (pivots_in, pivots), (r_in, r))
    fetch += [pltpu.make_async_copy(src, dst, in_sem.at[i]) for i, (src, dst) in enumerate(whole)]
    for f in fetch[group:] + fetch[:group]:
        f.start()
    barrier = pltpu.get_barrier_semaphore()

    def hello(device):
        pl.semaphore_signal(barrier, inc=1, device_id=device, device_id_type=pl.DeviceIdType.MESH)

    for o in range(1, SPAN):
        hello(x_peer(o))
    for o in range(1, ny):
        hello(y_peer(o))
    for o in range(1, nz):
        hello(z_peer(o))
    has_before, has_next = me > 0, me < nr - 1
    from_before, to_next = first & has_before, last & has_next

    @pl.when(from_before)
    def _():
        hello((me - 1, mz))

    @pl.when(to_next)
    def _():
        hello((me + 1, mz))

    half = cells // 2

    def block(i, j):
        return (slice(i * bs, (i + 1) * bs), slice(j * bs, (j + 1) * bs))

    nothing = jnp.zeros((bs, bs), F32)
    for f in fetch[group:]:
        f.wait()
    for i in range(group):
        fetch[i].wait()
        away = [cols[i, k] - cols[i, 0] for k in range(1, slots)]
        for delta in range(-group, group + 1):
            tile = held[i, 0] if delta == 0 else None
            for k in range(1, slots):
                term = held[i, k] * (away[k - 1] == delta).astype(F32)
                tile = term if tile is None else tile + term
            j = i + delta
            if 0 <= j < group:
                dense[block(group + i, j)] = tile
            else:
                dense[block(group + j, i)] = tile.T
        for j in range(group):
            if j < i:
                dense[block(j, i)] = nothing
            if j > i:
                dense[block(2 * group + j, i)] = nothing

    def block_diagonal(first_row):
        zero = jnp.zeros((bs, bs), F32)
        count = half // bs
        return jnp.concatenate(
            [
                jnp.concatenate([pivots[first_row + i] if i == j else zero for j in range(count)], axis=1)
                for i in range(count)
            ],
            axis=0,
        )

    pa, pb = block_diagonal(0), block_diagonal(half // bs)
    row = lax.broadcasted_iota(jnp.int32, (half, half), 0)
    col = lax.broadcasted_iota(jnp.int32, (half, half), 1)
    same_pair = row // (2 * bs) == col // (2 * bs)
    eye = (row == col).astype(F32)
    lower = row // bs > col // bs

    def inverse(block):
        within = jnp.where(same_pair, block, 0.0)
        f = eye - within
        return f - mul(mul(f, block - within), f)

    o = cells
    ga = mul(jnp.where(lower, dense[o : o + half, 0:half], 0.0), pa)
    gb = mul(jnp.where(lower, dense[o + half : o + cells, half:cells], 0.0), pb)
    gx = mul(dense[o + half : o + cells, 0:half], pa)
    fa, fb = inverse(ga), inverse(gb)
    fx = -mul(mul(fb, gx), fa)
    pf[0:half, 0:half] = mul(pa, fa)
    pf[0:half, half:cells] = jnp.zeros((half, half), F32)
    pf[half:cells, 0:half] = mul(pb, fx)
    pf[half:cells, half:cells] = mul(pb, fb)
    n = mul(dense[2 * cells : 3 * cells], pf[...])
    nh[...], nl[...] = parts(n, 2)
    nt = n.T
    tf[...] = nt
    th[...], tl[...] = parts(nt, 2)

    edges = from_before.astype(jnp.int32) + to_next.astype(jnp.int32)
    pl.semaphore_wait(barrier, SPAN - 1 + ny - 1 + nz - 1 + edges)

    def copy(src, dst, send, recv, device):
        return pltpu.make_async_remote_copy(
            src_ref=src, dst_ref=dst, send_sem=send, recv_sem=recv,
            device_id=device, device_id_type=pl.DeviceIdType.MESH,
        )

    def link(kind, m, src, dst, device):
        return copy(src, dst.at[m], link_send.at[kind, m], link_recv.at[kind, m], (device, mz))

    def links(m):
        z = va.at[mz, m]
        return dict(
            u=link(0, m, u_src.at[m], u_dst, me + 1),
            s=link(1, m, s_src.at[m], s_dst, me - 1),
            k=link(2, m, k_src.at[m], k_dst, me + 2),
            w=link(3, m, w_src.at[m], w_dst, me + 1),
            far=link(4, m, z, far, me - 2),
            back=link(5, m, z, above, me - 1),
            on=link(6, m, z, below, me + 1),
            g=link(7, m, g_src.at[m], g_dst, me + 4),
            h=link(8, m, z, h_dst, me - 4),
            e=link(9, m, e_src.at[m], e_dst, me - 2),
        )

    def to_z(array, m, kind):
        return [
            copy(array.at[mz, m], array.at[mz, m], z_send.at[kind, o - 1], z_recv.at[kind, o - 1], z_peer(o))
            for o in range(1, nz)
        ]

    def spread(array, at, send, recv, peer, count):
        return [
            copy(array.at[at], array.at[at], send.at[o - 1], recv.at[o - 1], peer(o)) for o in range(1, count)
        ]

    begun = []

    def begin(copies):
        for s in copies:
            s.start()
        begun.extend(copies)

    def values(refs, rows=slice(None)):
        return [ref[rows] for ref in refs]

    n_refs, t_refs, s_refs = (nh, nl), (th, tl), (sh, sl)
    turn = chip == chips - 1
    ahead = chip < chips - 1
    pair_n = copy(tf, other, pair_send.at[0], pair_recv.at[0], (me - 1, mz))
    pair_s = copy(sf, other, pair_send.at[1], pair_recv.at[1], (me - 1, mz))

    @pl.when(odd & ahead)
    def _():
        pair_n.start()

    pair_k = [
        copy(other.at[part], third.at[part], pair_send.at[2 + i], pair_recv.at[2 + i], (me - 2, mz))
        for i, part in enumerate((slice(0, half), slice(half, cells)))
    ]
    at_once = links(0)

    @pl.when(first)
    def _():
        w_src[0] = times(r[...], values(t_refs))
        at_once["w"].start()

    @pl.when(pos == 1)
    def _():
        at_once["w"].wait_recv()
        c[...] = r[...] - w_dst[0]
        u_src[0] = times(c[...], values(t_refs))
        at_once["u"].start()

    def middle():
        low = mul(fb.T, pf[half:cells])
        sf[half:cells] = low
        sh[half:cells], sl[half:cells] = parts(low, 2)
        high = mul(fx.T, pf[half:cells])
        corner = mul(fa.T, pf[0:half, 0:half])
        high = jnp.concatenate([high[:, 0:half] + corner, high[:, half:cells]], axis=1)
        sf[0:half] = high
        sh[0:half], sl[0:half] = parts(high, 2)

    kt_refs, k_refs = (joint.at[0], joint.at[1]), (joint.at[2], joint.at[3])
    two_t, two = (joint.at[4], joint.at[5]), (joint.at[6], joint.at[7])

    @pl.when(even & ahead)
    def _():
        pair_n.wait_recv()
        kt = mul_parts(values(t_refs), parts(other[...], 2))
        for ref, p in zip(kt_refs, parts(kt, 2)):
            ref[...] = p
        other[...] = kt

    @pl.when(pos == 4)
    def _():
        pair_k[0].start()

    @pl.when(pos != 2)
    def _():
        middle()

    @pl.when(last)
    def _():
        pair_s.start()

    @pl.when(me == 0)
    def _():
        below[...] = jnp.zeros(below.shape, F32)

    @pl.when(me == nr - 1)
    def _():
        above[...] = jnp.zeros(above.shape, F32)


    def split_dense():
        for i in range(3):
            rows = slice(i * cells, (i + 1) * cells)
            for ref, p in zip((dh, dm, dl), parts(dense[rows], 3)):
                ref[rows] = p

    @pl.when(even & turn)
    def _():
        pair_s.wait_recv()
        x = mul_parts(parts(other[...], 2), values(n_refs))
        e = sf[...] + mul_parts(values(t_refs), parts(x, 2))
        for ref, p in zip(s_refs, parts(e, 2)):
            ref[...] = p

    def back_product():
        for ref, p in zip(k_refs, parts(other[...].T, 2)):
            ref[...] = p

    for m in range(2):
        source = r if m == 0 else wa.at[mz, 0]
        at = links(m)
        begins = 1 if m == 0 else 0

        @pl.when(odd & ahead & (chip >= begins))
        def _():
            u_src[m] = times(source[...], values(t_refs))
            at["u"].start()

        @pl.when(last)
        def _():
            s_src[m] = times(source[...], values(s_refs))
            at["s"].start()

        if m == 0:

            @pl.when((pos > 2))
            def _():
                split_dense()

        early = to_z(va, 0, 0) + to_z(wa, 0, 1) if m == 1 else []

        if m == 1:

            @pl.when(odd | (chip >= chips - 2))
            def _():
                for s in early:
                    s.start()

        @pl.when(odd & (chip >= begins))
        def _():
            at["w"].wait_recv()
            c[...] = source[...] - w_dst[m]

        @pl.when(odd & ahead)
        def _():
            s_src[m] = times(c[...], values(s_refs))
            at["s"].start()

        if m == 0:

            @pl.when(pos == 1)
            def _():
                split_dense()

        @pl.when(odd & ahead)
        def _():
            at["back"].wait_recv()
            va[mz, m] = s_src[m] - times(above[m], values(n_refs))

        @pl.when(last)
        def _():
            va[mz, m] = times(c[...], values(s_refs))

        @pl.when(first)
        def _():
            c[...] = source[...]

        def other_half():
            at["s"].wait_recv()
            sv[...] = times(s_dst[m], values(n_refs))

        @pl.when(even & turn)
        def _():
            other_half()

        @pl.when(even & (chip > 0))
        def _():
            at["u"].wait_recv()
            c[...] = source[...] - u_dst[m]

        direct = m == 1
        if direct:

            @pl.when(pos == 4)
            def _():
                k_src[m] = times(c[...], values(kt_refs))
                at["k"].start()

        @pl.when(even & (chip > begins))
        def _():
            at["k"].wait_recv()
            c[...] = c[...] + k_dst[m]

        if direct:

            @pl.when(pos == 6)
            def _():
                at["g"].wait_recv()
                c[...] = c[...] + g_dst[m]

            @pl.when(pos == 2)
            def _():
                g_src[m] = times(c[...], values(two_t))
                at["g"].start()

        @pl.when(even & ahead & (chip >= begins) & ((pos != 4) if direct else (pos >= 0)))
        def _():
            k_src[m] = times(c[...], values(kt_refs))
            at["k"].start()

        @pl.when(even & ahead & (chip >= begins))
        def _():
            w_src[m] = times(c[...], values(t_refs))
            at["w"].start()

        if m == 1:

            @pl.when(even & (chip < chips - 2))
            def _():
                for s in early:
                    s.start()

        begun.extend(early)
        if m == 0:

            @pl.when(pos == 2)
            def _():
                middle()

            @pl.when(even & ahead)
            def _():
                back_product()

            @pl.when(even & (pos <= 2))
            def _():
                split_dense()

        @pl.when(even & ahead)
        def _():
            other_half()
            c[...] = times(c[...], values(s_refs)) - sv[...]

        if direct:

            @pl.when(pos == 4)
            def _():
                e_src[m] = c[...]
                at["e"].start()

            @pl.when(pos == 2)
            def _():
                at["e"].wait_recv()
                c[...] = c[...] + times(e_dst[m], values(k_refs))
                at["h"].wait_recv()
                va[mz, m] = c[...] + times(h_dst[m], values(two))

        @pl.when(even & ahead & ((pos != 2) if direct else (pos >= 0)))
        def _():
            at["far"].wait_recv()
            va[mz, m] = c[...] + times(far[m], values(k_refs))

        @pl.when(even & turn)
        def _():
            va[mz, m] = times(c[...], values(s_refs)) - sv[...]

        if direct:

            @pl.when(pos == 6)
            def _():
                at["h"].start()

        @pl.when(even & (chip > 0) & ((pos != 4) if direct else (pos >= 0)))
        def _():
            at["far"].start()

        @pl.when(even & turn)
        def _():
            w_src[m] = times(c[...], values(t_refs))
            at["w"].start()

        @pl.when(has_before)
        def _():
            at["back"].start()

        @pl.when(has_next)
        def _():
            at["on"].start()

        if m == 1:
            begin(to_z(va, 1, 2))

        if m == 0:

            @pl.when(pos == 4)
            def _():
                pair_k[1].start()

        d = (dh, dm, dl)

        def part(value, i):
            return times(value, values(d, slice(i * cells, (i + 1) * cells)))

        c[...] = part(va[mz, m], 1)

        @pl.when(from_before)
        def _():
            at["on"].wait_recv()

        @pl.when(first)
        def _():
            wa[mz, m] = part(below[m], 0)

        @pl.when(jnp.logical_not(odd) )
        def _():
            at["back"].wait_recv()

        @pl.when(jnp.logical_not(last))
        def _():
            sv[...] = part(above[m], 2)

        if m == 1:
            @pl.when(first)
            def _():
                far[0] = 0.5 * c[...] + sv[...] + wa[mz, m]

            @pl.when(jnp.logical_not(first | last))
            def _():
                far[0] = 0.5 * c[...] + sv[...]

            @pl.when(last)
            def _():
                far[0] = 0.5 * c[...]

            for kind in range(2):
                for s in to_z(va, kind, 2 * kind):
                    s.wait_recv()
            left = jnp.concatenate([wa[mz, 0], far[0], r[...]], axis=0)
            right = va[...].reshape(nz * 16, cells)
            red_x[pos] = lax.dot_general(
                left, right, (((1,), (1,)), ((), ())),
                precision=lax.Precision.HIGHEST, preferred_element_type=F32,
            )
            over_x = spread(red_x, pos, x_send, x_recv, x_peer, SPAN)
            begin(over_x)

        @pl.when(to_next)
        def _():
            at["back"].wait_recv()

        @pl.when(last)
        def _():
            sv[...] = part(above[m], 2)

        @pl.when(has_before & jnp.logical_not(first))
        def _():
            at["on"].wait_recv()

        @pl.when(jnp.logical_not(first))
        def _():
            wa[mz, m] = part(below[m], 0)

        wa[mz, m] = c[...] + sv[...] + wa[mz, m]
        if m == 1:
            begin(to_z(wa, 1, 3))

        else:

            @pl.when(pos == 2)
            def _():
                for p in pair_k:
                    p.wait_recv()
                t = mul_parts(values(kt_refs), parts(third[...], 2))
                for ref, p in zip(two_t, parts(t, 2)):
                    ref[...] = p
                for ref, p in zip(two, parts(t.T, 2)):
                    ref[...] = p


    def total(array, count):
        value = array[0]
        for i in range(1, count):
            value = value + array[i]
        return value

    for s in over_x:
        s.wait_recv()
    red_y[where] = total(red_x, SPAN)
    over_y = spread(red_y, where, y_send, y_recv, y_peer, ny)
    begin(over_y)
    for s in over_y:
        s.wait_recv()
    both = total(red_y, ny)
    r_out[...] = both[16:24]
    red_z[mz] = both[0:16]
    over_z = spread(red_z, mz, k_send, k_recv, z_peer, nz)
    begin(over_z)
    for m in range(2):
        for s in to_z(wa, m, 2 * m + 1):
            s.wait_recv()
    v_out[...] = va[...].reshape(nz * 16, cells)
    w_out[...] = wa[...].reshape(nz * 16, cells)
    for s in over_z:
        s.wait_recv()
    k_out[...] = red_z[...].reshape(nz * 16, nz * 16)
    for s in begun:
        s.wait_send()

    @pl.when(odd & ahead)
    def _():
        pair_n.wait_send()

    @pl.when(last)
    def _():
        pair_s.wait_send()

    @pl.when(pos == 4)
    def _():
        for p in pair_k:
            p.wait_send()

    for m in range(2):
        at = links(m)
        for name, started in (
            ("u", odd & ahead),
            ("s", odd),
            ("k", even & ahead & (chip >= (1 if m == 0 else 0))),
            ("w", even),
            ("far", even & (chip > 0) & ((pos != 4) if m == 1 else (pos >= 0))),
            ("g", (pos == 2) & (m == 1)),
            ("h", (pos == 6) & (m == 1)),
            ("e", (pos == 4) & (m == 1)),
            ("back", has_before),
            ("on", has_next),
        ):

            @pl.when(started)
            def _():
                at[name].wait_send()


def krylov(nr, nz, cols, tiles, r, pivots):
    rhs, cells = r.shape
    ny = nr // SPAN
    dma = pltpu.SemaphoreType.DMA
    every = nz * 2 * rhs
    vector = pltpu.VMEM((rhs, cells), F32)
    square, square_half = pltpu.VMEM((cells, cells), F32), pltpu.VMEM((cells, cells), BF)
    vectors = pltpu.VMEM((2, rhs, cells), F32)
    return pl.pallas_call(
        functools.partial(krylov_kernel, nr, nz),
        out_shape=[
            jax.ShapeDtypeStruct((every, cells), F32),
            jax.ShapeDtypeStruct((every, cells), F32),
            jax.ShapeDtypeStruct((every, every), F32),
            jax.ShapeDtypeStruct((rhs, every), F32),
        ],
        in_specs=[pl.BlockSpec(memory_space=pltpu.HBM)] * 4,
        out_specs=[VMEM] * 4,
        scratch_shapes=[pltpu.SMEM(cols.shape, jnp.int32), vector, pltpu.VMEM(pivots.shape, F32)]
        + [pltpu.VMEM(tiles.shape, F32), pltpu.VMEM((3 * cells, cells), F32)]
        + [pltpu.VMEM((3 * cells, cells), BF)] * 3
        + [square_half] * 6
        + [square] * 3
        + [pltpu.VMEM((nz, 2, rhs, cells), F32)] * 2
        + [vector] * 2
        + [square, square, pltpu.VMEM((8, cells, cells), BF)]
        + [vectors] * 16
        + [
            pltpu.VMEM((SPAN, 3 * rhs, every), F32),
            pltpu.VMEM((ny, 3 * rhs, every), F32),
            pltpu.VMEM((nz, 2 * rhs, every), F32),
        ]
        + [dma((tiles.shape[0],)), dma((3,))]
        + [dma((10, 2))] * 2
        + [dma((4,))] * 2
        + [dma((4, max(nz - 1, 1)))] * 2
        + [dma((SPAN - 1,))] * 2
        + [dma((max(ny - 1, 1),))] * 2
        + [dma((max(nz - 1, 1),))] * 2,
        compiler_params=pltpu.CompilerParams(
            collective_id=0, has_side_effects=True, vmem_limit_bytes=60 * MIB
        ),
    )(cols, tiles, r, pivots)


def spd_inverse(k, block):
    size = k.shape[0]
    row_of = lax.broadcasted_iota(jnp.int32, (size, 1), 0)
    col_of = lax.broadcasted_iota(jnp.int32, (1, size), 1)
    span = range(block)
    for b in range(0, size, block):
        d = [[jnp.broadcast_to(k[b + i : b + i + 1, b + j : b + j + 1], (1, size)) for j in span] for i in span]
        for p in span:
            inv = 1.0 / d[p][p]
            row = [inv if j == p else d[p][j] * inv for j in span]
            for i in span:
                if i != p:
                    f = d[i][p]
                    d[i] = [-f * row[p] if j == p else d[i][j] - f * row[j] for j in span]
            d[p] = row
        in_cols = (col_of >= b) & (col_of < b + block)
        in_rows = (row_of >= b) & (row_of < b + block)
        base = jnp.where(in_rows | in_cols, 0.0, k)
        for i in span:
            row, corner = d[i][0] * k[b : b + 1, :], d[i][0]
            for j in range(1, block):
                row = row + d[i][j] * k[b + j : b + j + 1, :]
                corner = jnp.where(col_of == b + j, d[i][j], corner)
            row = jnp.where(in_cols, corner, row)
            col = jnp.where(in_rows, jnp.where(row_of == b + i, -1.0, 0.0), k[:, b + i : b + i + 1])
            base = base - col * row
        k = base
    return k


def solve_kernel(k_in, rt_in, v_in, w_in, r_in, x_out, r_out, k_buf, rt, v, w, r, sems):
    whole = ((k_in, k_buf), (rt_in, rt), (v_in, v), (w_in, w), (r_in, r))
    fetch = [pltpu.make_async_copy(src, dst, sems.at[i]) for i, (src, dst) in enumerate(whole)]
    for f in fetch:
        f.start()
    fetch[0].wait()
    size = k_buf.shape[0]
    k = k_buf[...]
    kt = k.T
    row_of = lax.broadcasted_iota(jnp.int32, (size, 1), 0)
    col_of = lax.broadcasted_iota(jnp.int32, (1, size), 1)
    row_p, col_p = lax.rem(row_of // 8, 2) == 1, lax.rem(col_of // 8, 2) == 1
    both = k + kt
    k = jnp.where(row_p, jnp.where(col_p, both, kt), jnp.where(col_p, k, 0.5 * both))
    high = lax.Precision.HIGHEST
    inverse = spd_inverse(k, 4)
    for f in fetch[1:]:
        f.wait()
    c = jnp.dot(rt[...], inverse, precision=high, preferred_element_type=F32)
    x_out[...] = jnp.dot(c, v[...], precision=high, preferred_element_type=F32)
    r_out[...] = r[...] - jnp.dot(c, w[...], precision=high, preferred_element_type=F32)


def solve(k, rt, v, w, r):
    operands = (k, rt, v, w, r)
    return pl.pallas_call(
        solve_kernel,
        out_shape=[jax.ShapeDtypeStruct(r.shape, F32)] * 2,
        in_specs=[pl.BlockSpec(memory_space=pltpu.HBM)] * 5,
        out_specs=[VMEM] * 2,
        scratch_shapes=[pltpu.VMEM(o.shape, F32) for o in operands] + [pltpu.SemaphoreType.DMA((5,))],
        compiler_params=pltpu.CompilerParams(vmem_limit_bytes=60 * MIB),
    )(*operands)


def solution(mesh):
    nr, nz = mesh.shape["rows"], mesh.shape["rhs"]

    def shards(right_side, tiles, pivots, columns):
        v, w, k, rt = krylov(nr, nz, columns, tiles, right_side, pivots)
        return tuple(solve(k, rt, v, w, right_side))

    return jax.shard_map(
        shards,
        mesh=mesh,
        in_specs=(
            P("rhs", "rows"),
            P("rows", None, None, None),
            P("rows", None, None),
            P("rows", None),
        ),
        out_specs=(P("rhs", "rows"), P("rhs", "rows")),
        check_vma=False,
    )
```

```python
import functools

import jax
import jax.numpy as jnp
from jax import lax
from jax.experimental import pallas as pl
from jax.experimental.pallas import tpu as pltpu
from jax.sharding import PartitionSpec as P

SPAN = 8
BF, F32 = jnp.bfloat16, jnp.float32
MIB = 1 << 20
VMEM = pl.BlockSpec(memory_space=pltpu.VMEM)
SMEM = pl.BlockSpec(memory_space=pltpu.SMEM)


def parts(x, n):
    out = []
    for _ in range(n):
        high = x.astype(BF)
        out.append(high)
        x = x - high.astype(F32)
    return out


def dot(a, b):
    return jnp.dot(a, b, preferred_element_type=F32)


def mul(a, b):
    (ah, al), (bh, bl) = parts(a, 2), parts(b, 2)
    return dot(ah, bh) + (dot(ah, bl) + dot(al, bh))


def times(x, weights):
    n = x.shape[0]
    count = len(weights)
    stack = jnp.concatenate([p.astype(F32) for p in parts(x, count)], axis=0)
    if count * n % 16:
        stack = jnp.concatenate([stack, jnp.zeros((16 - count * n % 16, x.shape[1]), F32)], axis=0)
    stack = stack.astype(BF)
    total = None
    for w in reversed(weights):
        y = dot(stack, w)
        for i in reversed(range(count)):
            y_i = y[i * n : (i + 1) * n]
            total = y_i if total is None else total + y_i
    return total


def mul_parts(a, b):
    (ah, al), (bh, bl) = a, b
    return dot(ah, bh) + (dot(ah, bl) + dot(al, bh))


def krylov_kernel(
    nr, nz,
    cols_in, tiles, r_in, pivots_in,
    v_out, w_out, k_out, r_out,
    cols, r, pivots, held, dense, dh, dm, dl, nh, nl, th, tl, sh, sl, tf, sf, pf,
    va, wa, c, sv, other, third, joint,
    u_src, u_dst, s_src, s_dst, k_src, k_dst, w_src, w_dst, far, above, below,
    g_src, g_dst, h_dst, e_src, e_dst,
    red_x, red_y, red_z, rt,
    tile_sem, in_sem, out_sem, link_send, link_recv, pair_send, pair_recv,
    z_send, z_recv, x_send, x_recv, y_send, y_recv, k_send, k_recv,
):
    me, mz = lax.axis_index("rows"), lax.axis_index("rhs")
    pos, where = lax.rem(me, SPAN), lax.div(me, SPAN)
    chip, odd = lax.div(pos, 2), lax.rem(pos, 2) == 1
    even = jnp.logical_not(odd)
    chips = SPAN // 2
    ny = nr // SPAN
    first, last = pos == 0, pos == SPAN - 1
    cells = r.shape[1]

    def x_peer(o):
        return (where * SPAN + lax.rem(pos + o, SPAN), mz)

    def y_peer(o):
        return (lax.rem(where + o, ny) * SPAN + pos, mz)

    def z_peer(o):
        return (me, lax.rem(mz + o, nz))

    group, slots, bs = held.shape[0], held.shape[1], held.shape[2]
    fetch = [pltpu.make_async_copy(tiles.at[i], held.at[i], tile_sem.at[i]) for i in range(group)]
    whole = ((cols_in, cols), (pivots_in, pivots), (r_in, r))
    fetch += [pltpu.make_async_copy(src, dst, in_sem.at[i]) for i, (src, dst) in enumerate(whole)]
    for f in fetch[group:] + fetch[:group]:
        f.start()
    barrier = pltpu.get_barrier_semaphore()

    def hello(device):
        pl.semaphore_signal(barrier, inc=1, device_id=device, device_id_type=pl.DeviceIdType.MESH)

    for o in range(1, SPAN):
        hello(x_peer(o))
    for o in range(1, ny):
        hello(y_peer(o))
    for o in range(1, nz):
        hello(z_peer(o))
    has_before, has_next = me > 0, me < nr - 1
    from_before, to_next = first & has_before, last & has_next

    @pl.when(from_before)
    def _():
        hello((me - 1, mz))

    @pl.when(to_next)
    def _():
        hello((me + 1, mz))

    half = cells // 2

    def block(i, j):
        return (slice(i * bs, (i + 1) * bs), slice(j * bs, (j + 1) * bs))

    nothing = jnp.zeros((bs, bs), F32)
    for f in fetch[group:]:
        f.wait()
    for i in range(group):
        fetch[i].wait()
        away = [cols[i, k] - cols[i, 0] for k in range(1, slots)]
        for delta in range(-group, group + 1):
            tile = held[i, 0] if delta == 0 else None
            for k in range(1, slots):
                term = held[i, k] * (away[k - 1] == delta).astype(F32)
                tile = term if tile is None else tile + term
            j = i + delta
            if 0 <= j < group:
                dense[block(group + i, j)] = tile
            else:
                dense[block(group + j, i)] = tile.T
        for j in range(group):
            if j < i:
                dense[block(j, i)] = nothing
            if j > i:
                dense[block(2 * group + j, i)] = nothing

    def block_diagonal(first_row):
        zero = jnp.zeros((bs, bs), F32)
        count = half // bs
        return jnp.concatenate(
            [
                jnp.concatenate([pivots[first_row + i] if i == j else zero for j in range(count)], axis=1)
                for i in range(count)
            ],
            axis=0,
        )

    pa, pb = block_diagonal(0), block_diagonal(half // bs)
    row = lax.broadcasted_iota(jnp.int32, (half, half), 0)
    col = lax.broadcasted_iota(jnp.int32, (half, half), 1)
    same_pair = row // (2 * bs) == col // (2 * bs)
    eye = (row == col).astype(F32)
    lower = row // bs > col // bs

    def inverse(block):
        within = jnp.where(same_pair, block, 0.0)
        f = eye - within
        return f - mul(mul(f, block - within), f)

    o = cells
    ga = mul(jnp.where(lower, dense[o : o + half, 0:half], 0.0), pa)
    gb = mul(jnp.where(lower, dense[o + half : o + cells, half:cells], 0.0), pb)
    gx = mul(dense[o + half : o + cells, 0:half], pa)
    fa, fb = inverse(ga), inverse(gb)
    fx = -mul(mul(fb, gx), fa)
    pf[0:half, 0:half] = mul(pa, fa)
    pf[0:half, half:cells] = jnp.zeros((half, half), F32)
    pf[half:cells, 0:half] = mul(pb, fx)
    pf[half:cells, half:cells] = mul(pb, fb)
    n = mul(dense[2 * cells : 3 * cells], pf[...])
    nh[...], nl[...] = parts(n, 2)
    nt = n.T
    tf[...] = nt
    th[...], tl[...] = parts(nt, 2)

    edges = from_before.astype(jnp.int32) + to_next.astype(jnp.int32)
    pl.semaphore_wait(barrier, SPAN - 1 + ny - 1 + nz - 1 + edges)

    def copy(src, dst, send, recv, device):
        return pltpu.make_async_remote_copy(
            src_ref=src, dst_ref=dst, send_sem=send, recv_sem=recv,
            device_id=device, device_id_type=pl.DeviceIdType.MESH,
        )

    def link(kind, m, src, dst, device):
        return copy(src, dst.at[m], link_send.at[kind, m], link_recv.at[kind, m], (device, mz))

    def links(m):
        z = va.at[mz, m]
        return dict(
            u=link(0, m, u_src.at[m], u_dst, me + 1),
            s=link(1, m, s_src.at[m], s_dst, me - 1),
            k=link(2, m, k_src.at[m], k_dst, me + 2),
            w=link(3, m, w_src.at[m], w_dst, me + 1),
            far=link(4, m, z, far, me - 2),
            back=link(5, m, z, above, me - 1),
            on=link(6, m, z, below, me + 1),
            g=link(7, m, g_src.at[m], g_dst, me + 4),
            h=link(8, m, z, h_dst, me - 4),
            e=link(9, m, e_src.at[m], e_dst, me - 2),
        )

    def to_z(array, m, kind):
        return [
            copy(array.at[mz, m], array.at[mz, m], z_send.at[kind, o - 1], z_recv.at[kind, o - 1], z_peer(o))
            for o in range(1, nz)
        ]

    def spread(array, at, send, recv, peer, count):
        return [
            copy(array.at[at], array.at[at], send.at[o - 1], recv.at[o - 1], peer(o)) for o in range(1, count)
        ]

    begun = []

    def begin(copies):
        for s in copies:
            s.start()
        begun.extend(copies)

    def values(refs, rows=slice(None)):
        return [ref[rows] for ref in refs]

    n_refs, t_refs, s_refs = (nh, nl), (th, tl), (sh, sl)
    turn = chip == chips - 1
    ahead = chip < chips - 1
    pair_n = copy(tf, other, pair_send.at[0], pair_recv.at[0], (me - 1, mz))
    pair_s = copy(sf, other, pair_send.at[1], pair_recv.at[1], (me - 1, mz))

    @pl.when(odd & ahead)
    def _():
        pair_n.start()

    pair_k = [
        copy(other.at[part], third.at[part], pair_send.at[2 + i], pair_recv.at[2 + i], (me - 2, mz))
        for i, part in enumerate((slice(0, half), slice(half, cells)))
    ]
    at_once = links(0)

    @pl.when(first)
    def _():
        w_src[0] = times(r[...], values(t_refs))
        at_once["w"].start()

    @pl.when(pos == 1)
    def _():
        at_once["w"].wait_recv()
        c[...] = r[...] - w_dst[0]
        u_src[0] = times(c[...], values(t_refs))
        at_once["u"].start()

    def middle():
        low = mul(fb.T, pf[half:cells])
        sf[half:cells] = low
        sh[half:cells], sl[half:cells] = parts(low, 2)
        high = mul(fx.T, pf[half:cells])
        corner = mul(fa.T, pf[0:half, 0:half])
        high = jnp.concatenate([high[:, 0:half] + corner, high[:, half:cells]], axis=1)
        sf[0:half] = high
        sh[0:half], sl[0:half] = parts(high, 2)

    kt_refs, k_refs = (joint.at[0], joint.at[1]), (joint.at[2], joint.at[3])
    two_t, two = (joint.at[4], joint.at[5]), (joint.at[6], joint.at[7])

    @pl.when(even & ahead)
    def _():
        pair_n.wait_recv()
        kt = mul_parts(values(t_refs), parts(other[...], 2))
        for ref, p in zip(kt_refs, parts(kt, 2)):
            ref[...] = p
        other[...] = kt

    @pl.when(pos == 4)
    def _():
        pair_k[0].start()

    @pl.when(pos != 2)
    def _():
        middle()

    @pl.when(last)
    def _():
        pair_s.start()

    @pl.when(me == 0)
    def _():
        below[...] = jnp.zeros(below.shape, F32)

    @pl.when(me == nr - 1)
    def _():
        above[...] = jnp.zeros(above.shape, F32)


    def split_dense():
        for i in range(3):
            rows = slice(i * cells, (i + 1) * cells)
            for ref, p in zip((dh, dm, dl), parts(dense[rows], 3)):
                ref[rows] = p

    @pl.when(even & turn)
    def _():
        pair_s.wait_recv()
        x = mul_parts(parts(other[...], 2), values(n_refs))
        e = sf[...] + mul_parts(values(t_refs), parts(x, 2))
        for ref, p in zip(s_refs, parts(e, 2)):
            ref[...] = p

    def back_product():
        for ref, p in zip(k_refs, parts(other[...].T, 2)):
            ref[...] = p

    for m in range(2):
        source = r if m == 0 else wa.at[mz, 0]
        at = links(m)
        begins = 1 if m == 0 else 0

        @pl.when(odd & ahead & (chip >= begins))
        def _():
            u_src[m] = times(source[...], values(t_refs))
            at["u"].start()

        @pl.when(last)
        def _():
            s_src[m] = times(source[...], values(s_refs))
            at["s"].start()

        if m == 0:

            @pl.when((pos > 2))
            def _():
                split_dense()

        early = to_z(va, 0, 0) + to_z(wa, 0, 1) if m == 1 else []

        if m == 1:

            @pl.when(odd | (chip >= chips - 2))
            def _():
                for s in early:
                    s.start()

        @pl.when(odd & (chip >= begins))
        def _():
            at["w"].wait_recv()
            c[...] = source[...] - w_dst[m]

        @pl.when(odd & ahead)
        def _():
            s_src[m] = times(c[...], values(s_refs))
            at["s"].start()

        if m == 0:

            @pl.when(pos == 1)
            def _():
                split_dense()

        @pl.when(odd & ahead)
        def _():
            at["back"].wait_recv()
            va[mz, m] = s_src[m] - times(above[m], values(n_refs))

        @pl.when(last)
        def _():
            va[mz, m] = times(c[...], values(s_refs))

        @pl.when(first)
        def _():
            c[...] = source[...]

        def other_half():
            at["s"].wait_recv()
            sv[...] = times(s_dst[m], values(n_refs))

        @pl.when(even & turn)
        def _():
            other_half()

        @pl.when(even & (chip > 0))
        def _():
            at["u"].wait_recv()
            c[...] = source[...] - u_dst[m]

        direct = m == 1
        if direct:

            @pl.when(pos == 4)
            def _():
                k_src[m] = times(c[...], values(kt_refs))
                at["k"].start()

        @pl.when(even & (chip > begins))
        def _():
            at["k"].wait_recv()
            c[...] = c[...] + k_dst[m]

        if direct:

            @pl.when(pos == 6)
            def _():
                at["g"].wait_recv()
                c[...] = c[...] + g_dst[m]

            @pl.when(pos == 2)
            def _():
                g_src[m] = times(c[...], values(two_t))
                at["g"].start()

        @pl.when(even & ahead & (chip >= begins) & ((pos != 4) if direct else (pos >= 0)))
        def _():
            k_src[m] = times(c[...], values(kt_refs))
            at["k"].start()

        @pl.when(even & ahead & (chip >= begins))
        def _():
            w_src[m] = times(c[...], values(t_refs))
            at["w"].start()

        if m == 1:

            @pl.when(even & (chip < chips - 2))
            def _():
                for s in early:
                    s.start()

        begun.extend(early)
        if m == 0:

            @pl.when(pos == 2)
            def _():
                middle()

            @pl.when(even & ahead)
            def _():
                back_product()

            @pl.when(even & (pos <= 2))
            def _():
                split_dense()

        @pl.when(even & ahead)
        def _():
            other_half()
            c[...] = times(c[...], values(s_refs)) - sv[...]

        if direct:

            @pl.when(pos == 4)
            def _():
                e_src[m] = c[...]
                at["e"].start()

            @pl.when(pos == 2)
            def _():
                at["e"].wait_recv()
                c[...] = c[...] + times(e_dst[m], values(k_refs))
                at["h"].wait_recv()
                va[mz, m] = c[...] + times(h_dst[m], values(two))

        @pl.when(even & ahead & ((pos != 2) if direct else (pos >= 0)))
        def _():
            at["far"].wait_recv()
            va[mz, m] = c[...] + times(far[m], values(k_refs))

        @pl.when(even & turn)
        def _():
            va[mz, m] = times(c[...], values(s_refs)) - sv[...]

        if direct:

            @pl.when(pos == 6)
            def _():
                at["h"].start()

        @pl.when(even & (chip > 0) & ((pos != 4) if direct else (pos >= 0)))
        def _():
            at["far"].start()

        @pl.when(even & turn)
        def _():
            w_src[m] = times(c[...], values(t_refs))
            at["w"].start()

        @pl.when(has_before)
        def _():
            at["back"].start()

        @pl.when(has_next)
        def _():
            at["on"].start()

        if m == 1:
            begin(to_z(va, 1, 2))

        if m == 0:

            @pl.when(pos == 4)
            def _():
                pair_k[1].start()

        d = (dh, dm, dl)

        def part(value, i):
            return times(value, values(d, slice(i * cells, (i + 1) * cells)))

        c[...] = part(va[mz, m], 1)

        @pl.when(from_before)
        def _():
            at["on"].wait_recv()

        @pl.when(first)
        def _():
            wa[mz, m] = part(below[m], 0)

        @pl.when(jnp.logical_not(odd) )
        def _():
            at["back"].wait_recv()

        @pl.when(jnp.logical_not(last))
        def _():
            sv[...] = part(above[m], 2)

        if m == 1:
            @pl.when(first)
            def _():
                far[0] = 0.5 * c[...] + sv[...] + wa[mz, m]

            @pl.when(jnp.logical_not(first | last))
            def _():
                far[0] = 0.5 * c[...] + sv[...]

            @pl.when(last)
            def _():
                far[0] = 0.5 * c[...]

            for kind in range(2):
                for s in to_z(va, kind, 2 * kind):
                    s.wait_recv()
            left = jnp.concatenate([wa[mz, 0], far[0], r[...]], axis=0)
            right = va[...].reshape(nz * 16, cells)
            red_x[pos] = lax.dot_general(
                left, right, (((1,), (1,)), ((), ())),
                precision=lax.Precision.HIGHEST, preferred_element_type=F32,
            )
            over_x = spread(red_x, pos, x_send, x_recv, x_peer, SPAN)
            begin(over_x)

        @pl.when(to_next)
        def _():
            at["back"].wait_recv()

        @pl.when(last)
        def _():
            sv[...] = part(above[m], 2)

        @pl.when(has_before & jnp.logical_not(first))
        def _():
            at["on"].wait_recv()

        @pl.when(jnp.logical_not(first))
        def _():
            wa[mz, m] = part(below[m], 0)

        wa[mz, m] = c[...] + sv[...] + wa[mz, m]
        if m == 1:
            begin(to_z(wa, 1, 3))

        else:

            @pl.when(pos == 2)
            def _():
                for p in pair_k:
                    p.wait_recv()
                t = mul_parts(values(kt_refs), parts(third[...], 2))
                for ref, p in zip(two_t, parts(t, 2)):
                    ref[...] = p
                for ref, p in zip(two, parts(t.T, 2)):
                    ref[...] = p


    def total(array, count):
        value = array[0]
        for i in range(1, count):
            value = value + array[i]
        return value

    for s in over_x:
        s.wait_recv()
    red_y[where] = total(red_x, SPAN)
    over_y = spread(red_y, where, y_send, y_recv, y_peer, ny)
    begin(over_y)
    for s in over_y:
        s.wait_recv()
    both = total(red_y, ny)
    red_z[mz] = both[0:16]
    before = list(begun)
    over_z = spread(red_z, mz, k_send, k_recv, z_peer, nz)
    begin(over_z)
    rt[...] = both[16:24]
    results = [
        pltpu.make_async_copy(src, dst, out_sem.at[i])
        for i, (src, dst) in enumerate(((red_z, k_out), (rt, r_out), (va, v_out), (wa, w_out)))
    ]
    results[1].start()
    results[2].start()
    for m in range(2):
        for s in to_z(wa, m, 2 * m + 1):
            s.wait_recv()
    results[3].start()
    for s in before:
        s.wait_send()

    @pl.when(odd & ahead)
    def _():
        pair_n.wait_send()

    @pl.when(last)
    def _():
        pair_s.wait_send()

    @pl.when(pos == 4)
    def _():
        for p in pair_k:
            p.wait_send()

    for m in range(2):
        at = links(m)
        for name, started in (
            ("u", odd & ahead),
            ("s", odd),
            ("k", even & ahead & (chip >= (1 if m == 0 else 0))),
            ("w", even),
            ("far", even & (chip > 0) & ((pos != 4) if m == 1 else (pos >= 0))),
            ("g", (pos == 2) & (m == 1)),
            ("h", (pos == 6) & (m == 1)),
            ("e", (pos == 4) & (m == 1)),
            ("back", has_before),
            ("on", has_next),
        ):

            @pl.when(started)
            def _():
                at[name].wait_send()

    for s in over_z:
        s.wait_recv()
    results[0].start()
    for s in over_z:
        s.wait_send()
    for f in results:
        f.wait()


def krylov(nr, nz, cols, tiles, r, pivots):
    rhs, cells = r.shape
    ny = nr // SPAN
    dma = pltpu.SemaphoreType.DMA
    every = nz * 2 * rhs
    vector = pltpu.VMEM((rhs, cells), F32)
    square, square_half = pltpu.VMEM((cells, cells), F32), pltpu.VMEM((cells, cells), BF)
    vectors = pltpu.VMEM((2, rhs, cells), F32)
    return pl.pallas_call(
        functools.partial(krylov_kernel, nr, nz),
        out_shape=[
            jax.ShapeDtypeStruct((nz, 2, rhs, cells), F32),
            jax.ShapeDtypeStruct((nz, 2, rhs, cells), F32),
            jax.ShapeDtypeStruct((nz, 2 * rhs, every), F32),
            jax.ShapeDtypeStruct((rhs, every), F32),
        ],
        in_specs=[pl.BlockSpec(memory_space=pltpu.HBM)] * 4,
        out_specs=[pl.BlockSpec(memory_space=pltpu.HBM)] * 4,
        scratch_shapes=[pltpu.SMEM(cols.shape, jnp.int32), vector, pltpu.VMEM(pivots.shape, F32)]
        + [pltpu.VMEM(tiles.shape, F32), pltpu.VMEM((3 * cells, cells), F32)]
        + [pltpu.VMEM((3 * cells, cells), BF)] * 3
        + [square_half] * 6
        + [square] * 3
        + [pltpu.VMEM((nz, 2, rhs, cells), F32)] * 2
        + [vector] * 2
        + [square, square, pltpu.VMEM((8, cells, cells), BF)]
        + [vectors] * 16
        + [
            pltpu.VMEM((SPAN, 3 * rhs, every), F32),
            pltpu.VMEM((ny, 3 * rhs, every), F32),
            pltpu.VMEM((nz, 2 * rhs, every), F32),
            pltpu.VMEM((rhs, every), F32),
        ]
        + [dma((tiles.shape[0],)), dma((3,)), dma((4,))]
        + [dma((10, 2))] * 2
        + [dma((4,))] * 2
        + [dma((4, max(nz - 1, 1)))] * 2
        + [dma((SPAN - 1,))] * 2
        + [dma((max(ny - 1, 1),))] * 2
        + [dma((max(nz - 1, 1),))] * 2,
        compiler_params=pltpu.CompilerParams(
            collective_id=0, has_side_effects=True, vmem_limit_bytes=60 * MIB
        ),
    )(cols, tiles, r, pivots)


def spd_inverse(k, block):
    size = k.shape[0]
    row_of = lax.broadcasted_iota(jnp.int32, (size, 1), 0)
    col_of = lax.broadcasted_iota(jnp.int32, (1, size), 1)
    span = range(block)
    for b in range(0, size, block):
        d = [[jnp.broadcast_to(k[b + i : b + i + 1, b + j : b + j + 1], (1, size)) for j in span] for i in span]
        for p in span:
            inv = 1.0 / d[p][p]
            row = [inv if j == p else d[p][j] * inv for j in span]
            for i in span:
                if i != p:
                    f = d[i][p]
                    d[i] = [-f * row[p] if j == p else d[i][j] - f * row[j] for j in span]
            d[p] = row
        in_cols = (col_of >= b) & (col_of < b + block)
        in_rows = (row_of >= b) & (row_of < b + block)
        base = jnp.where(in_rows | in_cols, 0.0, k)
        for i in span:
            row, corner = d[i][0] * k[b : b + 1, :], d[i][0]
            for j in range(1, block):
                row = row + d[i][j] * k[b + j : b + j + 1, :]
                corner = jnp.where(col_of == b + j, d[i][j], corner)
            row = jnp.where(in_cols, corner, row)
            col = jnp.where(in_rows, jnp.where(row_of == b + i, -1.0, 0.0), k[:, b + i : b + i + 1])
            base = base - col * row
        k = base
    return k


def solve_kernel(k_in, rt_in, v_in, w_in, r_in, x_out, r_out, k_buf, rt, v, w, r, sems):
    whole = ((k_in, k_buf), (rt_in, rt), (v_in, v), (w_in, w), (r_in, r))
    fetch = [pltpu.make_async_copy(src, dst, sems.at[i]) for i, (src, dst) in enumerate(whole)]
    for f in fetch:
        f.start()
    fetch[0].wait()
    size, cells = rt.shape[1], r.shape[1]
    k = k_buf[...].reshape(size, size)
    kt = k.T
    row_of = lax.broadcasted_iota(jnp.int32, (size, 1), 0)
    col_of = lax.broadcasted_iota(jnp.int32, (1, size), 1)
    row_p, col_p = lax.rem(row_of // 8, 2) == 1, lax.rem(col_of // 8, 2) == 1
    both = k + kt
    k = jnp.where(row_p, jnp.where(col_p, both, kt), jnp.where(col_p, k, 0.5 * both))
    high = lax.Precision.HIGHEST
    inverse = spd_inverse(k, 4)
    for f in fetch[1:]:
        f.wait()
    c = jnp.dot(rt[...], inverse, precision=high, preferred_element_type=F32)
    x_out[...] = jnp.dot(c, v[...].reshape(size, cells), precision=high, preferred_element_type=F32)
    r_out[...] = r[...] - jnp.dot(c, w[...].reshape(size, cells), precision=high, preferred_element_type=F32)


def solve(k, rt, v, w, r):
    operands = (k, rt, v, w, r)
    return pl.pallas_call(
        solve_kernel,
        out_shape=[jax.ShapeDtypeStruct(r.shape, F32)] * 2,
        in_specs=[pl.BlockSpec(memory_space=pltpu.HBM)] * 5,
        out_specs=[VMEM] * 2,
        scratch_shapes=[pltpu.VMEM(o.shape, F32) for o in operands] + [pltpu.SemaphoreType.DMA((5,))],
        compiler_params=pltpu.CompilerParams(vmem_limit_bytes=60 * MIB),
    )(*operands)


def solution(mesh):
    nr, nz = mesh.shape["rows"], mesh.shape["rhs"]

    def shards(right_side, tiles, pivots, columns):
        v, w, k, rt = krylov(nr, nz, columns, tiles, right_side, pivots)
        return tuple(solve(k, rt, v, w, right_side))

    return jax.shard_map(
        shards,
        mesh=mesh,
        in_specs=(
            P("rhs", "rows"),
            P("rows", None, None, None),
            P("rows", None, None),
            P("rows", None),
        ),
        out_specs=(P("rhs", "rows"), P("rhs", "rows")),
        check_vma=False,
    )
```

```python
import functools

import jax
import jax.numpy as jnp
from jax import lax
from jax.experimental import pallas as pl
from jax.experimental.pallas import tpu as pltpu
from jax.sharding import PartitionSpec as P

SPAN = 8
BF, F32 = jnp.bfloat16, jnp.float32
MIB = 1 << 20
VMEM = pl.BlockSpec(memory_space=pltpu.VMEM)
SMEM = pl.BlockSpec(memory_space=pltpu.SMEM)


def parts(x, n):
    out = []
    for _ in range(n):
        high = x.astype(BF)
        out.append(high)
        x = x - high.astype(F32)
    return out


def dot(a, b):
    return jnp.dot(a, b, preferred_element_type=F32)


def mul(a, b):
    (ah, al), (bh, bl) = parts(a, 2), parts(b, 2)
    return dot(ah, bh) + (dot(ah, bl) + dot(al, bh))


def times(x, weights):
    n = x.shape[0]
    count = len(weights)
    stack = jnp.concatenate([p.astype(F32) for p in parts(x, count)], axis=0)
    if count * n % 16:
        stack = jnp.concatenate([stack, jnp.zeros((16 - count * n % 16, x.shape[1]), F32)], axis=0)
    stack = stack.astype(BF)
    total = None
    for w in reversed(weights):
        y = dot(stack, w)
        for i in reversed(range(count)):
            y_i = y[i * n : (i + 1) * n]
            total = y_i if total is None else total + y_i
    return total


def mul_parts(a, b):
    (ah, al), (bh, bl) = a, b
    return dot(ah, bh) + (dot(ah, bl) + dot(al, bh))


def krylov_kernel(
    nr, nz,
    cols_in, tiles, r_in, pivots_in,
    v_out, w_out, k_out, r_out,
    cols, r, pivots, held, dense, dh, dm, dl, nh, nl, th, tl, sh, sl, tf, sf, pf,
    va, wa, c, sv, other, third, joint,
    u_src, u_dst, s_src, s_dst, k_src, k_dst, w_src, w_dst, far, above, below,
    g_src, g_dst, h_dst, e_src, e_dst,
    mine, theirs, red_x, red_y, red_z, rt,
    tile_sem, in_sem, out_sem, link_send, link_recv, pair_send, pair_recv,
    z_send, z_recv, x_send, x_recv, y_send, y_recv, k_send, k_recv,
):
    me, mz = lax.axis_index("rows"), lax.axis_index("rhs")
    pos, where = lax.rem(me, SPAN), lax.div(me, SPAN)
    chip, odd = lax.div(pos, 2), lax.rem(pos, 2) == 1
    even = jnp.logical_not(odd)
    chips = SPAN // 2
    ny = nr // SPAN
    first, last = pos == 0, pos == SPAN - 1
    cells = r.shape[1]

    def x_peer(o):
        return (where * SPAN + lax.rem(pos + o, SPAN), mz)

    def y_peer(o):
        return (lax.rem(where + o, ny) * SPAN + pos, mz)

    def z_peer(o):
        return (me, lax.rem(mz + o, nz))

    group, slots, bs = held.shape[0], held.shape[1], held.shape[2]
    fetch = [pltpu.make_async_copy(tiles.at[i], held.at[i], tile_sem.at[i]) for i in range(group)]
    whole = ((cols_in, cols), (pivots_in, pivots), (r_in, r))
    fetch += [pltpu.make_async_copy(src, dst, in_sem.at[i]) for i, (src, dst) in enumerate(whole)]
    for f in fetch[group:] + fetch[:group]:
        f.start()
    barrier = pltpu.get_barrier_semaphore()

    def hello(device):
        pl.semaphore_signal(barrier, inc=1, device_id=device, device_id_type=pl.DeviceIdType.MESH)

    for o in range(1, SPAN):
        hello(x_peer(o))
    for o in range(1, ny):
        hello(y_peer(o))
    for o in range(1, nz):
        hello(z_peer(o))
    has_before, has_next = me > 0, me < nr - 1
    from_before, to_next = first & has_before, last & has_next

    @pl.when(from_before)
    def _():
        hello((me - 1, mz))

    @pl.when(to_next)
    def _():
        hello((me + 1, mz))

    half = cells // 2

    def block(i, j):
        return (slice(i * bs, (i + 1) * bs), slice(j * bs, (j + 1) * bs))

    nothing = jnp.zeros((bs, bs), F32)
    for f in fetch[group:]:
        f.wait()
    for i in range(group):
        fetch[i].wait()
        away = [cols[i, k] - cols[i, 0] for k in range(1, slots)]
        for delta in range(-group, group + 1):
            tile = held[i, 0] if delta == 0 else None
            for k in range(1, slots):
                term = held[i, k] * (away[k - 1] == delta).astype(F32)
                tile = term if tile is None else tile + term
            j = i + delta
            if 0 <= j < group:
                dense[block(group + i, j)] = tile
            else:
                dense[block(group + j, i)] = tile.T
        for j in range(group):
            if j < i:
                dense[block(j, i)] = nothing
            if j > i:
                dense[block(2 * group + j, i)] = nothing

    def block_diagonal(first_row):
        zero = jnp.zeros((bs, bs), F32)
        count = half // bs
        return jnp.concatenate(
            [
                jnp.concatenate([pivots[first_row + i] if i == j else zero for j in range(count)], axis=1)
                for i in range(count)
            ],
            axis=0,
        )

    pa, pb = block_diagonal(0), block_diagonal(half // bs)
    row = lax.broadcasted_iota(jnp.int32, (half, half), 0)
    col = lax.broadcasted_iota(jnp.int32, (half, half), 1)
    same_pair = row // (2 * bs) == col // (2 * bs)
    eye = (row == col).astype(F32)
    lower = row // bs > col // bs

    def inverse(block):
        within = jnp.where(same_pair, block, 0.0)
        f = eye - within
        return f - mul(mul(f, block - within), f)

    o = cells
    ga = mul(jnp.where(lower, dense[o : o + half, 0:half], 0.0), pa)
    gb = mul(jnp.where(lower, dense[o + half : o + cells, half:cells], 0.0), pb)
    gx = mul(dense[o + half : o + cells, 0:half], pa)
    fa, fb = inverse(ga), inverse(gb)
    fx = -mul(mul(fb, gx), fa)
    pf[0:half, 0:half] = mul(pa, fa)
    pf[0:half, half:cells] = jnp.zeros((half, half), F32)
    pf[half:cells, 0:half] = mul(pb, fx)
    pf[half:cells, half:cells] = mul(pb, fb)
    n = mul(dense[2 * cells : 3 * cells], pf[...])
    nh[...], nl[...] = parts(n, 2)
    nt = n.T
    tf[...] = nt
    th[...], tl[...] = parts(nt, 2)

    edges = from_before.astype(jnp.int32) + to_next.astype(jnp.int32)
    pl.semaphore_wait(barrier, SPAN - 1 + ny - 1 + nz - 1 + edges)

    def copy(src, dst, send, recv, device):
        return pltpu.make_async_remote_copy(
            src_ref=src, dst_ref=dst, send_sem=send, recv_sem=recv,
            device_id=device, device_id_type=pl.DeviceIdType.MESH,
        )

    def link(kind, m, src, dst, device):
        return copy(src, dst.at[m], link_send.at[kind, m], link_recv.at[kind, m], (device, mz))

    def links(m):
        z = va.at[mz, m]
        return dict(
            u=link(0, m, u_src.at[m], u_dst, me + 1),
            s=link(1, m, s_src.at[m], s_dst, me - 1),
            k=link(2, m, k_src.at[m], k_dst, me + 2),
            w=link(3, m, w_src.at[m], w_dst, me + 1),
            far=link(4, m, z, far, me - 2),
            back=link(5, m, z, above, me - 1),
            on=link(6, m, z, below, me + 1),
            g=link(7, m, g_src.at[m], g_dst, me + 4),
            h=link(8, m, z, h_dst, me - 4),
            e=link(9, m, e_src.at[m], e_dst, me - 2),
        )

    def to_z(array, m, kind):
        return [
            copy(array.at[mz, m], array.at[mz, m], z_send.at[kind, o - 1], z_recv.at[kind, o - 1], z_peer(o))
            for o in range(1, nz)
        ]

    def spread(array, at, send, recv, peer, count):
        return [
            copy(array.at[at], array.at[at], send.at[o - 1], recv.at[o - 1], peer(o)) for o in range(1, count)
        ]

    begun = []

    def begin(copies):
        for s in copies:
            s.start()
        begun.extend(copies)

    def values(refs, rows=slice(None)):
        return [ref[rows] for ref in refs]

    n_refs, t_refs, s_refs = (nh, nl), (th, tl), (sh, sl)
    turn = chip == chips - 1
    ahead = chip < chips - 1
    pair_n = copy(tf, other, pair_send.at[0], pair_recv.at[0], (me - 1, mz))
    pair_s = copy(sf, other, pair_send.at[1], pair_recv.at[1], (me - 1, mz))

    @pl.when(odd & ahead)
    def _():
        pair_n.start()

    pair_k = [
        copy(other.at[part], third.at[part], pair_send.at[2 + i], pair_recv.at[2 + i], (me - 2, mz))
        for i, part in enumerate((slice(0, half), slice(half, cells)))
    ]
    at_once = links(0)

    @pl.when(first)
    def _():
        w_src[0] = times(r[...], values(t_refs))
        at_once["w"].start()

    @pl.when(pos == 1)
    def _():
        at_once["w"].wait_recv()
        c[...] = r[...] - w_dst[0]
        u_src[0] = times(c[...], values(t_refs))
        at_once["u"].start()

    def middle():
        low = mul(fb.T, pf[half:cells])
        sf[half:cells] = low
        sh[half:cells], sl[half:cells] = parts(low, 2)
        high = mul(fx.T, pf[half:cells])
        corner = mul(fa.T, pf[0:half, 0:half])
        high = jnp.concatenate([high[:, 0:half] + corner, high[:, half:cells]], axis=1)
        sf[0:half] = high
        sh[0:half], sl[0:half] = parts(high, 2)

    kt_refs, k_refs = (joint.at[0], joint.at[1]), (joint.at[2], joint.at[3])
    two_t, two = (joint.at[4], joint.at[5]), (joint.at[6], joint.at[7])

    @pl.when(even & ahead)
    def _():
        pair_n.wait_recv()
        kt = mul_parts(values(t_refs), parts(other[...], 2))
        for ref, p in zip(kt_refs, parts(kt, 2)):
            ref[...] = p
        other[...] = kt

    @pl.when(pos == 4)
    def _():
        pair_k[0].start()

    @pl.when(pos != 2)
    def _():
        middle()

    @pl.when(last)
    def _():
        pair_s.start()

    @pl.when(me == 0)
    def _():
        below[...] = jnp.zeros(below.shape, F32)

    @pl.when(me == nr - 1)
    def _():
        above[...] = jnp.zeros(above.shape, F32)


    def split_dense():
        for i in range(3):
            rows = slice(i * cells, (i + 1) * cells)
            for ref, p in zip((dh, dm, dl), parts(dense[rows], 3)):
                ref[rows] = p

    @pl.when(even & turn)
    def _():
        pair_s.wait_recv()
        x = mul_parts(parts(other[...], 2), values(n_refs))
        e = sf[...] + mul_parts(values(t_refs), parts(x, 2))
        for ref, p in zip(s_refs, parts(e, 2)):
            ref[...] = p

    def back_product():
        for ref, p in zip(k_refs, parts(other[...].T, 2)):
            ref[...] = p

    for m in range(2):
        source = r if m == 0 else wa.at[mz, 0]
        at = links(m)
        begins = 1 if m == 0 else 0

        @pl.when(odd & ahead & (chip >= begins))
        def _():
            u_src[m] = times(source[...], values(t_refs))
            at["u"].start()

        @pl.when(last)
        def _():
            s_src[m] = times(source[...], values(s_refs))
            at["s"].start()

        if m == 0:

            @pl.when((pos > 2))
            def _():
                split_dense()

        early = to_z(va, 0, 0) + to_z(wa, 0, 1) if m == 1 else []

        if m == 1:

            @pl.when(odd | (chip >= chips - 2))
            def _():
                for s in early:
                    s.start()

        @pl.when(odd & (chip >= begins))
        def _():
            at["w"].wait_recv()
            c[...] = source[...] - w_dst[m]

        @pl.when(odd & ahead)
        def _():
            s_src[m] = times(c[...], values(s_refs))
            at["s"].start()

        if m == 0:

            @pl.when(pos == 1)
            def _():
                split_dense()

        @pl.when(odd & ahead)
        def _():
            at["back"].wait_recv()
            va[mz, m] = s_src[m] - times(above[m], values(n_refs))

        @pl.when(last)
        def _():
            va[mz, m] = times(c[...], values(s_refs))

        @pl.when(first)
        def _():
            c[...] = source[...]

        def other_half():
            at["s"].wait_recv()
            sv[...] = times(s_dst[m], values(n_refs))

        @pl.when(even & turn)
        def _():
            other_half()

        @pl.when(even & (chip > 0))
        def _():
            at["u"].wait_recv()
            c[...] = source[...] - u_dst[m]

        direct = m == 1
        if direct:

            @pl.when(pos == 4)
            def _():
                k_src[m] = times(c[...], values(kt_refs))
                at["k"].start()

        @pl.when(even & (chip > begins))
        def _():
            at["k"].wait_recv()
            c[...] = c[...] + k_dst[m]

        if direct:

            @pl.when(pos == 6)
            def _():
                at["g"].wait_recv()
                c[...] = c[...] + g_dst[m]

            @pl.when(pos == 2)
            def _():
                g_src[m] = times(c[...], values(two_t))
                at["g"].start()

        @pl.when(even & ahead & (chip >= begins) & ((pos != 4) if direct else (pos >= 0)))
        def _():
            k_src[m] = times(c[...], values(kt_refs))
            at["k"].start()

        @pl.when(even & ahead & (chip >= begins))
        def _():
            w_src[m] = times(c[...], values(t_refs))
            at["w"].start()

        if m == 1:

            @pl.when(even & (chip < chips - 2))
            def _():
                for s in early:
                    s.start()

        begun.extend(early)
        if m == 0:

            @pl.when(pos == 2)
            def _():
                middle()

            @pl.when(even & ahead)
            def _():
                back_product()

            @pl.when(even & (pos <= 2))
            def _():
                split_dense()

        @pl.when(even & ahead)
        def _():
            other_half()
            c[...] = times(c[...], values(s_refs)) - sv[...]

        if direct:

            @pl.when(pos == 4)
            def _():
                e_src[m] = c[...]
                at["e"].start()

            @pl.when(pos == 2)
            def _():
                at["e"].wait_recv()
                c[...] = c[...] + times(e_dst[m], values(k_refs))
                at["h"].wait_recv()
                va[mz, m] = c[...] + times(h_dst[m], values(two))

        @pl.when(even & ahead & ((pos != 2) if direct else (pos >= 0)))
        def _():
            at["far"].wait_recv()
            va[mz, m] = c[...] + times(far[m], values(k_refs))

        @pl.when(even & turn)
        def _():
            va[mz, m] = times(c[...], values(s_refs)) - sv[...]

        if direct:

            @pl.when(pos == 6)
            def _():
                at["h"].start()

        @pl.when(even & (chip > 0) & ((pos != 4) if direct else (pos >= 0)))
        def _():
            at["far"].start()

        @pl.when(even & turn)
        def _():
            w_src[m] = times(c[...], values(t_refs))
            at["w"].start()

        @pl.when(has_before)
        def _():
            at["back"].start()

        @pl.when(has_next)
        def _():
            at["on"].start()

        if m == 1:
            begin(to_z(va, 1, 2))

        if m == 0:

            @pl.when(pos == 4)
            def _():
                pair_k[1].start()

        d = (dh, dm, dl)

        def part(value, i):
            return times(value, values(d, slice(i * cells, (i + 1) * cells)))

        c[...] = part(va[mz, m], 1)

        @pl.when(from_before)
        def _():
            at["on"].wait_recv()

        @pl.when(first)
        def _():
            wa[mz, m] = part(below[m], 0)

        @pl.when(jnp.logical_not(odd) )
        def _():
            at["back"].wait_recv()

        @pl.when(jnp.logical_not(last))
        def _():
            sv[...] = part(above[m], 2)

        if m == 1:
            @pl.when(first)
            def _():
                far[0] = 0.5 * c[...] + sv[...] + wa[mz, m]

            @pl.when(jnp.logical_not(first | last))
            def _():
                far[0] = 0.5 * c[...] + sv[...]

            @pl.when(last)
            def _():
                far[0] = 0.5 * c[...]

            for kind in range(2):
                for s in to_z(va, kind, 2 * kind):
                    s.wait_recv()
            left = jnp.concatenate([wa[mz, 0], far[0], r[...]], axis=0)
            right = va[...].reshape(nz * 16, cells)
            mine[...] = lax.dot_general(
                left, right, (((1,), (1,)), ((), ())),
                precision=lax.Precision.HIGHEST, preferred_element_type=F32,
            )
            to_odd = copy(mine, theirs, pair_send.at[4], pair_recv.at[4], (me + 1, mz))
            over_x = [
                copy(red_x.at[chip], red_x.at[chip], x_send.at[o - 1], x_recv.at[o - 1], x_peer(2 * o))
                for o in range(1, chips)
            ]

            @pl.when(even)
            def _():
                to_odd.start()

            @pl.when(odd)
            def _():
                to_odd.wait_recv()
                red_x[chip] = theirs[...] + mine[...]
                for s in over_x:
                    s.start()

        @pl.when(to_next)
        def _():
            at["back"].wait_recv()

        @pl.when(last)
        def _():
            sv[...] = part(above[m], 2)

        @pl.when(has_before & jnp.logical_not(first))
        def _():
            at["on"].wait_recv()

        @pl.when(jnp.logical_not(first))
        def _():
            wa[mz, m] = part(below[m], 0)

        wa[mz, m] = c[...] + sv[...] + wa[mz, m]
        if m == 1:
            begin(to_z(wa, 1, 3))

        else:

            @pl.when(pos == 2)
            def _():
                for p in pair_k:
                    p.wait_recv()
                t = mul_parts(values(kt_refs), parts(third[...], 2))
                for ref, p in zip(two_t, parts(t, 2)):
                    ref[...] = p
                for ref, p in zip(two, parts(t.T, 2)):
                    ref[...] = p


    def total(array, count):
        value = array[0]
        for i in range(1, count):
            value = value + array[i]
        return value

    before = list(begun)
    over_y = spread(red_y, where, y_send, y_recv, y_peer, ny)
    over_z = spread(red_z, mz, k_send, k_recv, z_peer, nz)
    to_even = [
        copy(ref, ref, pair_send.at[5 + i], pair_recv.at[5 + i], (me - 1, mz)) for i, ref in enumerate((red_z, rt))
    ]

    @pl.when(odd)
    def _():
        for s in over_x:
            s.wait_recv()
        red_y[where] = total(red_x, chips)
        for s in over_y:
            s.start()
        for s in over_y:
            s.wait_recv()
        both = total(red_y, ny)
        red_z[mz] = both[0:16]
        for s in over_z:
            s.start()
        rt[...] = both[16:24]
        to_even[1].start()

    results = [
        pltpu.make_async_copy(src, dst, out_sem.at[i])
        for i, (src, dst) in enumerate(((red_z, k_out), (rt, r_out), (va, v_out), (wa, w_out)))
    ]
    results[2].start()
    for m in range(2):
        for s in to_z(wa, m, 2 * m + 1):
            s.wait_recv()
    results[3].start()
    for s in before:
        s.wait_send()

    @pl.when(odd & ahead)
    def _():
        pair_n.wait_send()

    @pl.when(last)
    def _():
        pair_s.wait_send()

    @pl.when(pos == 4)
    def _():
        for p in pair_k:
            p.wait_send()

    for m in range(2):
        at = links(m)
        for name, started in (
            ("u", odd & ahead),
            ("s", odd),
            ("k", even & ahead & (chip >= (1 if m == 0 else 0))),
            ("w", even),
            ("far", even & (chip > 0) & ((pos != 4) if m == 1 else (pos >= 0))),
            ("g", (pos == 2) & (m == 1)),
            ("h", (pos == 6) & (m == 1)),
            ("e", (pos == 4) & (m == 1)),
            ("back", has_before),
            ("on", has_next),
        ):

            @pl.when(started)
            def _():
                at[name].wait_send()

    @pl.when(odd)
    def _():
        for s in over_z:
            s.wait_recv()
        to_even[0].start()

    @pl.when(even)
    def _():
        for s in to_even:
            s.wait_recv()

    results[0].start()
    results[1].start()

    @pl.when(odd)
    def _():
        for s in over_x + over_y + over_z + to_even:
            s.wait_send()

    @pl.when(even)
    def _():
        to_odd.wait_send()

    for f in results:
        f.wait()


def krylov(nr, nz, cols, tiles, r, pivots):
    rhs, cells = r.shape
    ny = nr // SPAN
    dma = pltpu.SemaphoreType.DMA
    every = nz * 2 * rhs
    vector = pltpu.VMEM((rhs, cells), F32)
    square, square_half = pltpu.VMEM((cells, cells), F32), pltpu.VMEM((cells, cells), BF)
    vectors = pltpu.VMEM((2, rhs, cells), F32)
    return pl.pallas_call(
        functools.partial(krylov_kernel, nr, nz),
        out_shape=[
            jax.ShapeDtypeStruct((nz, 2, rhs, cells), F32),
            jax.ShapeDtypeStruct((nz, 2, rhs, cells), F32),
            jax.ShapeDtypeStruct((nz, 2 * rhs, every), F32),
            jax.ShapeDtypeStruct((rhs, every), F32),
        ],
        in_specs=[pl.BlockSpec(memory_space=pltpu.HBM)] * 4,
        out_specs=[pl.BlockSpec(memory_space=pltpu.HBM)] * 4,
        scratch_shapes=[pltpu.SMEM(cols.shape, jnp.int32), vector, pltpu.VMEM(pivots.shape, F32)]
        + [pltpu.VMEM(tiles.shape, F32), pltpu.VMEM((3 * cells, cells), F32)]
        + [pltpu.VMEM((3 * cells, cells), BF)] * 3
        + [square_half] * 6
        + [square] * 3
        + [pltpu.VMEM((nz, 2, rhs, cells), F32)] * 2
        + [vector] * 2
        + [square, square, pltpu.VMEM((8, cells, cells), BF)]
        + [vectors] * 16
        + [
            pltpu.VMEM((3 * rhs, every), F32),
            pltpu.VMEM((3 * rhs, every), F32),
            pltpu.VMEM((SPAN // 2, 3 * rhs, every), F32),
            pltpu.VMEM((ny, 3 * rhs, every), F32),
            pltpu.VMEM((nz, 2 * rhs, every), F32),
            pltpu.VMEM((rhs, every), F32),
        ]
        + [dma((tiles.shape[0],)), dma((3,)), dma((4,))]
        + [dma((10, 2))] * 2
        + [dma((7,))] * 2
        + [dma((4, max(nz - 1, 1)))] * 2
        + [dma((SPAN - 1,))] * 2
        + [dma((max(ny - 1, 1),))] * 2
        + [dma((max(nz - 1, 1),))] * 2,
        compiler_params=pltpu.CompilerParams(
            collective_id=0, has_side_effects=True, vmem_limit_bytes=60 * MIB
        ),
    )(cols, tiles, r, pivots)


def spd_inverse(k, block):
    size = k.shape[0]
    row_of = lax.broadcasted_iota(jnp.int32, (size, 1), 0)
    col_of = lax.broadcasted_iota(jnp.int32, (1, size), 1)
    span = range(block)
    for b in range(0, size, block):
        d = [[jnp.broadcast_to(k[b + i : b + i + 1, b + j : b + j + 1], (1, size)) for j in span] for i in span]
        for p in span:
            inv = 1.0 / d[p][p]
            row = [inv if j == p else d[p][j] * inv for j in span]
            for i in span:
                if i != p:
                    f = d[i][p]
                    d[i] = [-f * row[p] if j == p else d[i][j] - f * row[j] for j in span]
            d[p] = row
        in_cols = (col_of >= b) & (col_of < b + block)
        in_rows = (row_of >= b) & (row_of < b + block)
        base = jnp.where(in_rows | in_cols, 0.0, k)
        for i in span:
            row, corner = d[i][0] * k[b : b + 1, :], d[i][0]
            for j in range(1, block):
                row = row + d[i][j] * k[b + j : b + j + 1, :]
                corner = jnp.where(col_of == b + j, d[i][j], corner)
            row = jnp.where(in_cols, corner, row)
            col = jnp.where(in_rows, jnp.where(row_of == b + i, -1.0, 0.0), k[:, b + i : b + i + 1])
            base = base - col * row
        k = base
    return k


def solve_kernel(k_in, rt_in, v_in, w_in, r_in, x_out, r_out, k_buf, rt, v, w, r, sems):
    whole = ((k_in, k_buf), (rt_in, rt), (v_in, v), (w_in, w), (r_in, r))
    fetch = [pltpu.make_async_copy(src, dst, sems.at[i]) for i, (src, dst) in enumerate(whole)]
    for f in fetch:
        f.start()
    fetch[0].wait()
    size, cells = rt.shape[1], r.shape[1]
    k = k_buf[...].reshape(size, size)
    kt = k.T
    row_of = lax.broadcasted_iota(jnp.int32, (size, 1), 0)
    col_of = lax.broadcasted_iota(jnp.int32, (1, size), 1)
    row_p, col_p = lax.rem(row_of // 8, 2) == 1, lax.rem(col_of // 8, 2) == 1
    both = k + kt
    k = jnp.where(row_p, jnp.where(col_p, both, kt), jnp.where(col_p, k, 0.5 * both))
    high = lax.Precision.HIGHEST
    inverse = spd_inverse(k, 4)
    for f in fetch[1:]:
        f.wait()
    c = jnp.dot(rt[...], inverse, precision=high, preferred_element_type=F32)
    x_out[...] = jnp.dot(c, v[...].reshape(size, cells), precision=high, preferred_element_type=F32)
    r_out[...] = r[...] - jnp.dot(c, w[...].reshape(size, cells), precision=high, preferred_element_type=F32)


def solve(k, rt, v, w, r):
    operands = (k, rt, v, w, r)
    return pl.pallas_call(
        solve_kernel,
        out_shape=[jax.ShapeDtypeStruct(r.shape, F32)] * 2,
        in_specs=[pl.BlockSpec(memory_space=pltpu.HBM)] * 5,
        out_specs=[VMEM] * 2,
        scratch_shapes=[pltpu.VMEM(o.shape, F32) for o in operands] + [pltpu.SemaphoreType.DMA((5,))],
        compiler_params=pltpu.CompilerParams(vmem_limit_bytes=60 * MIB),
    )(*operands)


def solution(mesh):
    nr, nz = mesh.shape["rows"], mesh.shape["rhs"]

    def shards(right_side, tiles, pivots, columns):
        v, w, k, rt = krylov(nr, nz, columns, tiles, right_side, pivots)
        return tuple(solve(k, rt, v, w, right_side))

    return jax.shard_map(
        shards,
        mesh=mesh,
        in_specs=(
            P("rhs", "rows"),
            P("rows", None, None, None),
            P("rows", None, None),
            P("rows", None),
        ),
        out_specs=(P("rhs", "rows"), P("rhs", "rows")),
        check_vma=False,
    )
```

```python
import functools

import jax
import jax.numpy as jnp
from jax import lax
from jax.experimental import pallas as pl
from jax.experimental.pallas import tpu as pltpu
from jax.sharding import PartitionSpec as P

SPAN = 8
BF, F32 = jnp.bfloat16, jnp.float32
MIB = 1 << 20
VMEM = pl.BlockSpec(memory_space=pltpu.VMEM)
SMEM = pl.BlockSpec(memory_space=pltpu.SMEM)


def parts(x, n):
    out = []
    for _ in range(n):
        high = x.astype(BF)
        out.append(high)
        x = x - high.astype(F32)
    return out


def dot(a, b):
    return jnp.dot(a, b, preferred_element_type=F32)


def mul(a, b):
    (ah, al), (bh, bl) = parts(a, 2), parts(b, 2)
    return dot(ah, bh) + (dot(ah, bl) + dot(al, bh))


def times(x, weights):
    n = x.shape[0]
    count = len(weights)
    stack = jnp.concatenate([p.astype(F32) for p in parts(x, count)], axis=0)
    if count * n % 16:
        stack = jnp.concatenate([stack, jnp.zeros((16 - count * n % 16, x.shape[1]), F32)], axis=0)
    stack = stack.astype(BF)
    total = None
    for w in reversed(weights):
        y = dot(stack, w)
        for i in reversed(range(count)):
            y_i = y[i * n : (i + 1) * n]
            total = y_i if total is None else total + y_i
    return total


def mul_parts(a, b):
    (ah, al), (bh, bl) = a, b
    return dot(ah, bh) + (dot(ah, bl) + dot(al, bh))


def krylov_kernel(
    nr, nz,
    cols_in, tiles, r_in, pivots_in,
    v_out, w_out, k_out, r_out,
    cols, r, pivots, held, dense, dh, dm, dl, nh, nl, th, tl, sh, sl, tf, sf, pf,
    va, wa, c, sv, other, third, joint,
    u_src, u_dst, s_src, s_dst, k_src, k_dst, w_src, w_dst, far, above, below,
    g_src, g_dst, h_dst, e_src, e_dst,
    mine, theirs, red_x, red_y, red_z, rt,
    tile_sem, in_sem, out_sem, link_send, link_recv, pair_send, pair_recv,
    z_send, z_recv, x_send, x_recv, y_send, y_recv, k_send, k_recv,
):
    me, mz = lax.axis_index("rows"), lax.axis_index("rhs")
    pos, where = lax.rem(me, SPAN), lax.div(me, SPAN)
    chip, odd = lax.div(pos, 2), lax.rem(pos, 2) == 1
    even = jnp.logical_not(odd)
    chips = SPAN // 2
    ny = nr // SPAN
    first, last = pos == 0, pos == SPAN - 1
    cells = r.shape[1]

    def x_peer(o):
        return (where * SPAN + lax.rem(pos + o, SPAN), mz)

    def y_peer(o):
        return (lax.rem(where + o, ny) * SPAN + pos, mz)

    def z_peer(o):
        return (me, lax.rem(mz + o, nz))

    group, slots, bs = held.shape[0], held.shape[1], held.shape[2]
    fetch = [pltpu.make_async_copy(tiles.at[i], held.at[i], tile_sem.at[i]) for i in range(group)]
    whole = ((cols_in, cols), (pivots_in, pivots), (r_in, r))
    fetch += [pltpu.make_async_copy(src, dst, in_sem.at[i]) for i, (src, dst) in enumerate(whole)]
    for f in fetch[group:] + fetch[:group]:
        f.start()
    barrier = pltpu.get_barrier_semaphore()

    def hello(device):
        pl.semaphore_signal(barrier, inc=1, device_id=device, device_id_type=pl.DeviceIdType.MESH)

    for o in range(1, SPAN):
        hello(x_peer(o))
    for o in range(1, ny):
        hello(y_peer(o))
    for o in range(1, nz):
        hello(z_peer(o))
    has_before, has_next = me > 0, me < nr - 1
    from_before, to_next = first & has_before, last & has_next

    @pl.when(from_before)
    def _():
        hello((me - 1, mz))

    @pl.when(to_next)
    def _():
        hello((me + 1, mz))

    half = cells // 2

    def block(i, j):
        return (slice(i * bs, (i + 1) * bs), slice(j * bs, (j + 1) * bs))

    nothing = jnp.zeros((bs, bs), F32)
    for f in fetch[group:]:
        f.wait()
    for i in range(group):
        fetch[i].wait()
        away = [cols[i, k] - cols[i, 0] for k in range(1, slots)]
        for delta in range(-group, group + 1):
            tile = held[i, 0] if delta == 0 else None
            for k in range(1, slots):
                term = held[i, k] * (away[k - 1] == delta).astype(F32)
                tile = term if tile is None else tile + term
            j = i + delta
            if 0 <= j < group:
                dense[block(group + i, j)] = tile
            else:
                dense[block(group + j, i)] = tile.T
        for j in range(group):
            if j < i:
                dense[block(j, i)] = nothing
            if j > i:
                dense[block(2 * group + j, i)] = nothing

    def block_diagonal(first_row):
        zero = jnp.zeros((bs, bs), F32)
        count = half // bs
        return jnp.concatenate(
            [
                jnp.concatenate([pivots[first_row + i] if i == j else zero for j in range(count)], axis=1)
                for i in range(count)
            ],
            axis=0,
        )

    pa, pb = block_diagonal(0), block_diagonal(half // bs)
    row = lax.broadcasted_iota(jnp.int32, (half, half), 0)
    col = lax.broadcasted_iota(jnp.int32, (half, half), 1)
    same_pair = row // (2 * bs) == col // (2 * bs)
    eye = (row == col).astype(F32)
    lower = row // bs > col // bs

    def inverse(block):
        within = jnp.where(same_pair, block, 0.0)
        f = eye - within
        return f - mul(mul(f, block - within), f)

    o = cells
    ga = mul(jnp.where(lower, dense[o : o + half, 0:half], 0.0), pa)
    gb = mul(jnp.where(lower, dense[o + half : o + cells, half:cells], 0.0), pb)
    gx = mul(dense[o + half : o + cells, 0:half], pa)
    fa, fb = inverse(ga), inverse(gb)
    fx = -mul(mul(fb, gx), fa)
    pf[0:half, 0:half] = mul(pa, fa)
    pf[0:half, half:cells] = jnp.zeros((half, half), F32)
    pf[half:cells, 0:half] = mul(pb, fx)
    pf[half:cells, half:cells] = mul(pb, fb)
    n = mul(dense[2 * cells : 3 * cells], pf[...])
    nh[...], nl[...] = parts(n, 2)
    nt = n.T
    tf[...] = nt
    th[...], tl[...] = parts(nt, 2)

    edges = from_before.astype(jnp.int32) + to_next.astype(jnp.int32)
    pl.semaphore_wait(barrier, SPAN - 1 + ny - 1 + nz - 1 + edges)

    def copy(src, dst, send, recv, device):
        return pltpu.make_async_remote_copy(
            src_ref=src, dst_ref=dst, send_sem=send, recv_sem=recv,
            device_id=device, device_id_type=pl.DeviceIdType.MESH,
        )

    def link(kind, m, src, dst, device):
        return copy(src, dst.at[m], link_send.at[kind, m], link_recv.at[kind, m], (device, mz))

    def links(m):
        z = va.at[mz, m]
        return dict(
            u=link(0, m, u_src.at[m], u_dst, me + 1),
            s=link(1, m, s_src.at[m], s_dst, me - 1),
            k=link(2, m, k_src.at[m], k_dst, me + 2),
            w=link(3, m, w_src.at[m], w_dst, me + 1),
            far=link(4, m, z, far, me - 2),
            back=link(5, m, z, above, me - 1),
            on=link(6, m, z, below, me + 1),
            g=link(7, m, g_src.at[m], g_dst, me + 4),
            h=link(8, m, z, h_dst, me - 4),
            e=link(9, m, e_src.at[m], e_dst, me - 2),
        )

    def to_z(array, m, kind):
        return [
            copy(array.at[mz, m], array.at[mz, m], z_send.at[kind, o - 1], z_recv.at[kind, o - 1], z_peer(o))
            for o in range(1, nz)
        ]

    def spread(array, at, send, recv, peer, count):
        return [
            copy(array.at[at], array.at[at], send.at[o - 1], recv.at[o - 1], peer(o)) for o in range(1, count)
        ]

    begun = []

    def begin(copies):
        for s in copies:
            s.start()
        begun.extend(copies)

    def values(refs, rows=slice(None)):
        return [ref[rows] for ref in refs]

    n_refs, t_refs, s_refs = (nh, nl), (th, tl), (sh, sl)
    turn = chip == chips - 1
    ahead = chip < chips - 1
    pair_n = copy(tf, other, pair_send.at[0], pair_recv.at[0], (me - 1, mz))
    pair_s = copy(sf, other, pair_send.at[1], pair_recv.at[1], (me - 1, mz))

    @pl.when(odd & ahead)
    def _():
        pair_n.start()

    pair_k = [
        copy(other.at[part], third.at[part], pair_send.at[2 + i], pair_recv.at[2 + i], (me - 2, mz))
        for i, part in enumerate((slice(0, half), slice(half, cells)))
    ]
    at_once = links(0)

    @pl.when(first)
    def _():
        w_src[0] = times(r[...], values(t_refs))
        at_once["w"].start()

    @pl.when(pos == 1)
    def _():
        at_once["w"].wait_recv()
        c[...] = r[...] - w_dst[0]
        u_src[0] = times(c[...], values(t_refs))
        at_once["u"].start()

    def middle():
        low = mul(fb.T, pf[half:cells])
        sf[half:cells] = low
        sh[half:cells], sl[half:cells] = parts(low, 2)
        high = mul(fx.T, pf[half:cells])
        corner = mul(fa.T, pf[0:half, 0:half])
        high = jnp.concatenate([high[:, 0:half] + corner, high[:, half:cells]], axis=1)
        sf[0:half] = high
        sh[0:half], sl[0:half] = parts(high, 2)

    kt_refs, k_refs = (joint.at[0], joint.at[1]), (joint.at[2], joint.at[3])
    two_t, two = (joint.at[4], joint.at[5]), (joint.at[6], joint.at[7])

    @pl.when(even & ahead)
    def _():
        pair_n.wait_recv()
        kt = mul_parts(values(t_refs), parts(other[...], 2))
        for ref, p in zip(kt_refs, parts(kt, 2)):
            ref[...] = p
        other[...] = kt

    @pl.when(pos == 4)
    def _():
        pair_k[0].start()

    @pl.when(pos != 2)
    def _():
        middle()

    @pl.when(last)
    def _():
        pair_s.start()

    @pl.when(me == 0)
    def _():
        below[...] = jnp.zeros(below.shape, F32)

    @pl.when(me == nr - 1)
    def _():
        above[...] = jnp.zeros(above.shape, F32)


    def split_dense():
        for i in range(3):
            rows = slice(i * cells, (i + 1) * cells)
            for ref, p in zip((dh, dm, dl), parts(dense[rows], 3)):
                ref[rows] = p

    @pl.when(even & turn)
    def _():
        pair_s.wait_recv()
        x = mul_parts(parts(other[...], 2), values(n_refs))
        e = sf[...] + mul_parts(values(t_refs), parts(x, 2))
        for ref, p in zip(s_refs, parts(e, 2)):
            ref[...] = p

    def back_product():
        for ref, p in zip(k_refs, parts(other[...].T, 2)):
            ref[...] = p

    for m in range(2):
        source = r if m == 0 else wa.at[mz, 0]
        at = links(m)
        begins = 1 if m == 0 else 0

        @pl.when(odd & ahead & (chip >= begins))
        def _():
            u_src[m] = times(source[...], values(t_refs))
            at["u"].start()

        @pl.when(last)
        def _():
            s_src[m] = times(source[...], values(s_refs))
            at["s"].start()

        if m == 0:

            @pl.when((pos > 2))
            def _():
                split_dense()

        early = to_z(va, 0, 0) + to_z(wa, 0, 1) if m == 1 else []

        if m == 1:

            @pl.when(odd | (chip >= chips - 2))
            def _():
                for s in early:
                    s.start()

        @pl.when(odd & (chip >= begins))
        def _():
            at["w"].wait_recv()
            c[...] = source[...] - w_dst[m]

        @pl.when(odd & ahead)
        def _():
            s_src[m] = times(c[...], values(s_refs))
            at["s"].start()

        if m == 0:

            @pl.when(pos == 1)
            def _():
                split_dense()

        @pl.when(odd & ahead)
        def _():
            at["back"].wait_recv()
            va[mz, m] = s_src[m] - times(above[m], values(n_refs))

        @pl.when(last)
        def _():
            va[mz, m] = times(c[...], values(s_refs))

        @pl.when(first)
        def _():
            c[...] = source[...]

        def other_half():
            at["s"].wait_recv()
            sv[...] = times(s_dst[m], values(n_refs))

        @pl.when(even & turn)
        def _():
            other_half()

        @pl.when(even & (chip > 0))
        def _():
            at["u"].wait_recv()
            c[...] = source[...] - u_dst[m]

        direct = m == 1
        if direct:

            @pl.when(pos == 4)
            def _():
                k_src[m] = times(c[...], values(kt_refs))
                at["k"].start()

        @pl.when(even & (chip > begins))
        def _():
            at["k"].wait_recv()
            c[...] = c[...] + k_dst[m]

        if direct:

            @pl.when(pos == 6)
            def _():
                at["g"].wait_recv()
                c[...] = c[...] + g_dst[m]

            @pl.when(pos == 2)
            def _():
                g_src[m] = times(c[...], values(two_t))
                at["g"].start()

        @pl.when(even & ahead & (chip >= begins) & ((pos != 4) if direct else (pos >= 0)))
        def _():
            k_src[m] = times(c[...], values(kt_refs))
            at["k"].start()

        @pl.when(even & ahead & (chip >= begins))
        def _():
            w_src[m] = times(c[...], values(t_refs))
            at["w"].start()

        if m == 1:

            @pl.when(even & (chip < chips - 2))
            def _():
                for s in early:
                    s.start()

        begun.extend(early)
        if m == 0:

            @pl.when(pos == 2)
            def _():
                middle()

            @pl.when(even & ahead)
            def _():
                back_product()

            @pl.when(even & (pos <= 2))
            def _():
                split_dense()

        @pl.when(even & ahead)
        def _():
            other_half()
            c[...] = times(c[...], values(s_refs)) - sv[...]

        if direct:

            @pl.when(pos == 4)
            def _():
                e_src[m] = c[...]
                at["e"].start()

            @pl.when(pos == 2)
            def _():
                at["e"].wait_recv()
                c[...] = c[...] + times(e_dst[m], values(k_refs))
                at["h"].wait_recv()
                va[mz, m] = c[...] + times(h_dst[m], values(two))

        @pl.when(even & ahead & ((pos != 2) if direct else (pos >= 0)))
        def _():
            at["far"].wait_recv()
            va[mz, m] = c[...] + times(far[m], values(k_refs))

        @pl.when(even & turn)
        def _():
            va[mz, m] = times(c[...], values(s_refs)) - sv[...]

        if direct:

            @pl.when(pos == 6)
            def _():
                at["h"].start()

        @pl.when(even & (chip > 0) & ((pos != 4) if direct else (pos >= 0)))
        def _():
            at["far"].start()

        @pl.when(even & turn)
        def _():
            w_src[m] = times(c[...], values(t_refs))
            at["w"].start()

        if m == 1:
            begin(to_z(va, 1, 2))

        @pl.when(has_before)
        def _():
            at["back"].start()

        @pl.when(has_next)
        def _():
            at["on"].start()


        if m == 0:

            @pl.when(pos == 4)
            def _():
                pair_k[1].start()

        d = (dh, dm, dl)

        def part(value, i):
            return times(value, values(d, slice(i * cells, (i + 1) * cells)))

        c[...] = part(va[mz, m], 1)

        @pl.when(from_before)
        def _():
            at["on"].wait_recv()

        @pl.when(first)
        def _():
            wa[mz, m] = part(below[m], 0)

        @pl.when(jnp.logical_not(odd) )
        def _():
            at["back"].wait_recv()

        @pl.when(jnp.logical_not(last))
        def _():
            sv[...] = part(above[m], 2)

        if m == 1:
            @pl.when(first)
            def _():
                far[0] = 0.5 * c[...] + sv[...] + wa[mz, m]

            @pl.when(jnp.logical_not(first | last))
            def _():
                far[0] = 0.5 * c[...] + sv[...]

            @pl.when(last)
            def _():
                far[0] = 0.5 * c[...]

            for kind in range(2):
                for s in to_z(va, kind, 2 * kind):
                    s.wait_recv()
            left = jnp.concatenate([wa[mz, 0], far[0], r[...]], axis=0)
            right = va[...].reshape(nz * 16, cells)
            mine[...] = lax.dot_general(
                left, right, (((1,), (1,)), ((), ())),
                precision=lax.Precision.HIGHEST, preferred_element_type=F32,
            )
            to_odd = copy(mine, theirs, pair_send.at[4], pair_recv.at[4], (me + 1, mz))
            over_x = [
                copy(red_x.at[chip], red_x.at[chip], x_send.at[o - 1], x_recv.at[o - 1], x_peer(2 * o))
                for o in range(1, chips)
            ]

            @pl.when(even)
            def _():
                to_odd.start()

            @pl.when(odd)
            def _():
                to_odd.wait_recv()
                red_x[chip] = theirs[...] + mine[...]
                for s in over_x:
                    s.start()

        @pl.when(to_next)
        def _():
            at["back"].wait_recv()

        @pl.when(last)
        def _():
            sv[...] = part(above[m], 2)

        @pl.when(has_before & jnp.logical_not(first))
        def _():
            at["on"].wait_recv()

        @pl.when(jnp.logical_not(first))
        def _():
            wa[mz, m] = part(below[m], 0)

        wa[mz, m] = c[...] + sv[...] + wa[mz, m]
        if m == 1:
            begin(to_z(wa, 1, 3))

        else:

            @pl.when(pos == 2)
            def _():
                for p in pair_k:
                    p.wait_recv()
                t = mul_parts(values(kt_refs), parts(third[...], 2))
                for ref, p in zip(two_t, parts(t, 2)):
                    ref[...] = p
                for ref, p in zip(two, parts(t.T, 2)):
                    ref[...] = p


    def total(array, count):
        value = array[0]
        for i in range(1, count):
            value = value + array[i]
        return value

    before = list(begun)
    over_y = spread(red_y, where, y_send, y_recv, y_peer, ny)
    over_z = spread(red_z, mz, k_send, k_recv, z_peer, nz)
    to_even = [
        copy(ref, ref, pair_send.at[5 + i], pair_recv.at[5 + i], (me - 1, mz)) for i, ref in enumerate((red_z, rt))
    ]

    @pl.when(odd)
    def _():
        for s in over_x:
            s.wait_recv()
        red_y[where] = total(red_x, chips)
        for s in over_y:
            s.start()
        for s in over_y:
            s.wait_recv()
        both = total(red_y, ny)
        red_z[mz] = both[0:16]
        for s in over_z:
            s.start()
        rt[...] = both[16:24]
        to_even[1].start()

    results = [
        pltpu.make_async_copy(src, dst, out_sem.at[i])
        for i, (src, dst) in enumerate(((red_z, k_out), (rt, r_out), (va, v_out), (wa, w_out)))
    ]
    results[2].start()
    for m in range(2):
        for s in to_z(wa, m, 2 * m + 1):
            s.wait_recv()
    results[3].start()
    for s in before:
        s.wait_send()

    @pl.when(odd & ahead)
    def _():
        pair_n.wait_send()

    @pl.when(last)
    def _():
        pair_s.wait_send()

    @pl.when(pos == 4)
    def _():
        for p in pair_k:
            p.wait_send()

    for m in range(2):
        at = links(m)
        for name, started in (
            ("u", odd & ahead),
            ("s", odd),
            ("k", even & ahead & (chip >= (1 if m == 0 else 0))),
            ("w", even),
            ("far", even & (chip > 0) & ((pos != 4) if m == 1 else (pos >= 0))),
            ("g", (pos == 2) & (m == 1)),
            ("h", (pos == 6) & (m == 1)),
            ("e", (pos == 4) & (m == 1)),
            ("back", has_before),
            ("on", has_next),
        ):

            @pl.when(started)
            def _():
                at[name].wait_send()

    @pl.when(odd)
    def _():
        for s in over_z:
            s.wait_recv()
        to_even[0].start()

    @pl.when(even)
    def _():
        for s in to_even:
            s.wait_recv()

    results[0].start()
    results[1].start()

    @pl.when(odd)
    def _():
        for s in over_x + over_y + over_z + to_even:
            s.wait_send()

    @pl.when(even)
    def _():
        to_odd.wait_send()

    for f in results:
        f.wait()


def krylov(nr, nz, cols, tiles, r, pivots):
    rhs, cells = r.shape
    ny = nr // SPAN
    dma = pltpu.SemaphoreType.DMA
    every = nz * 2 * rhs
    vector = pltpu.VMEM((rhs, cells), F32)
    square, square_half = pltpu.VMEM((cells, cells), F32), pltpu.VMEM((cells, cells), BF)
    vectors = pltpu.VMEM((2, rhs, cells), F32)
    return pl.pallas_call(
        functools.partial(krylov_kernel, nr, nz),
        out_shape=[
            jax.ShapeDtypeStruct((nz, 2, rhs, cells), F32),
            jax.ShapeDtypeStruct((nz, 2, rhs, cells), F32),
            jax.ShapeDtypeStruct((nz, 2 * rhs, every), F32),
            jax.ShapeDtypeStruct((rhs, every), F32),
        ],
        in_specs=[pl.BlockSpec(memory_space=pltpu.HBM)] * 4,
        out_specs=[pl.BlockSpec(memory_space=pltpu.HBM)] * 4,
        scratch_shapes=[pltpu.SMEM(cols.shape, jnp.int32), vector, pltpu.VMEM(pivots.shape, F32)]
        + [pltpu.VMEM(tiles.shape, F32), pltpu.VMEM((3 * cells, cells), F32)]
        + [pltpu.VMEM((3 * cells, cells), BF)] * 3
        + [square_half] * 6
        + [square] * 3
        + [pltpu.VMEM((nz, 2, rhs, cells), F32)] * 2
        + [vector] * 2
        + [square, square, pltpu.VMEM((8, cells, cells), BF)]
        + [vectors] * 16
        + [
            pltpu.VMEM((3 * rhs, every), F32),
            pltpu.VMEM((3 * rhs, every), F32),
            pltpu.VMEM((SPAN // 2, 3 * rhs, every), F32),
            pltpu.VMEM((ny, 3 * rhs, every), F32),
            pltpu.VMEM((nz, 2 * rhs, every), F32),
            pltpu.VMEM((rhs, every), F32),
        ]
        + [dma((tiles.shape[0],)), dma((3,)), dma((4,))]
        + [dma((10, 2))] * 2
        + [dma((7,))] * 2
        + [dma((4, max(nz - 1, 1)))] * 2
        + [dma((SPAN - 1,))] * 2
        + [dma((max(ny - 1, 1),))] * 2
        + [dma((max(nz - 1, 1),))] * 2,
        compiler_params=pltpu.CompilerParams(
            collective_id=0, has_side_effects=True, vmem_limit_bytes=60 * MIB
        ),
    )(cols, tiles, r, pivots)


def spd_inverse(k, block):
    size = k.shape[0]
    row_of = lax.broadcasted_iota(jnp.int32, (size, 1), 0)
    col_of = lax.broadcasted_iota(jnp.int32, (1, size), 1)
    span = range(block)
    for b in range(0, size, block):
        d = [[jnp.broadcast_to(k[b + i : b + i + 1, b + j : b + j + 1], (1, size)) for j in span] for i in span]
        for p in span:
            inv = 1.0 / d[p][p]
            row = [inv if j == p else d[p][j] * inv for j in span]
            for i in span:
                if i != p:
                    f = d[i][p]
                    d[i] = [-f * row[p] if j == p else d[i][j] - f * row[j] for j in span]
            d[p] = row
        in_cols = (col_of >= b) & (col_of < b + block)
        in_rows = (row_of >= b) & (row_of < b + block)
        base = jnp.where(in_rows | in_cols, 0.0, k)
        for i in span:
            row, corner = d[i][0] * k[b : b + 1, :], d[i][0]
            for j in range(1, block):
                row = row + d[i][j] * k[b + j : b + j + 1, :]
                corner = jnp.where(col_of == b + j, d[i][j], corner)
            row = jnp.where(in_cols, corner, row)
            col = jnp.where(in_rows, jnp.where(row_of == b + i, -1.0, 0.0), k[:, b + i : b + i + 1])
            base = base - col * row
        k = base
    return k


def solve_kernel(k_in, rt_in, v_in, w_in, r_in, x_out, r_out, k_buf, rt, v, w, r, sems):
    whole = ((k_in, k_buf), (rt_in, rt), (v_in, v), (w_in, w), (r_in, r))
    fetch = [pltpu.make_async_copy(src, dst, sems.at[i]) for i, (src, dst) in enumerate(whole)]
    for f in fetch:
        f.start()
    fetch[0].wait()
    size, cells = rt.shape[1], r.shape[1]
    k = k_buf[...].reshape(size, size)
    kt = k.T
    row_of = lax.broadcasted_iota(jnp.int32, (size, 1), 0)
    col_of = lax.broadcasted_iota(jnp.int32, (1, size), 1)
    row_p, col_p = lax.rem(row_of // 8, 2) == 1, lax.rem(col_of // 8, 2) == 1
    both = k + kt
    k = jnp.where(row_p, jnp.where(col_p, both, kt), jnp.where(col_p, k, 0.5 * both))
    high = lax.Precision.HIGHEST
    inverse = spd_inverse(k, 4)
    for f in fetch[1:]:
        f.wait()
    c = jnp.dot(rt[...], inverse, precision=high, preferred_element_type=F32)
    x_out[...] = jnp.dot(c, v[...].reshape(size, cells), precision=high, preferred_element_type=F32)
    r_out[...] = r[...] - jnp.dot(c, w[...].reshape(size, cells), precision=high, preferred_element_type=F32)


def solve(k, rt, v, w, r):
    operands = (k, rt, v, w, r)
    return pl.pallas_call(
        solve_kernel,
        out_shape=[jax.ShapeDtypeStruct(r.shape, F32)] * 2,
        in_specs=[pl.BlockSpec(memory_space=pltpu.HBM)] * 5,
        out_specs=[VMEM] * 2,
        scratch_shapes=[pltpu.VMEM(o.shape, F32) for o in operands] + [pltpu.SemaphoreType.DMA((5,))],
        compiler_params=pltpu.CompilerParams(vmem_limit_bytes=60 * MIB),
    )(*operands)


def solution(mesh):
    nr, nz = mesh.shape["rows"], mesh.shape["rhs"]

    def shards(right_side, tiles, pivots, columns):
        v, w, k, rt = krylov(nr, nz, columns, tiles, right_side, pivots)
        return tuple(solve(k, rt, v, w, right_side))

    return jax.shard_map(
        shards,
        mesh=mesh,
        in_specs=(
            P("rhs", "rows"),
            P("rows", None, None, None),
            P("rows", None, None),
            P("rows", None),
        ),
        out_specs=(P("rhs", "rows"), P("rhs", "rows")),
        check_vma=False,
    )
```
